32 devices in a mesh: tile: 8 (over z, y), fs: 4 (over x, core).
Axes of the slice: x: 2, y: 2, z: 4, core: 2. Of those that a mesh axis runs over, the one named last changes fastest.
Arguments:
- cells: bfloat16 [4, 3072, 1024], P('fs', 'tile'), may hold values from -6 to 6
- spatial_flag: int32 [4, 3072], P('fs', 'tile'), may hold values 0 or 1
- neighbours: int32 [4, 3072, 32], P('fs', 'tile'), may hold values from 0 to 3071, as said below
- kl_step: int32 [1], replicated, may hold values from 250 to 1000
- noise: float32 [4, 3072, 512], P('fs', 'tile'), may hold values from -5 to 5
- out_cot: bfloat16 [4, 3072, 1024], P('fs', 'tile'), may hold values from -6 to 6
- first_gain: bfloat16 [1024], P(('tile', 'fs')), may hold values from 0.5 to 1.5
- first_shift: bfloat16 [1024], P(('tile', 'fs')), may hold values from -1.75 to 1.75
- triple_proj: bfloat16 [1024, 3072], P('tile', 'fs'), may hold values from -0.1875 to 0.1875
- merge_proj: bfloat16 [1024, 1024], P('tile', 'fs'), may hold values from -0.375 to 0.375
- second_gain: bfloat16 [1024], P(('tile', 'fs')), may hold values from 0.5 to 1.5
- second_shift: bfloat16 [1024], P(('tile', 'fs')), may hold values from -1.75 to 1.75
- expand_weight: bfloat16 [1024, 4096], P('tile', 'fs'), may hold values from -0.1875 to 0.1875
- expand_bias: bfloat16 [4096], P(('tile', 'fs')), may hold values from -1.75 to 1.75
- reduce_weight: bfloat16 [4096, 1024], P('tile', 'fs'), may hold values from -0.125 to 0.125
- reduce_bias: bfloat16 [1024], P(('tile', 'fs')), may hold values from -1.75 to 1.75
- third_gain: bfloat16 [1024], P(('tile', 'fs')), may hold values from 0.5 to 1.5
- third_shift: bfloat16 [1024], P(('tile', 'fs')), may hold values from -1.75 to 1.75
- encode_weight: bfloat16 [1024, 1024], P('tile', 'fs'), may hold values from -0.1875 to 0.1875
- encode_bias: bfloat16 [1024], P(('tile', 'fs')), may hold values from -1.75 to 1.75
- decode_weight: bfloat16 [512, 1024], P('tile', 'fs'), may hold values from -0.25 to 0.25
- decode_bias: bfloat16 [1024], P(('tile', 'fs')), may hold values from -1.75 to 1.75
- mixture_logits: float32 [16], replicated, may hold values from -6 to 6
- mixture_means: float32 [16, 512], replicated, may hold values from -0.1875 to 0.1875
- mixture_logvars: float32 [16, 512], replicated, may hold values from -0.05 to 0.05
Outputs:
- decoded: bfloat16 [4, 3072, 1024], P('fs', 'tile')
- cells_grad: float32 [4, 3072, 1024], P('fs', 'tile')
- first_gain_grad: float32 [1024], P(('tile', 'fs'))
- first_shift_grad: float32 [1024], P(('tile', 'fs'))
- triple_proj_grad: float32 [1024, 3072], P('tile', 'fs')
- merge_proj_grad: float32 [1024, 1024], P('tile', 'fs')
- second_gain_grad: float32 [1024], P(('tile', 'fs'))
- second_shift_grad: float32 [1024], P(('tile', 'fs'))
- expand_weight_grad: float32 [1024, 4096], P('tile', 'fs')
- expand_bias_grad: float32 [4096], P(('tile', 'fs'))
- reduce_weight_grad: float32 [4096, 1024], P('tile', 'fs')
- reduce_bias_grad: float32 [1024], P(('tile', 'fs'))
- third_gain_grad: float32 [1024], P(('tile', 'fs'))
- third_shift_grad: float32 [1024], P(('tile', 'fs'))
- encode_weight_grad: float32 [1024, 1024], P('tile', 'fs')
- encode_bias_grad: float32 [1024], P(('tile', 'fs'))
- decode_weight_grad: float32 [512, 1024], P('tile', 'fs')
- decode_bias_grad: float32 [1024], P(('tile', 'fs'))
- mixture_logits_grad: float32 [16], replicated
- mixture_means_grad: float32 [16, 512], replicated
- mixture_logvars_grad: float32 [16, 512], replicated
The draws below stay inside these ranges and needn't reach their ends.
Inputs may be any that keep to these rules, and one draw needn't show every extreme that they name: `neighbours`: each entry names a cell of the same slide whose position differs from the cell's own by at most 128.
All inputs are finite; a program needn't handle non-finite values. No bound on the sum of `spatial_flag` on one device may be relied on, other than what follows from the above.
Results may differ from the reference program's by a relative error of at most 0.017.
Values may be sent and summed in bfloat16 or wider, within the bound.
A program may use at most 256 MiB of HBM per device.

```python
import jax
import jax.numpy as jnp
from jax import lax

D = 1024
HEADS = 16
FF = 4096
LAT = 512
COMP = 16
TOK_DEV = 384
WIN = 128
NB = 32
WARMUP = 1000
SLIDE = 3072
SLIDES = 4


def draw_neighbours(key, part):
    offsets = jax.random.randint(key, (SLIDES, SLIDE, NB), -WIN, WIN + 1)
    places = jnp.arange(SLIDE, dtype=jnp.int32)[None, :, None] + offsets
    return jnp.clip(places, 0, SLIDE - 1).astype(jnp.int32)


def touch_ends(entries, key, smallest, high):
    longest = entries.shape.index(max(entries.shape))
    spots = []
    for shift in (0, 1):
        where = [jax.random.randint(jax.random.fold_in(key, axis), (), 0, length) for axis, length in enumerate(entries.shape)]
        where[longest] = (where[longest] + shift) % entries.shape[longest]
        spots.append(tuple(where))
    return entries.at[spots[0]].set(smallest).at[spots[1]].set(high)


def steps_of(own_key, extent, split, smallest, top_value):
    factor_of, own = 1.0, jax.random.fold_in(own_key, 6)
    for axis_at, shards_of in split:
        heights = jnp.exp(jax.random.uniform(jax.random.fold_in(own, axis_at), (shards_of,), jnp.float32, smallest / len(split), top_value / len(split)))
        factor_of = factor_of * jnp.repeat(heights, extent[axis_at] // shards_of).reshape([-1 if axis == axis_at else 1 for axis in range(len(extent))])
    return factor_of


def normal_values(key, extent, scale, reach, pieces=(), kind=jnp.bfloat16):
    drawn = jax.random.normal(key, extent, jnp.float32) * scale
    if len(pieces) > 0:
        drawn = steps_of(key, extent, pieces, -0.22, 0.18) * drawn
    return jnp.clip(drawn, min=-reach, max=reach).astype(kind)


def setup_inputs(seed: int = 0) -> dict:
    arg_keys = jax.random.split(jax.random.key(seed), 26)
    cells = normal_values(arg_keys[0], (SLIDES, SLIDE, D), 1.0, 6.0, ((0, 4), (1, 8)))
    spatial_flag = touch_ends((jax.random.randint(arg_keys[1], (SLIDES, SLIDE), 0, 4) < 3).astype(jnp.int32), jax.random.fold_in(arg_keys[1], 1), 0, 1)
    neighbours = draw_neighbours(jax.random.fold_in(arg_keys[25], 71), 0)
    kl_step = jax.random.randint(arg_keys[3], (1,), WARMUP // 4, WARMUP + 1).astype(jnp.int32)
    noise = normal_values(arg_keys[4], (SLIDES, SLIDE, LAT), 1.0, 5.0, ((0, 4), (1, 8)), jnp.float32)
    out_cot = normal_values(arg_keys[5], (SLIDES, SLIDE, D), 1.0, 6.0, ((0, 4), (1, 8)))
    first_gain = jnp.clip(1.0 + 0.1 * jax.random.normal(arg_keys[6], (D,), jnp.float32), 0.5, 1.5).astype(jnp.bfloat16)
    first_shift = normal_values(arg_keys[7], (D,), 0.3, 1.75, ((0, 32),))
    triple_proj = normal_values(arg_keys[8], (D, 3 * D), D ** -0.5, 0.1875, ((0, 8), (1, 4)))
    merge_proj = normal_values(arg_keys[9], (D, D), (D // 4) ** -0.5, 0.375, ((0, 8), (1, 4)))
    second_gain = jnp.clip(1.0 + 0.1 * jax.random.normal(arg_keys[10], (D,), jnp.float32), 0.5, 1.5).astype(jnp.bfloat16)
    second_shift = normal_values(arg_keys[11], (D,), 0.3, 1.75, ((0, 32),))
    expand_weight = normal_values(arg_keys[12], (D, FF), D ** -0.5, 0.1875, ((0, 8), (1, 4)))
    expand_bias = normal_values(arg_keys[13], (FF,), 0.3, 1.75, ((0, 32),))
    reduce_weight = normal_values(arg_keys[14], (FF, D), (FF // 2) ** -0.5, 0.125, ((0, 8), (1, 4)))
    reduce_bias = normal_values(arg_keys[15], (D,), 0.3, 1.75, ((0, 32),))
    third_gain = jnp.clip(1.0 + 0.1 * jax.random.normal(arg_keys[16], (D,), jnp.float32), 0.5, 1.5).astype(jnp.bfloat16)
    third_shift = normal_values(arg_keys[17], (D,), 0.3, 1.75, ((0, 32),))
    encode_weight = normal_values(arg_keys[18], (D, 2 * LAT), D ** -0.5, 0.1875, ((0, 8), (1, 4)))
    encode_bias = normal_values(arg_keys[19], (2 * LAT,), 0.3, 1.75, ((0, 32),))
    decode_weight = normal_values(arg_keys[20], (LAT, D), LAT ** -0.5, 0.25, ((0, 8), (1, 4)))
    decode_bias = normal_values(arg_keys[21], (D,), 0.3, 1.75, ((0, 32),))
    mixture_logits = normal_values(arg_keys[22], (COMP,), 1.0, 6.0, (), jnp.float32)
    mixture_means = normal_values(arg_keys[23], (COMP, LAT), 0.03, 0.1875, (), jnp.float32)
    mixture_logvars = jnp.clip(jax.random.uniform(arg_keys[24], (COMP, LAT), jnp.float32, -0.05, 0.05), -0.05, 0.05)
    return {"cells": cells, "spatial_flag": spatial_flag, "neighbours": neighbours, "kl_step": kl_step, "noise": noise, "out_cot": out_cot, "first_gain": first_gain, "first_shift": first_shift, "triple_proj": triple_proj, "merge_proj": merge_proj, "second_gain": second_gain, "second_shift": second_shift, "expand_weight": expand_weight, "expand_bias": expand_bias, "reduce_weight": reduce_weight, "reduce_bias": reduce_bias, "third_gain": third_gain, "third_shift": third_shift, "encode_weight": encode_weight, "encode_bias": encode_bias, "decode_weight": decode_weight, "decode_bias": decode_bias, "mixture_logits": mixture_logits, "mixture_means": mixture_means, "mixture_logvars": mixture_logvars}


EPSILON = 1e-05
LOG_TWO_PI = 1.8378770664093453
FREE_BITS = 0.8
SOFT_WIDTH = 0.1
HIGHEST = lax.Precision.HIGHEST

@jax.custom_vjp
def low(v):
    return lax.optimization_barrier(v.astype(jnp.bfloat16)).astype(jnp.float32)

@jax.custom_vjp
def low_back(v):
    return v

def low_keep(v):
    return (low(v), None)

def low_pass(kept, grad):
    return (grad,)

def back_keep(v):
    return (v, None)

def back_low(kept, grad):
    return (low(grad),)
low.defvjp(low_keep, low_pass)
low_back.defvjp(back_keep, back_low)

def normalize(values, gain_vec, offset):
    center = values - lax.optimization_barrier(jnp.mean(values, -1, keepdims=True))
    spread = lax.optimization_barrier(jnp.mean(center * center, -1, keepdims=True))
    return center * lax.rsqrt(spread + EPSILON) * gain_vec + offset

def mixture_terms(latent, log_var, noise_rows, logits, means, logvars):
    log_prior = jax.nn.log_softmax(logits)
    precision_tab = jnp.exp(-logvars)
    weighted = means * precision_tab
    squared = means * weighted
    quadratic = jnp.dot(latent * latent, precision_tab.T, precision=HIGHEST) - 2.0 * jnp.dot(latent, weighted.T, precision=HIGHEST) + lax.optimization_barrier(jnp.sum(squared, 1))
    ell_rows = log_prior - 0.5 * (LOG_TWO_PI * latent.shape[1] + lax.optimization_barrier(jnp.sum(logvars, 1))) - 0.5 * quadratic
    log_resp = jax.nn.log_softmax(ell_rows, -1)
    resp_rows = jnp.exp(log_resp)
    cross_terms = -0.5 * (LOG_TWO_PI + jnp.dot(resp_rows, logvars, precision=HIGHEST) + latent * latent * jnp.dot(resp_rows, precision_tab, precision=HIGHEST) - 2.0 * latent * jnp.dot(resp_rows, weighted, precision=HIGHEST) + jnp.dot(resp_rows, squared, precision=HIGHEST))
    log_post = -0.5 * (LOG_TWO_PI + log_var + noise_rows * noise_rows)
    return (log_post - cross_terms, lax.optimization_barrier(jnp.sum(resp_rows * (log_resp - log_prior), 1)))

def window_mask(neighbour_rows, flag_rows, first_row, row_count):
    query_pos = first_row + jnp.arange(row_count, dtype=jnp.int32)
    key_pos = first_row - WIN + jnp.arange(row_count + 2 * WIN, dtype=jnp.int32)
    listed = jnp.any(neighbour_rows[:, :, None] == key_pos[None, None, :], axis=1)
    listed = listed | (query_pos[:, None] == key_pos[None, :])
    own_bin = (key_pos >= first_row) & (key_pos < first_row + row_count)
    return listed & ((flag_rows[:, None] == 1) | own_bin[None, :])

def window_block(query_heads, key_heads, value_heads, neighbour_rows, flag_rows, first_row):
    allowed = window_mask(neighbour_rows, flag_rows, first_row, query_heads.shape[0])
    scores = jnp.einsum('qhd,khd->hqk', query_heads, key_heads, precision=HIGHEST) * query_heads.shape[2] ** (-0.5)
    scores = low_back(scores)
    scores = jnp.where(allowed[None], scores, -1e+30)
    row_max = lax.optimization_barrier(jnp.max(scores, -1, keepdims=True))
    exp_rows = jnp.exp(scores - row_max)
    probs = low(exp_rows / lax.optimization_barrier(jnp.sum(exp_rows, -1, keepdims=True)))
    return jnp.einsum('hqk,khd->qhd', probs, value_heads, precision=HIGHEST)

def slide_pass(inputs, weights):
    cell_rows, flag_rows, neighbour_rows, noise_rows = inputs
    gain_one, shift_one, triple_proj, merge_proj, gain_two, shift_two, expand_weight, expand_bias, reduce_weight, reduce_bias, gain_three, shift_three, encode_weight, encode_bias, decode_weight, decode_bias, mixture_logits, mixture_means, mixture_logvars = weights
    features = cell_rows.shape[1]
    head_dim = features // HEADS
    normed_one = low(normalize(cell_rows, gain_one, shift_one))
    triple = low(low_back(jnp.dot(normed_one, triple_proj, precision=HIGHEST)))
    query_heads = triple[:, :features].reshape(-1, HEADS, head_dim)
    padding = ((WIN, WIN), (0, 0), (0, 0))
    key_pad = jnp.pad(triple[:, features:2 * features].reshape(-1, HEADS, head_dim), padding)
    value_pad = jnp.pad(triple[:, 2 * features:].reshape(-1, HEADS, head_dim), padding)
    block_starts = jnp.arange(cell_rows.shape[0] // TOK_DEV, dtype=jnp.int32) * TOK_DEV

    def one_block(first_row):
        query_blk = lax.dynamic_slice_in_dim(query_heads, first_row, TOK_DEV, 0)
        key_blk = lax.dynamic_slice_in_dim(key_pad, first_row, TOK_DEV + 2 * WIN, 0)
        value_blk = lax.dynamic_slice_in_dim(value_pad, first_row, TOK_DEV + 2 * WIN, 0)
        neigh_blk = lax.dynamic_slice_in_dim(neighbour_rows, first_row, TOK_DEV, 0)
        flag_blk = lax.dynamic_slice_in_dim(flag_rows, first_row, TOK_DEV, 0)
        return window_block(query_blk, key_blk, value_blk, neigh_blk, flag_blk, first_row).reshape(TOK_DEV, features)
    attended = lax.map(jax.checkpoint(one_block), block_starts).reshape(-1, features)
    attended = low(low_back(attended))
    hidden_one = cell_rows + low_back(jnp.dot(attended, merge_proj, precision=HIGHEST))
    normed_two = low(normalize(hidden_one, gain_two, shift_two))
    pre_act = low_back(jnp.dot(normed_two, expand_weight, precision=HIGHEST) + expand_bias)
    activated = low(jax.nn.gelu(pre_act, approximate=True))
    hidden_two = hidden_one + low_back(jnp.dot(activated, reduce_weight, precision=HIGHEST) + reduce_bias)
    normed_three = low(normalize(hidden_two, gain_three, shift_three))
    encoded = low_back(jnp.dot(normed_three, encode_weight, precision=HIGHEST) + encode_bias)
    latent_dim = encoded.shape[1] // 2
    lat_mean = encoded[:, :latent_dim]
    log_var = encoded[:, latent_dim:]
    latent = lat_mean + jnp.exp(0.5 * log_var) * noise_rows
    decoded = hidden_two + low_back(jnp.dot(low(latent), decode_weight, precision=HIGHEST) + decode_bias)
    kl_terms, mix_terms = mixture_terms(latent, log_var, noise_rows, mixture_logits, mixture_means, mixture_logvars)
    return (decoded, lax.optimization_barrier(jnp.sum(kl_terms, 0)), jnp.sum(mix_terms))

def reference(cells, spatial_flag, neighbours, kl_step, noise, out_cot, first_gain, first_shift, triple_proj, merge_proj, second_gain, second_shift, expand_weight, expand_bias, reduce_weight, reduce_bias, third_gain, third_shift, encode_weight, encode_bias, decode_weight, decode_bias, mixture_logits, mixture_means, mixture_logvars):
    weights = tuple((array.astype(jnp.float32) for array in (first_gain, first_shift, triple_proj, merge_proj, second_gain, second_shift, expand_weight, expand_bias, reduce_weight, reduce_bias, third_gain, third_shift, encode_weight, encode_bias, decode_weight, decode_bias, mixture_logits, mixture_means, mixture_logvars)))
    inputs32 = cells.astype(jnp.float32)
    noise32 = noise.astype(jnp.float32)
    kl_weight = kl_step[0].astype(jnp.float32) / WARMUP
    total_cells = SLIDES * SLIDE

    def objective(cell_arrays, params):

        def per_slide(items):
            return slide_pass(items, params)
        decoded, kl_sums, mix_sums = lax.map(jax.checkpoint(per_slide), (cell_arrays, spatial_flag, neighbours, noise32))
        average = lax.optimization_barrier(jnp.sum(kl_sums, 0)) / total_cells
        floored = FREE_BITS + SOFT_WIDTH * jax.nn.softplus((average - FREE_BITS) / SOFT_WIDTH)
        kl_loss = kl_weight * (total_cells * jnp.sum(floored) + jnp.sum(mix_sums))
        return (decoded, kl_loss)
    (decoded, kl_loss), pullback = jax.vjp(objective, inputs32, weights)
    cells_grad, grads = pullback((out_cot.astype(decoded.dtype), jnp.ones_like(kl_loss)))
    g_one, s_one, g_triple, g_merge, g_two, s_two, g_expand, b_expand, g_reduce, b_reduce, g_three, s_three, g_encode, b_encode, g_decode, b_decode, g_logits, g_means, g_logvars = grads
    return (decoded.astype(jnp.bfloat16), cells_grad, g_one, s_one, g_triple, g_merge, g_two, s_two, g_expand, b_expand, g_reduce, b_reduce, g_three, s_three, g_encode, b_encode, g_decode, b_decode, g_logits, g_means, g_logvars)
```

```python
import functools
from types import SimpleNamespace
import jax
import jax.numpy as jnp
from jax import lax
from jax.experimental import pallas as pl
from jax.experimental.pallas import tpu as pltpu

from jax.sharding import PartitionSpec as P

MESH = pl.DeviceIdType.MESH


class Place:
    def __init__(self, nt, nf):
        self.nt, self.nf = nt, nf
        self.nz, self.nx = nt // 2, nf // 2
        tile, fs = lax.axis_index("tile"), lax.axis_index("fs")
        self.tile, self.fs = tile, fs
        self.z, self.y = tile // 2, tile % 2
        self.x, self.c = fs // 2, fs % 2

    def zpeer(self, d):
        return (lax.rem(self.z + d, self.nz) * 2 + self.y, self.fs)

    def ypeer(self):
        return (self.z * 2 + 1 - self.y, self.fs)

    def xat(self, d):
        return lax.rem(self.x + d + self.nx, self.nx)

    def xpeer(self, d):
        return (self.tile, self.xat(d) * 2 + self.c)

    def sibling(self):
        return (self.tile, self.x * 2 + 1 - self.c)

    def peers(self):
        return (
            [self.zpeer(d) for d in range(1, self.nz)]
            + [self.ypeer()]
            + [self.xpeer(d) for d in range(1, self.nx)]
            + [self.sibling()]
        )


def greet(peers):
    barrier = pltpu.get_barrier_semaphore()
    for peer in peers:
        pl.semaphore_signal(barrier, inc=1, device_id=peer, device_id_type=MESH)
    pl.semaphore_wait(barrier, len(peers))


def half_of(rows):
    return max(rows * 5 // 8 // 16 * 16, 16) if rows % 32 == 0 else rows


class Copies:
    def __init__(self, send, recv):
        self.send, self.recv, self.used, self.slots, self.sent = send, recv, 0, {}, []

    def slot(self, key):
        if key not in self.slots:
            self.slots[key] = self.used
            self.used += 1
        return self.slots[key]

    def make(self, key, src, dst, peer):
        at = self.slot(key)
        return pltpu.make_async_remote_copy(
            src_ref=src,
            dst_ref=dst,
            send_sem=self.send.at[at],
            recv_sem=self.recv.at[at],
            device_id=peer,
            device_id_type=MESH,
        )

    def start(self, key, src, dst, peer):
        copy = self.make(key, src, dst, peer)
        copy.start()
        self.sent.append(copy)

    def arrived(self, key, where, peer):
        self.make(key, where, where, peer).wait_recv()

    def drain(self):
        for copy in self.sent:
            copy.wait_send()
        self.sent = []


GATHER_LAG = (0, 1, 2, 3, 4)


class Gather:
    def __init__(self, place, copies, local, key, shard, full, first, rows, left, cols):
        self.p, self.copies, self.local, self.key = place, copies, local, key
        self.shard, self.full, self.first, self.rows = shard, full, first, rows
        self.n, self.left, self.cols = shard.shape[1], left, cols

    def at(self, z, y, x, c, first=0, rows=None):
        rows = self.rows if rows is None else rows
        column = pl.multiple_of((x * 2 + c) * self.n + self.left, 128)
        return self.full.at[z, y, pl.ds(self.first + first, rows), pl.ds(column, self.cols)]

    def one(self):
        p = self.p
        mine = self.shard.at[pl.ds(self.first, self.rows), pl.ds(self.left, self.cols)]
        here = self.at(p.z, p.y, p.x, p.c)
        self.own = pltpu.make_async_copy(mine, here, self.local.at[self.copies.slot((self.key, "own"))])
        self.own.start()
        for d in range(1, p.nz):
            self.copies.start((self.key, "z", d), mine, here, p.zpeer(d))

    def two(self):
        p, key = self.p, self.key
        self.own.wait()
        for d in range(1, p.nz):
            zz = lax.rem(p.z - d + p.nz, p.nz)
            self.copies.arrived((key, "z", d), self.at(zz, p.y, p.x, p.c), p.zpeer(d))
        block = self.at(slice(None), p.y, p.x, p.c)
        self.copies.start((key, "y"), block, block, p.ypeer())
        for d in range(1, p.nx):
            self.copies.start((key, "x", d), block, block, p.xpeer(d))
        self.copies.start((key, "c"), block, block, p.sibling())

    def three(self):
        p, key = self.p, self.key
        half = half_of(self.rows)
        block = self.at(slice(None), 1 - p.y, p.x, p.c)
        self.copies.arrived((key, "y"), block, p.ypeer())
        part = self.at(slice(None), 1 - p.y, p.x, p.c, 0, half)
        for d in range(1, p.nx):
            self.copies.start((key, "yx", d), part, part, p.xpeer(d))
        for d in range(1, p.nx):
            far = p.xat(-d)
            other = self.at(slice(None), p.y, far, p.c)
            self.copies.arrived((key, "x", d), other, p.xpeer(d))
            if half < self.rows:
                part = self.at(slice(None), p.y, far, p.c, half, self.rows - half)
                self.copies.start((key, "xy", d), part, part, p.ypeer())
            self.copies.start((key, "xc", d), other, other, p.sibling())
        self.copies.start((key, "yc"), block, block, p.sibling())

    def four(self):
        p, key = self.p, self.key
        half = half_of(self.rows)
        for d in range(1, p.nx):
            far = p.xat(-d)
            self.copies.arrived((key, "yx", d), self.at(slice(None), 1 - p.y, far, p.c, 0, half), p.xpeer(d))
            if half < self.rows:
                part = self.at(slice(None), 1 - p.y, far, p.c, half, self.rows - half)
                self.copies.arrived((key, "xy", d), part, p.ypeer())
            block = self.at(slice(None), 1 - p.y, far, p.c)
            self.copies.start((key, "dc", d), block, block, p.sibling())

    def five(self):
        p, key = self.p, self.key
        other = 1 - p.c
        self.copies.arrived((key, "c"), self.at(slice(None), p.y, p.x, other), p.sibling())
        self.copies.arrived((key, "yc"), self.at(slice(None), 1 - p.y, p.x, other), p.sibling())
        for d in range(1, p.nx):
            far = p.xat(-d)
            self.copies.arrived((key, "xc", d), self.at(slice(None), p.y, far, other), p.sibling())
            self.copies.arrived((key, "dc", d), self.at(slice(None), 1 - p.y, far, other), p.sibling())


def gather_slots(nt, nf):
    return 1 + (nt // 2 - 1) + 3 + 5 * (nf // 2 - 1)


class Small:
    def __init__(self, place, copies, key, mine, slots):
        self.p, self.copies, self.key, self.mine, self.slots = place, copies, key, mine, slots
        p = place
        self.stages = [
            ([p.zpeer(d) for d in range(1, p.nz)], p.z, p.nz),
            ([p.ypeer()], p.y, 2),
            ([p.xpeer(d) for d in range(1, p.nx)], p.x, p.nx),
            ([p.sibling()], p.c, 2),
        ]

    def base(self, stage):
        return sum(size for _, _, size in self.stages[:stage])

    def send(self, stage):
        peers, at, _ = self.stages[stage]
        base = self.base(stage)
        self.slots[base + at] = self.mine[...]
        for i, peer in enumerate(peers):
            self.copies.start((self.key, stage, i), self.slots.at[base + at], self.slots.at[base + at], peer)

    def receive(self, stage):
        peers, at, size = self.stages[stage]
        base = self.base(stage)
        for i, peer in enumerate(peers):
            came = lax.rem(at - i - 1 + size, size)
            self.copies.arrived((self.key, stage, i), self.slots.at[base + came], peer)
        total = self.slots[base]
        for j in range(1, size):
            total = total + self.slots[base + j]
        self.mine[...] = total


def small_slots(nt, nf):
    return nt // 2 - 1 + 1 + nf // 2 - 1 + 1


def small_places(nt, nf):
    return nt // 2 + 2 + nf // 2 + 2


HEADS = 16
WIN = 128
WARMUP = 1000


EPSILON = 1e-05
LOG_TWO_PI = 1.8378770664093453
FREE_BITS = 0.8
SOFT_WIDTH = 0.1
HIGHEST = lax.Precision.HIGHEST


def row_dot(left, right):
    return lax.dot_general(left, right, (((1,), (1,)), ((), ())), preferred_element_type=jnp.float32)


def col_dot(left, right):
    return lax.dot_general(left, right, (((0,), (0,)), ((), ())), preferred_element_type=jnp.float32)


def plain_dot(left, right):
    return jnp.dot(left, right, preferred_element_type=jnp.float32)


def split_weights(shapes, order):
    cols = min(n for _, n in shapes)
    out = []
    for w in order:
        r, n = shapes[w]
        rows = min(r, 128)
        for i in range(r // rows):
            for j in range(n // cols):
                out.append((w, i * rows, rows, j * cols, cols))
    return out


def high_dot(left, right, left_dim, right_dim):
    return lax.dot_general(
        left,
        right,
        (((left_dim,), (right_dim,)), ((), ())),
        precision=HIGHEST,
        preferred_element_type=jnp.float32,
    )


def mixture_tables(logits, means, logvars):
    precision_tab = jnp.exp(-logvars)
    weighted = means * precision_tab
    top = jnp.max(logits, -1, keepdims=True)
    log_prior = logits - top - jnp.log(jnp.sum(jnp.exp(logits - top), -1, keepdims=True))
    return precision_tab, weighted, means * weighted, log_prior


def forward_kernel(nt, nf, piece, wide_piece, plan, names, *refs):
    r = SimpleNamespace(**dict(zip(names, refs)))
    p = Place(nt, nf)
    w_of, full_of = (r.w0, r.w1, r.w2, r.w3, r.w4, r.w5), (r.full0, r.full1, r.full2, r.full3, r.full4, r.full5)
    sib_of = (r.sib_n1, r.sib_att, r.sib_n2, r.sib_act, r.sib_n3, r.sib_lat)
    rows, features = r.cells.shape
    tiles, mine, vectors = r.tiles, r.mine, r.vectors
    edge = WIN
    lane = lax.broadcasted_iota(jnp.int32, (16, 128), 1)
    row = lax.broadcasted_iota(jnp.int32, (16, 128), 0)
    index = p.tile * nf + p.fs
    narrow_here = lane // piece == lax.rem(index, 128 // piece)
    wide_here = lane // wide_piece == lax.rem(index, 128 // wide_piece)
    here = ((row != 9) & narrow_here) | ((row == 9) & wide_here)
    mine[...] = jnp.where(here, r.packed[...].astype(jnp.float32), 0.0).astype(jnp.bfloat16)
    before = (lax.rem(p.tile + nt - 1, nt), p.fs)
    after = (lax.rem(p.tile + 1, nt), p.fs)
    greet(p.peers() + [before, after])
    copies = Copies(r.send, r.recv)
    local = r.local
    steps = [Gather(p, copies, r.own_sem, "vec", mine, tiles, 0, 16, 0, 128)]
    ends = {}
    for i, (w, f, n, c, m) in enumerate(plan):
        steps.append(Gather(p, copies, r.own_sem, i, w_of[w], full_of[w], f, n, c, m))
        ends[w] = i + 1
    lags = list(zip(("one", "two", "three", "four", "five"), GATHER_LAG))
    clock = [0]

    def pump(count=1):
        for _ in range(count):
            k = clock[0]
            for name, lag in lags:
                if 0 <= k - lag < len(steps):
                    getattr(steps[k - lag], name)()
            clock[0] += 1

    def need(step):
        while clock[0] <= step + GATHER_LAG[-1]:
            pump()

    used = [0]

    def share(i, src):
        copies.start(("a", i), src, sib_of[i], p.sibling())

    def put_out(src, dst):
        copy = pltpu.make_async_copy(src, dst, local.at[used[0]])
        used[0] += 1
        copy.start()
        return copy

    pump(2)
    first_row = p.tile * rows
    bias = r.bias
    near = r.near
    flag_row = r.flags[...].astype(jnp.float32)
    count = 3 * edge
    for b in range(rows // edge):
        at = b * edge
        diagonal = lax.broadcasted_iota(jnp.int32, (edge, edge), 0) == lax.broadcasted_iota(jnp.int32, (edge, edge), 1)
        flag = jnp.sum(jnp.where(diagonal, flag_row[:, at : at + edge], 0.0), 1, keepdims=True)
        offset = lax.broadcasted_iota(jnp.int32, (edge, count), 1)
        key = first_row + at - edge + offset
        query = first_row + at + lax.broadcasted_iota(jnp.int32, (edge, count), 0)
        listed = key == query
        for n in range(near.shape[1]):
            listed = listed | (near[at : at + edge, n : n + 1] == key)
        own_bin = (key >= first_row) & (key < first_row + rows)
        allowed = listed & ((flag > 0.5) | own_bin)
        bias[b] = jnp.where(allowed, 0.0, -1e30)
        pump()
    need(0)
    for at in range(nt * nf // (128 // piece)):
        total = jnp.zeros((16, 128), jnp.float32)
        for j in range(128 // piece):
            t, f = divmod(at * (128 // piece) + j, nf)
            total = total + tiles[t // 2, t % 2, :, f * 128 : (f + 1) * 128].astype(jnp.float32)
        vectors[0:9, at * 128 : (at + 1) * 128] = total[0:9]
    for at in range(nt * nf // (128 // wide_piece)):
        total = jnp.zeros((1, 128), jnp.float32)
        for j in range(128 // wide_piece):
            t, f = divmod(at * (128 // wide_piece) + j, nf)
            total = total + tiles[t // 2, t % 2, :, f * 128 : (f + 1) * 128].astype(jnp.float32)[9:10]
        vectors[9 + at // 8 : 10 + at // 8, at % 8 * 128 : (at % 8 + 1) * 128] = total

    def norm(values, gain_row, out):
        gain, shift = vectors[gain_row : gain_row + 1, :], vectors[gain_row + 1 : gain_row + 2, :]

        def one(i, carry):
            at = pl.ds(pl.multiple_of(i * 32, 32), 32)
            v = values[at, :].astype(jnp.float32)
            center = v - jnp.mean(v, -1, keepdims=True)
            inverse = lax.rsqrt(jnp.mean(center * center, -1, keepdims=True) + EPSILON)
            out[at, :] = (center * inverse * gain + shift).astype(jnp.bfloat16)
            return carry

        lax.fori_loop(0, rows // 32, one, 0)

    def stream(pieces, buffers, sems, body):
        def copy_of(i):
            src = pieces[i]
            dst = buffers.at[i % 2, pl.ds(0, src.shape[0]), pl.ds(0, src.shape[1])]
            return pltpu.make_async_copy(src, dst, sems.at[i % 2])

        copy_of(0).start()
        for i in range(len(pieces)):
            if i + 1 < len(pieces):
                copy_of(i + 1).start()
            copy_of(i).wait()
            body(i, i % 2)

    wide, tall = r.wide, r.tall

    def full_cols(w, first, width):
        full = full_of[w]
        flat = full.reshape(full.shape[0] * full.shape[1] * full.shape[2], full.shape[3])
        return flat.at[:, pl.ds(first, width)]

    def full_rows(w, first, height):
        full = full_of[w]
        flat = full.reshape(full.shape[0] * full.shape[1] * full.shape[2], full.shape[3])
        return flat.at[pl.ds(first, height), :]

    def times(left, w, width, use, tick=False):
        total = full_of[w].shape[3]
        depth = left.shape[1]

        def body(i, b):
            def one(j, carry):
                at = pl.multiple_of(j * 256, 256)
                use(i, at, plain_dot(left[...], wide[b, pl.ds(0, depth), pl.ds(at, 256)]))
                return carry

            lax.fori_loop(0, width // 256, one, 0)
            if tick:
                pump()

        stream([full_cols(w, i * width, width) for i in range(total // width)], wide, r.wide_sem, body)

    normed_one = r.n1_v
    norm(r.cells, 0, normed_one)
    outs = [put_out(normed_one, r.n1)]
    share(0, normed_one)
    need(ends[0])
    queries, keys, values = r.q_v, r.k_v, r.v_v
    here_rows = pl.ds(edge, rows)

    def keep_triple(i, at, value):
        value = value.astype(jnp.bfloat16)
        lanes = pl.ds(at, 256)
        which, first = divmod(i * 512, features)
        lanes = pl.ds(pl.multiple_of(first + at, 256), 256)
        if which == 0:
            queries[:, lanes] = value
        elif which == 1:
            keys[here_rows, lanes] = value
        else:
            values[here_rows, lanes] = value

    times(normed_one, 0, 512, keep_triple)

    def halo(which, up):
        ref = (keys, values)[which]
        if up:
            return copies.make(("halo", which, up), ref.at[pl.ds(rows, edge)], ref.at[pl.ds(0, edge)], after)
        return copies.make(("halo", which, up), ref.at[pl.ds(edge, edge)], ref.at[pl.ds(rows + edge, edge)], before)

    @pl.when(p.tile < nt - 1)
    def _():
        for which in range(2):
            halo(which, True).start()

    @pl.when(p.tile > 0)
    def _():
        for which in range(2):
            halo(which, False).start()

    outs.append(put_out(queries, r.q))
    pump()

    @pl.when(p.tile > 0)
    def _():
        for which in range(2):
            halo(which, True).wait_recv()

    @pl.when(p.tile == 0)
    def _():
        for ref in (keys, values):
            ref[0:edge, :] = jnp.zeros((edge, features), jnp.bfloat16)

    @pl.when(p.tile < nt - 1)
    def _():
        for which in range(2):
            halo(which, False).wait_recv()

    @pl.when(p.tile == nt - 1)
    def _():
        for ref in (keys, values):
            ref[edge + rows :, :] = jnp.zeros((edge, features), jnp.bfloat16)

    outs.append(put_out(keys, r.kext))
    outs.append(put_out(values, r.vext))

    pairs = features // 128
    scale = (features // HEADS) ** (-0.5)
    attended = r.att_v

    def probs_out(i, b):
        return pltpu.make_async_copy(r.p_v.at[b], r.probs.at[pl.ds(2 * i, 2)], r.pair_sem.at[b])

    def pair(i, carry):
        b = lax.rem(i, 2)

        @pl.when(i >= 2)
        def _():
            probs_out(i - 2, b).wait()

        lanes = pl.ds(pl.multiple_of(i * 128, 128), 128)
        zero = jnp.zeros((), jnp.bfloat16)
        for block in range(rows // edge):
            own_rows, keys_at = pl.ds(block * edge, edge), pl.ds(block * edge, count)
            head = lax.broadcasted_iota(jnp.int32, (edge, 128), 1) // 64
            key_head = lax.broadcasted_iota(jnp.int32, (count, 128), 1) // 64
            total = jnp.zeros((edge, 128), jnp.float32)
            for e in range(2):
                query = jnp.where(head == e, queries[own_rows, lanes], zero)
                score = row_dot(query, keys[keys_at, lanes]) * scale + bias[block]
                top = jnp.max(score, -1, keepdims=True)
                power = jnp.exp(score - top)
                prob = (power / jnp.sum(power, -1, keepdims=True)).astype(jnp.bfloat16)
                r.p_v[b, e, block] = prob
                total = total + plain_dot(prob, jnp.where(key_head == e, values[keys_at, lanes], zero))
            attended[own_rows, lanes] = total.astype(jnp.bfloat16)
        probs_out(i, b).start()
        return carry

    for i in range(pairs // 2):
        lax.fori_loop(2 * i, 2 * i + 2, pair, 0)
        pump()
    for i in range(pairs - 2, pairs):
        probs_out(i, i % 2).wait()
    outs.append(put_out(attended, r.att))
    share(1, attended)
    need(ends[1])
    hidden = r.hid_v

    def keep_hidden(i, at, value):
        lanes = pl.ds(pl.multiple_of(i * 512 + at, 256), 256)
        hidden[:, lanes] = r.cells[:, lanes].astype(jnp.float32) + value

    times(attended, 1, 512, keep_hidden)
    outs.append(put_out(hidden, r.hid))
    normed_two = r.n2_v
    norm(hidden, 2, normed_two)
    outs.append(put_out(normed_two, r.n2))
    share(2, normed_two)
    need(ends[2])

    root = 0.7978845608028654
    activated, pre_v = r.act_v, r.pre_v

    def pre_out(i):
        return pltpu.make_async_copy(pre_v.at[i % 2], r.pre.at[:, pl.ds(i * 512, 512)], r.pre_sem.at[i % 2])

    def keep_pre(i, at, value):
        vec_row, first = divmod(i * 512, features)
        lanes = pl.ds(pl.multiple_of(first + at, 256), 256)
        u = value + vectors[9 + vec_row : 10 + vec_row, lanes]
        pre_v[i % 2, :, pl.ds(at, 256)] = u
        gate = 0.5 * (1.0 + jnp.tanh(root * (u + 0.044715 * u * u * u)))
        activated[:, pl.ds(pl.multiple_of(i * 512 + at, 256), 256)] = (u * gate).astype(jnp.bfloat16)

    def up_body(i, b):
        if i >= 2:
            pre_out(i - 2).wait()

        def one(j, carry):
            at = pl.multiple_of(j * 256, 256)
            keep_pre(i, at, plain_dot(normed_two[...], wide[b, :, pl.ds(at, 256)]))
            return carry

        lax.fori_loop(0, 2, one, 0)
        pre_out(i).start()
        if i % 4 == 3:
            pump()

    depth = activated.shape[1]
    up_count = depth // 512
    stream([full_cols(2, i * 512, 512) for i in range(up_count)], wide, r.wide_sem, up_body)
    for i in range(up_count - 2, up_count):
        pre_out(i).wait()
    outs.append(put_out(activated, r.act))
    share(3, activated)
    need(ends[3])
    second = r.two_v

    def down_body(i, b):
        def one(j, carry):
            lanes = pl.ds(pl.multiple_of(j * 256, 256), 256)
            part = plain_dot(activated[:, i * 512 : (i + 1) * 512], tall[b, :, lanes])
            if i == 0:
                second[:, lanes] = hidden[:, lanes] + vectors[4:5, lanes] + part
            else:
                second[:, lanes] += part
            return carry

        lax.fori_loop(0, features // 256, one, 0)

    stream([full_rows(3, i * 512, 512) for i in range(up_count)], tall, r.tall_sem, down_body)
    outs.append(put_out(second, r.two))
    normed_three = r.n3_v
    norm(second, 5, normed_three)
    outs.append(put_out(normed_three, r.n3))
    share(4, normed_three)
    need(ends[4])
    encoded = r.enc_v

    def keep_encoded(i, at, value):
        lanes = pl.ds(pl.multiple_of(i * 512 + at, 256), 256)
        encoded[:, lanes] = value + vectors[7:8, lanes]

    times(normed_three, 4, 512, keep_encoded)
    outs.append(put_out(encoded, r.enc))
    latent, latent32 = r.lat_v, r.z_v
    half = features // 2
    tables = mixture_tables(r.logits[...], r.means[...], r.logvars[...])
    precision_tab, weighted, squared, log_prior = tables
    logvars = r.logvars[...]
    ones = jnp.ones((8, half), jnp.float32)
    constant = log_prior - 0.5 * (
        LOG_TWO_PI * half + high_dot(ones, logvars, 1, 1)[0:1] + high_dot(ones, squared, 1, 1)[0:1]
    )
    r.tab[...] = jnp.zeros_like(r.tab)
    r.klp[...] = jnp.zeros_like(r.klp)

    def latent_rows(i, carry):
        at = pl.ds(pl.multiple_of(i * 128, 128), 128)
        log_var, noise = encoded[at, half:], r.noise[at, :]
        z = encoded[at, 0:half] + jnp.exp(0.5 * log_var) * noise
        latent32[at, :] = z
        latent[at, :] = z.astype(jnp.bfloat16)
        square = z * z
        ell = constant - 0.5 * (high_dot(square, precision_tab, 1, 1) - 2.0 * high_dot(z, weighted, 1, 1))
        ell = ell - jnp.max(ell, -1, keepdims=True)
        log_resp = ell - jnp.log(jnp.sum(jnp.exp(ell), -1, keepdims=True))
        r.lr[at, :] = log_resp
        resp = jnp.exp(log_resp)
        r.tab[0] += high_dot(resp, z, 0, 0)
        r.tab[1] += high_dot(resp, square, 0, 0)
        r.tab[2] += high_dot(resp, jnp.ones_like(z), 0, 0)
        r.klp[0:1, :] += -0.5 * jnp.sum(LOG_TWO_PI + log_var + noise * noise, 0, keepdims=True)
        return carry

    lax.fori_loop(0, rows // 128, latent_rows, 0)
    cross = r.tab[2] * (LOG_TWO_PI + logvars + squared) + precision_tab * r.tab[1] - 2.0 * weighted * r.tab[0]
    r.klp[0:1, :] += 0.5 * jnp.sum(cross, 0, keepdims=True)
    outs.append(put_out(latent, r.lat))
    outs.append(put_out(latent32, r.z))
    share(5, latent)
    need(ends[5])
    decoded = r.dec_v

    def keep_decoded(i, at, value):
        lanes = pl.ds(pl.multiple_of(i * 512 + at, 256), 256)
        decoded[:, lanes] = (second[:, lanes] + value + vectors[8:9, lanes]).astype(jnp.bfloat16)

    times(latent, 5, 512, keep_decoded)
    outs.append(put_out(decoded, r.decoded))
    for i in range(6):
        copies.arrived(("a", i), sib_of[i], p.sibling())
    for copy in outs:
        copy.wait()

    @pl.when(p.tile < nt - 1)
    def _():
        for which in range(2):
            halo(which, True).wait_send()

    @pl.when(p.tile > 0)
    def _():
        for which in range(2):
            halo(which, False).wait_send()

    copies.drain()


def forward(cells, flags, near, noise, shards, small_vectors, mixture, nt, nf):
    piece, wide_piece = small_vectors[0].shape[0], small_vectors[9].shape[0]
    packed = jnp.stack([jnp.tile(v, 128 // v.shape[0]) for v in small_vectors])
    packed = jnp.pad(packed, ((0, 6), (0, 0)))
    shapes = [s.shape for s in shards]
    plan = split_weights(shapes, range(6))
    rows, features = cells.shape
    lats = noise.shape[1]
    depth = shapes[2][1] * nf
    keys = rows + 2 * WIN
    blocks = rows // WIN
    bf, f32 = jnp.bfloat16, jnp.float32
    nz = nt // 2
    slots = gather_slots(nt, nf) * (len(plan) + 1) + 4 + 6
    comps = mixture[1].shape[0]
    hbm, vmem = pl.BlockSpec(memory_space=pltpu.HBM), pl.BlockSpec(memory_space=pltpu.VMEM)
    fulls = [((nz, 2, s, n * nf), bf, hbm) for s, n in shapes]
    outs = dict(
        full0=fulls[0],
        full1=fulls[1],
        full2=fulls[2],
        full3=fulls[3],
        full4=fulls[4],
        full5=fulls[5],
        sib_n1=((rows, features), bf, hbm),
        sib_att=((rows, features), bf, hbm),
        sib_n2=((rows, features), bf, hbm),
        sib_act=((rows, depth), bf, hbm),
        sib_n3=((rows, features), bf, hbm),
        sib_lat=((rows, lats), bf, hbm),
        z=((rows, lats), f32, hbm),
        lr=((rows, comps), f32, vmem),
        tab=((3, comps, lats), f32, vmem),
        klp=((8, lats), f32, vmem),
        n1=((rows, features), bf, hbm),
        q=((rows, features), bf, hbm),
        kext=((keys, features), bf, hbm),
        vext=((keys, features), bf, hbm),
        probs=((HEADS, blocks, WIN, 3 * WIN), bf, hbm),
        att=((rows, features), bf, hbm),
        hid=((rows, features), f32, hbm),
        n2=((rows, features), bf, hbm),
        pre=((rows, depth), f32, hbm),
        act=((rows, depth), bf, hbm),
        two=((rows, features), f32, hbm),
        n3=((rows, features), bf, hbm),
        enc=((rows, features), f32, hbm),
        lat=((rows, lats), bf, hbm),
        decoded=((rows, features), bf, hbm),
        vectors=((16, features), f32, vmem),
    )
    dma = pltpu.SemaphoreType.DMA
    scratch = dict(
        tiles=pltpu.VMEM((nz, 2, 16, nf * 128), bf),
        mine=pltpu.VMEM((16, 128), bf),
        bias=pltpu.VMEM((blocks, WIN, 3 * WIN), f32),
        n1_v=pltpu.VMEM((rows, features), bf),
        q_v=pltpu.VMEM((rows, features), bf),
        k_v=pltpu.VMEM((keys, features), bf),
        v_v=pltpu.VMEM((keys, features), bf),
        p_v=pltpu.VMEM((2, 2, blocks, WIN, 3 * WIN), bf),
        pair_sem=dma((2,)),
        att_v=pltpu.VMEM((rows, features), bf),
        hid_v=pltpu.VMEM((rows, features), f32),
        n2_v=pltpu.VMEM((rows, features), bf),
        pre_v=pltpu.VMEM((2, rows, 512), f32),
        pre_sem=dma((2,)),
        act_v=pltpu.VMEM((rows, depth), bf),
        two_v=pltpu.VMEM((rows, features), f32),
        n3_v=pltpu.VMEM((rows, features), bf),
        enc_v=pltpu.VMEM((rows, features), f32),
        lat_v=pltpu.VMEM((rows, lats), bf),
        dec_v=pltpu.VMEM((rows, features), bf),
        wide=pltpu.VMEM((2, features, 512), bf),
        wide_sem=dma((2,)),
        tall=pltpu.VMEM((2, 512, features), bf),
        tall_sem=dma((2,)),
        send=dma((slots,)),
        recv=dma((slots,)),
        own_sem=dma((slots,)),
        local=dma((20,)),
        z_v=pltpu.VMEM((rows, lats), f32),
    )
    given = dict(
        w0=shards[0],
        w1=shards[1],
        w2=shards[2],
        w3=shards[3],
        w4=shards[4],
        w5=shards[5],
        noise=noise,
        packed=packed,
        cells=cells,
        flags=flags,
        near=near,
        logits=mixture[0][None],
        means=mixture[1],
        logvars=mixture[2],
    )
    names = [*given, *outs, *scratch]
    result = pl.pallas_call(
        functools.partial(forward_kernel, nt, nf, piece, wide_piece, plan, names),
        out_shape=[jax.ShapeDtypeStruct(o[0], o[1]) for o in outs.values()],
        in_specs=[hbm] * 6 + [vmem] * 8,
        out_specs=[o[2] for o in outs.values()],
        scratch_shapes=list(scratch.values()),
        compiler_params=pltpu.CompilerParams(collective_id=0, has_side_effects=True, vmem_limit_bytes=56 << 20),
        name="forward",
    )(*given.values())
    return SimpleNamespace(**dict(zip(outs, result)))


class Chunk:
    def __init__(self, number, weight, first_row, rows, first_col, cols):
        self.number, self.weight = number, weight
        self.first_row, self.rows, self.first_col, self.cols = first_row, rows, first_col, cols
        self.done = 0


def chunk_plan(shapes):
    return [Chunk(k, *item) for k, item in enumerate(split_weights(shapes, (5, 4, 3, 2, 1, 0)))]


LAG = 3
FILL = (0, 0, 1, 1)


class Ring:
    STEPS = 5

    def __init__(self, place, copies, plan, slots, own, diag, from_y, from_x, from_z, outs, free):
        self.p, self.copies, self.plan, self.slots, self.free = place, copies, plan, slots, free
        self.own, self.diag, self.from_y, self.from_x, self.from_z = own, diag, from_y, from_x, from_z
        self.outs, self.open, self.now = outs, [], 0

    def sides(self):
        p = self.p
        out = [(p.zpeer(d), d - 1, p.nz - d - 1) for d in range(1, p.nz)]
        out.append((p.ypeer(), p.nz - 1, p.nz - 1))
        return out + [(p.xpeer(d), p.nz + d - 1, p.nz + p.nx - d - 1) for d in range(1, p.nx)]

    def make_room(self, k):
        if k >= self.slots:
            old = self.plan[k - self.slots]
            while old.done < self.STEPS - 1:
                self.step(old)
            if old in self.open:
                self.open.remove(old)
            for copy in old.sent:
                copy.wait_send()

    def add(self, k):
        chunk = self.plan[k]
        if k >= self.slots:
            for _, here, _ in self.sides():
                pl.semaphore_wait(self.free.at[here], 1)
        chunk.sent = []
        self.open.append(chunk)
        self.step(chunk)

    def tick(self, lag=LAG):
        self.now += 1
        for chunk in list(self.open):
            if chunk.done < self.STEPS - 1 and self.now - chunk.at >= lag:
                self.step(chunk)
            if chunk.done == self.STEPS - 1:
                self.open.remove(chunk)

    def finish(self):
        while self.open:
            self.tick(1)
        for chunk in self.plan[-self.slots :]:
            for copy in chunk.sent:
                copy.wait_send()

    def step(self, chunk):
        (self.one, self.two, self.three, self.four)[chunk.done](chunk)
        chunk.done += 1
        chunk.at = self.now

    def start(self, chunk, key, src, dst, peer):
        copy = self.copies.make(("ring", chunk.number) + key, src, dst, peer)
        copy.start()
        chunk.sent.append(copy)

    def arrived(self, chunk, key, where, peer):
        self.copies.arrived(("ring", chunk.number) + key, where, peer)

    def parts(self, chunk):
        half = half_of(chunk.rows)
        high = pl.ds(half, chunk.rows - half) if half < chunk.rows else None
        return chunk.number % self.slots, pl.ds(0, chunk.rows), pl.ds(0, half), high

    def one(self, chunk):
        p, (s, _, low, high) = self.p, self.parts(chunk)
        for d in range(1, p.nx):
            far = p.xat(d)
            src, dst = self.own.at[s, far, :, 1 - p.y, low], self.diag.at[s, d - 1, :, low]
            self.start(chunk, ("yx", d), src, dst, p.xpeer(d))
            if high is not None:
                src, dst = self.own.at[s, far, :, 1 - p.y, high], self.diag.at[s, d - 1, :, high]
                self.start(chunk, ("xy", d), src, dst, p.ypeer())

    def two(self, chunk):
        p, (s, rows, low, high) = self.p, self.parts(chunk)
        for d in range(1, p.nx):
            self.arrived(chunk, ("yx", d), self.diag.at[s, d - 1, :, low], p.xpeer(d))
            if high is not None:
                self.arrived(chunk, ("xy", d), self.diag.at[s, d - 1, :, high], p.ypeer())

        def add(q, carry):
            for d in range(1, p.nx):
                got = self.diag[s, d - 1, q, low, :].astype(jnp.float32)
                had = self.own[s, p.x, q, 1 - p.y, low, :].astype(jnp.float32)
                self.own[s, p.x, q, 1 - p.y, low, :] = (had + got).astype(jnp.bfloat16)
                if high is not None:
                    far = p.xat(d)
                    got = self.diag[s, d - 1, q, high, :].astype(jnp.float32)
                    had = self.own[s, far, q, p.y, high, :].astype(jnp.float32)
                    self.own[s, far, q, p.y, high, :] = (had + got).astype(jnp.bfloat16)
            return carry

        lax.fori_loop(0, p.nz, add, 0)
        src = self.own.at[s, p.x, :, 1 - p.y, rows]
        self.start(chunk, ("y",), src, self.from_y.at[s, :, rows], p.ypeer())
        for d in range(1, p.nx):
            src = self.own.at[s, p.xat(d), :, p.y, rows]
            self.start(chunk, ("x", d), src, self.from_x.at[s, d - 1, :, rows], p.xpeer(d))

    def three(self, chunk):
        p, (s, rows, _, _) = self.p, self.parts(chunk)
        self.arrived(chunk, ("y",), self.from_y.at[s, :, rows], p.ypeer())
        for d in range(1, p.nx):
            self.arrived(chunk, ("x", d), self.from_x.at[s, d - 1, :, rows], p.xpeer(d))

        def add(q, carry):
            total = self.own[s, p.x, q, p.y, rows, :].astype(jnp.float32)
            total = total + self.from_y[s, q, rows, :].astype(jnp.float32)
            for d in range(1, p.nx):
                total = total + self.from_x[s, d - 1, q, rows, :].astype(jnp.float32)
            self.own[s, p.x, q, p.y, rows, :] = total.astype(jnp.bfloat16)
            return carry

        lax.fori_loop(0, p.nz, add, 0)
        for d in range(1, p.nz):
            to = lax.rem(p.z + d, p.nz)
            src = self.own.at[s, p.x, to, p.y, rows]
            self.start(chunk, ("z", d), src, self.from_z.at[s, d - 1, rows], p.zpeer(d))

    def four(self, chunk):
        p, (s, rows, _, _) = self.p, self.parts(chunk)
        total = self.own[s, p.x, p.z, p.y, rows, :].astype(jnp.float32)
        for d in range(1, p.nz):
            self.arrived(chunk, ("z", d), self.from_z.at[s, d - 1, rows], p.zpeer(d))
            total = total + self.from_z[s, d - 1, rows, :].astype(jnp.float32)
        out = self.outs[chunk.weight]
        out[pl.ds(chunk.first_row, chunk.rows), pl.ds(chunk.first_col, chunk.cols)] = total
        if chunk.number + self.slots < len(self.plan):
            for peer, _, there in self.sides():
                pl.semaphore_signal(self.free.at[there], inc=1, device_id=peer, device_id_type=MESH)


def ring_slots(nt, nf):
    return 3 * (nf // 2 - 1) + 1 + nt // 2 - 1


WEIGHTS = 6


def backward_kernel(nt, nf, plan, slots, names, *refs):
    r = SimpleNamespace(**dict(zip(names, refs)))
    out_of = (r.out0, r.out1, r.out2, r.out3, r.out4, r.out5)
    p = Place(nt, nf)
    held, vectors = r.held, r.vectors
    rows, features = r.gtwo_v.shape
    before = (lax.rem(p.tile + nt - 1, nt), p.fs)
    after = (lax.rem(p.tile + 1, nt), p.fs)
    greet(p.peers() + [before, after])
    copies = Copies(r.send, r.recv)
    local = r.local
    for chunk in plan:
        chunk.done = 0
    ring = Ring(
        p, copies, plan, slots, r.own, r.diag, r.from_y, r.from_x, r.from_z,
        out_of, r.free,
    )
    small = Small(p, copies, "small", r.rest, r.places)
    late = Small(p, copies, "late", r.last, r.late_places)
    small_work = [functools.partial(step, stage) for stage in range(4) for step in (small.send, small.receive)]
    used = [0]

    def fetch(src, dst):
        copy = pltpu.make_async_copy(src, dst, local.at[used[0]])
        used[0] += 1
        copy.start()
        return copy

    inputs = (r.n1, r.att, r.n2, r.act, r.n3, r.lat)
    siblings = (r.sib_n1, r.sib_att, r.sib_n2, r.sib_act, r.sib_n3, r.sib_lat)
    grads = [r.g_tri, r.g_mer, r.g_exp, r.g_red, r.g_enc, r.g_dec]
    others = [r.s_tri, r.s_mer, r.s_exp, r.s_red, r.s_enc, r.s_dec]

    def spread_in(src, dst):
        n = dst.shape[2]
        return [fetch(src.at[:, f * n : (f + 1) * n], dst.at[f]) for f in range(nf)]

    def ship(w):
        for x in range(p.nx):
            copies.start(("g", w, x), grads[w].at[x * 2 + 1 - p.c], others[w].at[x], p.sibling())

    average = Small(p, copies, "kl", r.kl, r.kl_places)
    r.kl[...] = r.klp[...]
    average.send(0)
    loads = spread_in(r.gout, r.g_dec)
    load_z = fetch(r.z, r.pre_v.at[0])
    load_noise = fetch(r.noise, r.pre_v.at[1])
    half = features // 2
    acc = r.acc
    load_var = fetch(r.enc.at[:, pl.ds(half, half)], acc.at[:, pl.ds(half, half)])
    load_two = fetch(r.two, r.hid_v)
    load_cells = fetch(r.cells, r.cells_v)
    for copy in loads:
        copy.wait()
    ship(5)

    keys = []
    for chunk in plan:
        if (chunk.weight, chunk.first_row) not in keys:
            keys.append((chunk.weight, chunk.first_row))

    def load_left(j):
        w, first = keys[j]
        chunk_rows = min(out_of[w].shape[0], 128)
        shard = out_of[w].shape[0]
        for side, src in enumerate((inputs[w], siblings[w])):
            if chunk_rows == shard:
                width = nt * shard
                copy = pltpu.make_async_copy(
                    src, r.left.at[j % 2, side, :, pl.ds(0, width)], r.left_sem.at[j % 2, side]
                )
                copy.start()
            else:
                for t in range(nt):
                    copy = pltpu.make_async_copy(
                        src.at[:, pl.ds(t * shard + first, chunk_rows)],
                        r.left.at[j % 2, side, :, pl.ds(t * chunk_rows, chunk_rows)],
                        r.left_sem.at[j % 2, side],
                    )
                    copy.start()

    state = {"loaded": 0, "ready": -1, "got": set()}

    def sums(k):
        chunk = plan[k]
        w, cols = chunk.weight, chunk.cols
        j = keys.index((w, chunk.first_row))
        while state["loaded"] <= min(j + 1, len(keys) - 1):
            load_left(state["loaded"])
            state["loaded"] += 1
        width = nt * chunk.rows
        if state["ready"] < j:
            for side in range(2):
                where = r.left.at[j % 2, side, :, pl.ds(0, width)]
                pltpu.make_async_copy(where, where, r.left_sem.at[j % 2, side]).wait()
            state["ready"] = j
        if w not in state["got"]:
            state["got"].add(w)
            for x in range(p.nx):
                copies.arrived(("g", w, x), others[w].at[x], p.sibling())
        ring.make_room(k)
        slot = k % slots
        step_rows = 256
        zs = step_rows // (2 * chunk.rows)
        piece = pl.ds(chunk.first_col, cols)

        def one(g, carry):
            lanes = pl.ds(pl.multiple_of(g * step_rows, step_rows), step_rows)
            mine = r.left[j % 2, 0, :, lanes].T
            theirs = r.left[j % 2, 1, :, lanes].T
            for x in range(p.nx):
                total = plain_dot(mine, grads[w][x * 2 + p.c, :, piece])
                total = total + plain_dot(theirs, others[w][x, :, piece])
                total = total.astype(jnp.bfloat16).reshape(zs, 2, chunk.rows, cols)
                r.own[slot, x, pl.ds(g * zs, zs), :, pl.ds(0, chunk.rows), :] = total
            return carry

        lax.fori_loop(0, width // step_rows, one, 0)
        ring.add(k)

    def stream(pieces, buffers, sems, body):
        def copy_of(i):
            src = pieces[i]
            dst = buffers.at[i % 2, pl.ds(0, src.shape[0]), pl.ds(0, src.shape[1])]
            return pltpu.make_async_copy(src, dst, sems.at[i % 2])

        copy_of(0).start()
        for i in range(len(pieces)):
            if i + 1 < len(pieces):
                copy_of(i + 1).start()
            copy_of(i).wait()
            body(i, i % 2)

    wide, tall = r.wide, r.tall

    def times_rows(grad, full, use):
        n = grad.shape[2]
        depth = full.shape[0]
        pieces = [full.at[pl.ds(i * 512, 512), :] for i in range(depth // 512)]

        def body(i, b):
            def one(j, carry):
                at = pl.ds(pl.multiple_of(j * 256, 256), 256)
                total = row_dot(grad[0], tall[b, at, 0:n])
                for f in range(1, nf):
                    total = total + row_dot(grad[f], tall[b, at, f * n : (f + 1) * n])
                use(i * 512 + j * 256, total)
                return carry

            lax.fori_loop(0, 2, one, 0)

        stream(pieces, tall, r.tall_sem, body)

    def times_cols(grad, full, acc, width):
        n = grad.shape[2]
        pieces = [full.at[:, pl.ds(i * width, width)] for i in range(nf * n // width)]

        def body(i, b):
            f, off = divmod(i * width, n)

            def one(j, carry):
                at = pl.ds(pl.multiple_of(j * 256, 256), 256)
                part = row_dot(grad[f, :, off : off + width], wide[b, at, 0:width])
                if i == 0:
                    acc[:, at] = part
                else:
                    acc[:, at] += part
                return carry

            lax.fori_loop(0, features // 256, one, 0)

        stream(pieces, wide, r.wide_sem, body)

    def norm_back(values, grad, gain_row, place_row, use):
        gain = vectors[gain_row : gain_row + 1, :]
        held[place_row : place_row + 2, :] = jnp.zeros((2, features), jnp.float32)

        def one(i, carry):
            at = pl.ds(pl.multiple_of(i * 32, 32), 32)
            v = values[at, :].astype(jnp.float32)
            center = v - jnp.mean(v, -1, keepdims=True)
            inverse = lax.rsqrt(jnp.mean(center * center, -1, keepdims=True) + EPSILON)
            unit = center * inverse
            e = grad[at, :]
            scaled = e * gain
            back = inverse * (
                scaled - jnp.mean(scaled, -1, keepdims=True) - unit * jnp.mean(scaled * unit, -1, keepdims=True)
            )
            held[place_row : place_row + 1, :] += jnp.sum(e * unit, 0, keepdims=True)
            held[place_row + 1 : place_row + 2, :] += jnp.sum(e, 0, keepdims=True)
            use(at, back)
            return carry

        lax.fori_loop(0, rows // 32, one, 0)

    def put(grad, at, value):
        n = grad.shape[2]
        for f in range(nf):
            grad[f, at, :] = value[:, f * n : (f + 1) * n].astype(jnp.bfloat16)

    held[...] = jnp.zeros_like(held)
    chunks_of = [[c.number for c in plan if c.weight == w] for w in range(WEIGHTS)]

    def column_sums(row, grad):
        n = grad.shape[2]
        for f in range(nf):
            held[row : row + 1, f * n : (f + 1) * n] = jnp.sum(grad[f].astype(jnp.float32), 0, keepdims=True)

    average.receive(0)
    average.send(1)

    def keep_latent(first, value):
        acc[:, pl.ds(pl.multiple_of(first, 256), 256)] = value

    times_rows(r.g_dec, r.w_dec, keep_latent)
    average.receive(1)
    average.send(2)
    for k in chunks_of[5]:
        sums(k)
    average.receive(2)
    average.send(3)
    column_sums(8, r.g_dec)

    precision_tab, weighted, squared, log_prior = mixture_tables(r.logits[...], r.means[...], r.logvars[...])
    means, logvars = r.means[...], r.logvars[...]
    comps = means.shape[0]
    weight = r.kl_step[0].astype(jnp.float32) / WARMUP
    average.receive(3)
    total_cells = rows * nt * nf
    slope = weight / (1.0 + jnp.exp((FREE_BITS - r.kl[0:1, :] / total_cells) / SOFT_WIDTH))
    sloped, sloped_weighted = slope * precision_tab, slope * weighted
    ones = jnp.ones((8, half), jnp.float32)
    constant = high_dot(ones, slope * (LOG_TWO_PI + logvars + squared), 1, 1)[0:1]
    r.mix[...] = jnp.zeros_like(r.mix)
    load_z.wait()
    load_noise.wait()
    load_var.wait()

    def divergence(i, carry):
        at = pl.ds(pl.multiple_of(i * 128, 128), 128)
        z, noise = r.pre_v[0, at, :], r.pre_v[1, at, :]
        std = jnp.exp(0.5 * acc[at, half:])
        square = z * z
        log_resp = r.lr[at, :]
        resp = jnp.exp(log_resp)
        value = -0.5 * (constant + high_dot(square, sloped, 1, 1) - 2.0 * high_dot(z, sloped_weighted, 1, 1))
        value = weight * (log_resp + 1.0 - log_prior) - value
        e = resp * (value - jnp.sum(resp * value, -1, keepdims=True))
        on_square = high_dot(e, precision_tab, 1, 0) - slope * high_dot(resp, precision_tab, 1, 0)
        on_z = high_dot(e, weighted, 1, 0) - slope * high_dot(resp, weighted, 1, 0)
        grad_latent = acc[at, 0:half] + on_z - z * on_square
        grad_var = grad_latent * 0.5 * std * noise - 0.5 * slope
        n = r.g_enc.shape[2]
        for f in range(nf):
            part = grad_latent if (f + 1) * n <= half else grad_var
            first = f * n % half
            r.g_enc[f, at, :] = part[:, first : first + n].astype(jnp.bfloat16)
        r.mix[0] += high_dot(e, z, 0, 0)
        r.mix[1] += high_dot(e, square, 0, 0)
        r.mix[2] += high_dot(e, jnp.ones_like(z), 0, 0)
        held[29:30, 0:comps] += jnp.sum(e - weight * resp, 0, keepdims=True)
        return carry

    lax.fori_loop(0, rows // 128, divergence, 0)
    ship(4)
    column_sums(7, r.g_enc)

    def keep_third(first, value):
        acc[:, pl.ds(pl.multiple_of(first, 256), 256)] = value

    times_rows(r.g_enc, r.w_enc, keep_third)
    for k in chunks_of[4]:
        sums(k)
    gtwo = r.gtwo_v
    load_two.wait()

    def to_two(at, back):
        n = r.g_dec.shape[2]
        for f in range(nf):
            lanes = slice(f * n, (f + 1) * n)
            value = r.g_dec[f, at, :].astype(jnp.float32) + back[:, lanes]
            low = value.astype(jnp.bfloat16)
            gtwo[at, lanes] = value
            r.g_red[f, at, :] = low
            held[4:5, lanes] += jnp.sum(low.astype(jnp.float32), 0, keepdims=True)

    norm_back(r.hid_v, acc, 5, 5, to_two)
    ship(3)
    load_hid = fetch(r.hid, r.hid_v)
    zero_order = r.mix[2] - slope * r.tab[2]
    first_order = r.mix[0] - slope * r.tab[0]
    second_order = r.mix[1] - slope * r.tab[1]
    held[13 : 13 + comps, 0:half] = precision_tab * (first_order - means * zero_order)
    held[13 : 13 + comps, half:] = -0.5 * (
        zero_order - precision_tab * (second_order - 2.0 * means * first_order + means * means * zero_order)
    )
    on_prior = held[29:30, 0:comps]
    held[29:30, 0:comps] = on_prior - jnp.exp(log_prior) * jnp.sum(on_prior, -1, keepdims=True)

    pre = r.pre
    pre_v, pre_sem = r.pre_v, r.pre_sem
    tiles = pre.shape[1] // 512

    def pre_copy(i):
        return pltpu.make_async_copy(pre.at[:, pl.ds(i * 512, 512)], pre_v.at[i % 2], pre_sem.at[i % 2])

    pre_copy(0).start()
    n_exp = r.g_exp.shape[2]
    root = 0.7978845608028654

    depth = r.w_red.shape[0]
    pieces = [r.w_red.at[pl.ds(i * 512, 512), :] for i in range(depth // 512)]
    n_red = r.g_red.shape[2]

    def ff_body(i, b):
        if i + 1 < tiles:
            pre_copy(i + 1).start()
        pre_copy(i).wait()
        f, off = divmod(i * 512, n_exp)

        def one(j, carry):
            at = pl.ds(pl.multiple_of(j * 256, 256), 256)
            total = row_dot(r.g_red[0], tall[b, at, 0:n_red])
            for q in range(1, nf):
                total = total + row_dot(r.g_red[q], tall[b, at, q * n_red : (q + 1) * n_red])
            u = pre_v[i % 2, :, at]
            square = u * u
            t = jnp.tanh(root * u * (1.0 + 0.044715 * square))
            slope = 0.5 * (1.0 + t) + (0.5 * root) * u * (1.0 - t * t) * (1.0 + 0.134145 * square)
            value = (total * slope).astype(jnp.bfloat16)
            here = pl.ds(pl.multiple_of(off + j * 256, 256), 256)
            r.g_exp[f, :, here] = value
            row, lane = divmod(i * 512, features)
            there = pl.ds(pl.multiple_of(lane + j * 256, 256), 256)
            held[9 + row : 10 + row, there] = jnp.sum(value.astype(jnp.float32), 0, keepdims=True)
            return carry

        lax.fori_loop(0, 2, one, 0)
        if i == tiles // 2:
            ring.tick()

    stream(pieces, tall, r.tall_sem, ff_body)
    ship(2)
    ring.tick()
    for k in chunks_of[3]:
        sums(k)
        ring.tick()
    times_cols(r.g_exp, r.w_exp, acc, 512)
    ring.tick()
    load_hid.wait()

    def to_one(at, back):
        value = gtwo[at, :] + back
        gtwo[at, :] = value
        put(r.g_mer, at, value)

    norm_back(r.hid_v, acc, 2, 2, to_one)
    ship(1)
    r.rest[...] = held[...]
    grad_att = r.gatt

    def keep_att(first, value):
        grad_att[:, pl.ds(pl.multiple_of(first, 256), 256)] = value.astype(jnp.bfloat16)

    times_rows(r.g_mer, r.w_mer, keep_att)
    ring.tick()
    filler = chunks_of[2] + chunks_of[1]

    pairs = features // 128
    win = r.kext.shape[0] - rows
    edge = win // 2
    count = 3 * edge
    scale = (features // HEADS) ** (-0.5)

    def fetch_pair(i, b):
        lanes = pl.ds(pl.multiple_of(i * 128, 128), 128)
        return [
            pltpu.make_async_copy(r.probs.at[pl.ds(2 * i, 2)], r.p_v.at[b], r.pair_sem.at[b, 0]),
            pltpu.make_async_copy(r.q.at[:, lanes], r.q_v.at[b], r.pair_sem.at[b, 1]),
            pltpu.make_async_copy(r.kext.at[:, lanes], r.k_v.at[b], r.pair_sem.at[b, 2]),
            pltpu.make_async_copy(r.vext.at[:, lanes], r.v_v.at[b], r.pair_sem.at[b, 3]),
        ]

    n_tri = r.g_tri.shape[2]
    rims, came = r.rims, r.came
    dkv = r.dkv

    def pair(i, carry):
        b = lax.rem(i, 2)

        @pl.when(i + 1 < pairs)
        def _():
            for copy in fetch_pair(i + 1, 1 - b):
                copy.start()

        for copy in fetch_pair(i, b):
            copy.wait()
        lanes = pl.ds(pl.multiple_of(i * 128, 128), 128)
        dkv[...] = jnp.zeros_like(dkv)
        for block in range(rows // edge):
            own_rows, keys_at = pl.ds(block * edge, edge), pl.ds(block * edge, count)
            head = lax.broadcasted_iota(jnp.int32, (edge, 128), 1) // 64
            key_head = lax.broadcasted_iota(jnp.int32, (count, 128), 1) // 64
            dq = jnp.zeros((edge, 128), jnp.float32)
            for e in range(2):
                prob = r.p_v[b, e, block]
                zero = jnp.zeros((), jnp.bfloat16)
                go = jnp.where(head == e, grad_att[own_rows, lanes], zero)
                query = jnp.where(head == e, r.q_v[b, own_rows, :], zero)
                key = jnp.where(key_head == e, r.k_v[b, keys_at, :], zero)
                grad_prob = row_dot(go, r.v_v[b, keys_at, :])
                prob32 = prob.astype(jnp.float32)
                delta = jnp.sum(grad_prob * prob32, -1, keepdims=True)
                score = (prob32 * (grad_prob - delta) * scale).astype(jnp.bfloat16)
                dq = dq + plain_dot(score, key)
                dkv[0, keys_at, :] += col_dot(score, query)
                dkv[1, keys_at, :] += col_dot(prob, go)
            at = i * 128
            r.g_tri[lax.div(at, n_tri), own_rows, pl.ds(pl.multiple_of(lax.rem(at, n_tri), 128), 128)] = dq.astype(
                jnp.bfloat16
            )
        for side in range(2):
            at = (side + 1) * features + i * 128
            value = dkv[side].astype(jnp.bfloat16)
            r.g_tri[lax.div(at, n_tri), :, pl.ds(pl.multiple_of(lax.rem(at, n_tri), 128), 128)] = value[edge : edge + rows]
            rims[0, side, :, lanes] = value[0:edge]
            rims[1, side, :, lanes] = value[edge + rows :]
        return carry

    def rim_copy(i, side, up):
        lanes = pl.ds(i * 256, 256)
        src = rims.at[1 if up else 0, side, :, lanes]
        dst = came.at[0 if up else 1, side, :, lanes]
        return copies.make(("rim", i, side, up), src, dst, after if up else before)

    for copy in fetch_pair(0, 0):
        copy.start()
    groups = pairs // 2
    for i in range(groups):
        lax.fori_loop(2 * i, 2 * i + 2, pair, 0)

        @pl.when(p.tile < nt - 1)
        def _():
            for side in range(2):
                rim_copy(i, side, True).start()

        @pl.when(p.tile > 0)
        def _():
            for side in range(2):
                rim_copy(i, side, False).start()

        for _ in range(2):
            small_work.pop(0)()
        for _ in range(FILL[i] if i < len(FILL) else 0):
            sums(filler.pop(0))
        ring.tick()

    def add_rim(up):
        where = pl.ds(0, edge) if up else pl.ds(rows - edge, edge)
        for i in range(groups):
            for side in range(2):
                rim_copy(i, side, up).wait_recv()

        def one(j, carry):
            for side in range(2):
                at = (side + 1) * features + j * 128
                lanes = pl.ds(pl.multiple_of(lax.rem(at, n_tri), 128), 128)
                got = came[0 if up else 1, side, :, pl.ds(pl.multiple_of(j * 128, 128), 128)]
                had = r.g_tri[lax.div(at, n_tri), where, lanes]
                total = had.astype(jnp.float32) + got.astype(jnp.float32)
                r.g_tri[lax.div(at, n_tri), where, lanes] = total.astype(jnp.bfloat16)
            return carry

        lax.fori_loop(0, pairs, one, 0)

    while filler:
        sums(filler.pop(0))
        ring.tick()

    @pl.when(p.tile > 0)
    def _():
        add_rim(True)

    @pl.when(p.tile < nt - 1)
    def _():
        add_rim(False)

    @pl.when(p.tile < nt - 1)
    def _():
        for i in range(groups):
            for side in range(2):
                rim_copy(i, side, True).wait_send()

    @pl.when(p.tile > 0)
    def _():
        for i in range(groups):
            for side in range(2):
                rim_copy(i, side, False).wait_send()

    ship(0)
    for k in chunks_of[0]:
        sums(k)
        ring.tick()
    times_cols(r.g_tri, r.w_tri, acc, n_tri)
    load_cells.wait()
    ring.tick()

    def to_cells(at, back):
        gtwo[at, :] = gtwo[at, :] + back

    norm_back(r.cells_v, acc, 0, 0, to_cells)
    out = fetch(gtwo, r.cells_grad)
    r.last[...] = held[0:8, :]
    for stage in range(4):
        late.send(stage)
        ring.tick(1)
        late.receive(stage)
    ring.finish()
    r.total[...] = r.rest[...]
    r.total[0:2, :] = r.last[0:2, :]
    out.wait()
    copies.drain()


def backward(given, shapes, nt, nf):
    plan = chunk_plan(shapes)
    nz, nx = nt // 2, nf // 2
    rows, features = given["cells"].shape
    depth = given["pre"].shape[1]
    lats = given["z"].shape[1]
    comps = given["means"].shape[0]
    block = (max(c.rows for c in plan), plan[0].cols)
    per_slot = (nx * nt + (max(nx - 1, 1) + 1 + max(nx - 1, 1)) * nz + max(nz - 1, 1)) * block[0] * block[1] * 2
    room = (20 << 20) - 8 * rows * max(nt * c.rows for c in plan)
    slots = max(1, min(len(plan), room // per_slot))
    keys = given["kext"].shape[0]
    edge = (keys - rows) // 2
    small = (32, features)
    bf, f32 = jnp.bfloat16, jnp.float32
    hbm, vmem = pl.BlockSpec(memory_space=pltpu.HBM), pl.BlockSpec(memory_space=pltpu.VMEM)
    smem = pl.BlockSpec(memory_space=pltpu.SMEM)
    outs = dict(
        cells_grad=((rows, features), f32, hbm),
        out0=(shapes[0], f32, vmem),
        out1=(shapes[1], f32, vmem),
        out2=(shapes[2], f32, vmem),
        out3=(shapes[3], f32, vmem),
        out4=(shapes[4], f32, vmem),
        out5=(shapes[5], f32, vmem),
        total=(small, f32, vmem),
    )
    n_copies = len(plan) * ring_slots(nt, nf) + 3 * small_slots(nt, nf) + 6 * nx + features // 256 * 4
    columns = [s[1] for s in shapes]
    dma = pltpu.SemaphoreType.DMA
    near, far = max(nx - 1, 1), max(nz - 1, 1)
    scratch = dict(
        own=pltpu.VMEM((slots, nx, nz, 2) + block, bf),
        diag=pltpu.VMEM((slots, near, nz) + block, bf),
        from_y=pltpu.VMEM((slots, nz) + block, bf),
        from_x=pltpu.VMEM((slots, near, nz) + block, bf),
        from_z=pltpu.VMEM((slots, far) + block, bf),
        g_tri=pltpu.VMEM((nf, rows, columns[0]), bf),
        g_mer=pltpu.VMEM((nf, rows, columns[1]), bf),
        g_exp=pltpu.VMEM((nf, rows, columns[2]), bf),
        g_red=pltpu.VMEM((nf, rows, columns[3]), bf),
        g_enc=pltpu.VMEM((nf, rows, columns[4]), bf),
        g_dec=pltpu.VMEM((nf, rows, columns[5]), bf),
        s_tri=pltpu.VMEM((nx, rows, columns[0]), bf),
        s_mer=pltpu.VMEM((nx, rows, columns[1]), bf),
        s_exp=pltpu.VMEM((nx, rows, columns[2]), bf),
        s_red=pltpu.VMEM((nx, rows, columns[3]), bf),
        s_enc=pltpu.VMEM((nx, rows, columns[4]), bf),
        s_dec=pltpu.VMEM((nx, rows, columns[5]), bf),
        left=pltpu.VMEM((2, 2, rows, max(nt * c.rows for c in plan)), bf),
        left_sem=dma((2, 2)),
        wide=pltpu.VMEM((2, features, max(columns[0], 512)), bf),
        wide_sem=dma((2,)),
        tall=pltpu.VMEM((2, 512, features), bf),
        tall_sem=dma((2,)),
        pre_v=pltpu.VMEM((2, rows, 512), f32),
        pre_sem=dma((2,)),
        gtwo_v=pltpu.VMEM((rows, features), f32),
        hid_v=pltpu.VMEM((rows, features), f32),
        cells_v=pltpu.VMEM((rows, features), bf),
        acc=pltpu.VMEM((rows, features), f32),
        gatt=pltpu.VMEM((rows, features), bf),
        p_v=pltpu.VMEM((2, 2, rows // edge, edge, 3 * edge), bf),
        q_v=pltpu.VMEM((2, rows, 128), bf),
        k_v=pltpu.VMEM((2, keys, 128), bf),
        v_v=pltpu.VMEM((2, keys, 128), bf),
        pair_sem=dma((2, 4)),
        dkv=pltpu.VMEM((2, keys, 128), f32),
        rims=pltpu.VMEM((2, 2, edge, features), bf),
        came=pltpu.VMEM((2, 2, edge, features), bf),
        mix=pltpu.VMEM((3, comps, lats), f32),
        kl=pltpu.VMEM((8, lats), f32),
        kl_places=pltpu.VMEM((small_places(nt, nf), 8, lats), f32),
        held=pltpu.VMEM(small, f32),
        rest=pltpu.VMEM(small, f32),
        places=pltpu.VMEM((small_places(nt, nf),) + small, f32),
        last=pltpu.VMEM((8, features), f32),
        late_places=pltpu.VMEM((small_places(nt, nf), 8, features), f32),
        send=dma((n_copies,)),
        recv=dma((n_copies,)),
        local=dma((nf + 8,)),
        free=pltpu.SemaphoreType.REGULAR((nz + nx,)),
    )
    on_chip = dict(vectors=vmem, lr=vmem, tab=vmem, klp=vmem, logits=vmem, means=vmem, logvars=vmem, kl_step=smem)
    result = pl.pallas_call(
        functools.partial(backward_kernel, nt, nf, plan, slots, [*given, *outs, *scratch]),
        out_shape=[jax.ShapeDtypeStruct(o[0], o[1]) for o in outs.values()],
        in_specs=[on_chip.get(name, hbm) for name in given],
        out_specs=[o[2] for o in outs.values()],
        scratch_shapes=list(scratch.values()),
        compiler_params=pltpu.CompilerParams(collective_id=2, has_side_effects=True, vmem_limit_bytes=62 << 20),
        name="backward",
    )(*given.values())
    return result[0], result[1 : 1 + WEIGHTS], result[1 + WEIGHTS]


def per_device(
    cells,
    spatial_flag,
    neighbours,
    kl_step,
    noise,
    out_cot,
    first_gain,
    first_shift,
    triple_proj,
    merge_proj,
    second_gain,
    second_shift,
    expand_weight,
    expand_bias,
    reduce_weight,
    reduce_bias,
    third_gain,
    third_shift,
    encode_weight,
    encode_bias,
    decode_weight,
    decode_bias,
    mixture_logits,
    mixture_means,
    mixture_logvars,
):
    nt, nf = lax.axis_size("tile"), lax.axis_size("fs")
    features = cells.shape[2]
    mixture = (mixture_logits, mixture_means, mixture_logvars)
    weights = (triple_proj, merge_proj, expand_weight, reduce_weight, encode_weight, decode_weight)
    kept = forward(
        cells[0],
        spatial_flag,
        neighbours[0],
        noise[0],
        weights,
        (
            first_gain,
            first_shift,
            second_gain,
            second_shift,
            reduce_bias,
            third_gain,
            third_shift,
            encode_bias,
            decode_bias,
            expand_bias,
        ),
        mixture,
        nt,
        nf,
    )

    def whole(full):
        return full.reshape(-1, full.shape[-1])

    given = dict(
        two=kept.two,
        pre=kept.pre,
        act=kept.act,
        hid=kept.hid,
        n2=kept.n2,
        att=kept.att,
        probs=kept.probs,
        q=kept.q,
        kext=kept.kext,
        vext=kept.vext,
        cells=cells[0],
        n1=kept.n1,
        lat=kept.lat,
        n3=kept.n3,
        sib_n1=kept.sib_n1,
        sib_att=kept.sib_att,
        sib_n2=kept.sib_n2,
        sib_act=kept.sib_act,
        sib_n3=kept.sib_n3,
        sib_lat=kept.sib_lat,
        z=kept.z,
        enc=kept.enc,
        noise=noise[0],
        gout=out_cot[0],
        w_tri=whole(kept.full0),
        w_mer=whole(kept.full1),
        w_exp=whole(kept.full2),
        w_red=whole(kept.full3),
        w_enc=whole(kept.full4),
        w_dec=whole(kept.full5),
        vectors=kept.vectors,
        lr=kept.lr,
        tab=kept.tab,
        klp=kept.klp,
        logits=mixture_logits[None],
        means=mixture_means,
        logvars=mixture_logvars,
        kl_step=kl_step,
    )
    cells_grad, sums, small = backward(given, [w.shape for w in weights], nt, nf)
    triple_sum, merge_sum, expand_sum, reduce_sum, encode_sum, decode_sum = sums
    index = lax.axis_index("tile") * nf + lax.axis_index("fs")
    piece, wide = first_gain.shape[0], expand_bias.shape[0]
    pieces = lax.dynamic_slice_in_dim(small[:9], index * piece, piece, 1)
    expand_piece = lax.dynamic_slice_in_dim(small[9:13].reshape(-1), index * wide, wide, 0)
    comps, lats = mixture_means.shape
    return (
        kept.decoded[None],
        cells_grad[None],
        pieces[0],
        pieces[1],
        triple_sum,
        merge_sum,
        pieces[2],
        pieces[3],
        expand_sum,
        expand_piece,
        reduce_sum,
        pieces[4],
        pieces[5],
        pieces[6],
        encode_sum,
        pieces[7],
        decode_sum,
        pieces[8],
        small[29, :comps],
        small[13 : 13 + comps, :lats],
        small[13 : 13 + comps, lats : 2 * lats],
    )


def solution(mesh):
    placed = (
        P("fs", "tile", None),
        P("fs", "tile"),
        P("fs", "tile", None),
        P(),
        P("fs", "tile", None),
        P("fs", "tile", None),
        P(("tile", "fs")),
        P(("tile", "fs")),
        P("tile", "fs"),
        P("tile", "fs"),
        P(("tile", "fs")),
        P(("tile", "fs")),
        P("tile", "fs"),
        P(("tile", "fs")),
        P("tile", "fs"),
        P(("tile", "fs")),
        P(("tile", "fs")),
        P(("tile", "fs")),
        P("tile", "fs"),
        P(("tile", "fs")),
        P("tile", "fs"),
        P(("tile", "fs")),
        P(),
        P(),
        P(),
    )
    return jax.shard_map(
        per_device,
        mesh=mesh,
        in_specs=placed,
        out_specs=(
            P("fs", "tile", None),
            P("fs", "tile", None),
            P(("tile", "fs")),
            P(("tile", "fs")),
            P("tile", "fs"),
            P("tile", "fs"),
            P(("tile", "fs")),
            P(("tile", "fs")),
            P("tile", "fs"),
            P(("tile", "fs")),
            P("tile", "fs"),
            P(("tile", "fs")),
            P(("tile", "fs")),
            P(("tile", "fs")),
            P("tile", "fs"),
            P(("tile", "fs")),
            P("tile", "fs"),
            P(("tile", "fs")),
            P(),
            P(),
            P(),
        ),
        check_vma=False,
    )
```

```python
import functools
from types import SimpleNamespace
import jax
import jax.numpy as jnp
from jax import lax
from jax.experimental import pallas as pl
from jax.experimental.pallas import tpu as pltpu

from jax.sharding import PartitionSpec as P

MESH = pl.DeviceIdType.MESH


class Place:
    def __init__(self, nt, nf):
        self.nt, self.nf = nt, nf
        self.nz, self.nx = nt // 2, nf // 2
        tile, fs = lax.axis_index("tile"), lax.axis_index("fs")
        self.tile, self.fs = tile, fs
        self.z, self.y = tile // 2, tile % 2
        self.x, self.c = fs // 2, fs % 2

    def zpeer(self, d):
        return (lax.rem(self.z + d, self.nz) * 2 + self.y, self.fs)

    def ypeer(self):
        return (self.z * 2 + 1 - self.y, self.fs)

    def xat(self, d):
        return lax.rem(self.x + d + self.nx, self.nx)

    def xpeer(self, d):
        return (self.tile, self.xat(d) * 2 + self.c)

    def sibling(self):
        return (self.tile, self.x * 2 + 1 - self.c)

    def peers(self):
        return (
            [self.zpeer(d) for d in range(1, self.nz)]
            + [self.ypeer()]
            + [self.xpeer(d) for d in range(1, self.nx)]
            + [self.sibling()]
        )


def greet(peers):
    barrier = pltpu.get_barrier_semaphore()
    for peer in peers:
        pl.semaphore_signal(barrier, inc=1, device_id=peer, device_id_type=MESH)
    pl.semaphore_wait(barrier, len(peers))


def half_of(rows):
    return max(rows * 5 // 8 // 16 * 16, 16) if rows % 32 == 0 else rows


class Copies:
    def __init__(self, send, recv):
        self.send, self.recv, self.used, self.slots, self.sent = send, recv, 0, {}, []

    def slot(self, key):
        if key not in self.slots:
            self.slots[key] = self.used
            self.used += 1
        return self.slots[key]

    def make(self, key, src, dst, peer):
        at = self.slot(key)
        return pltpu.make_async_remote_copy(
            src_ref=src,
            dst_ref=dst,
            send_sem=self.send.at[at],
            recv_sem=self.recv.at[at],
            device_id=peer,
            device_id_type=MESH,
        )

    def start(self, key, src, dst, peer):
        copy = self.make(key, src, dst, peer)
        copy.start()
        self.sent.append(copy)

    def arrived(self, key, where, peer):
        self.make(key, where, where, peer).wait_recv()

    def drain(self):
        for copy in self.sent:
            copy.wait_send()
        self.sent = []


GATHER_LAG = (0, 2, 4, 6, 7)


class Gather:
    def __init__(self, place, copies, local, key, shard, full, first, rows, left, cols):
        self.p, self.copies, self.local, self.key = place, copies, local, key
        self.shard, self.full, self.first, self.rows = shard, full, first, rows
        self.n, self.left, self.cols = shard.shape[1], left, cols

    def at(self, z, y, x, c, first=0, rows=None):
        rows = self.rows if rows is None else rows
        column = pl.multiple_of((x * 2 + c) * self.n + self.left, 128)
        return self.full.at[z, y, pl.ds(self.first + first, rows), pl.ds(column, self.cols)]

    def one(self):
        p = self.p
        mine = self.shard.at[pl.ds(self.first, self.rows), pl.ds(self.left, self.cols)]
        here = self.at(p.z, p.y, p.x, p.c)
        self.own = pltpu.make_async_copy(mine, here, self.local.at[self.copies.slot((self.key, "own"))])
        self.own.start()
        for d in range(1, p.nz):
            self.copies.start((self.key, "z", d), mine, here, p.zpeer(d))

    def two(self):
        p, key = self.p, self.key
        self.own.wait()
        for d in range(1, p.nz):
            zz = lax.rem(p.z - d + p.nz, p.nz)
            self.copies.arrived((key, "z", d), self.at(zz, p.y, p.x, p.c), p.zpeer(d))
        block = self.at(slice(None), p.y, p.x, p.c)
        self.copies.start((key, "y"), block, block, p.ypeer())
        for d in range(1, p.nx):
            self.copies.start((key, "x", d), block, block, p.xpeer(d))
        self.copies.start((key, "c"), block, block, p.sibling())

    def three(self):
        p, key = self.p, self.key
        half = half_of(self.rows)
        block = self.at(slice(None), 1 - p.y, p.x, p.c)
        self.copies.arrived((key, "y"), block, p.ypeer())
        part = self.at(slice(None), 1 - p.y, p.x, p.c, 0, half)
        for d in range(1, p.nx):
            self.copies.start((key, "yx", d), part, part, p.xpeer(d))
        for d in range(1, p.nx):
            far = p.xat(-d)
            other = self.at(slice(None), p.y, far, p.c)
            self.copies.arrived((key, "x", d), other, p.xpeer(d))
            if half < self.rows:
                part = self.at(slice(None), p.y, far, p.c, half, self.rows - half)
                self.copies.start((key, "xy", d), part, part, p.ypeer())
            self.copies.start((key, "xc", d), other, other, p.sibling())
        self.copies.start((key, "yc"), block, block, p.sibling())

    def four(self):
        p, key = self.p, self.key
        half = half_of(self.rows)
        for d in range(1, p.nx):
            far = p.xat(-d)
            self.copies.arrived((key, "yx", d), self.at(slice(None), 1 - p.y, far, p.c, 0, half), p.xpeer(d))
            if half < self.rows:
                part = self.at(slice(None), 1 - p.y, far, p.c, half, self.rows - half)
                self.copies.arrived((key, "xy", d), part, p.ypeer())
            block = self.at(slice(None), 1 - p.y, far, p.c)
            self.copies.start((key, "dc", d), block, block, p.sibling())

    def five(self):
        p, key = self.p, self.key
        other = 1 - p.c
        self.copies.arrived((key, "c"), self.at(slice(None), p.y, p.x, other), p.sibling())
        self.copies.arrived((key, "yc"), self.at(slice(None), 1 - p.y, p.x, other), p.sibling())
        for d in range(1, p.nx):
            far = p.xat(-d)
            self.copies.arrived((key, "xc", d), self.at(slice(None), p.y, far, other), p.sibling())
            self.copies.arrived((key, "dc", d), self.at(slice(None), 1 - p.y, far, other), p.sibling())


def gather_slots(nt, nf):
    return 1 + (nt // 2 - 1) + 3 + 5 * (nf // 2 - 1)


class Small:
    def __init__(self, place, copies, key, mine, slots):
        self.p, self.copies, self.key, self.mine, self.slots = place, copies, key, mine, slots
        p = place
        self.stages = [
            ([p.zpeer(d) for d in range(1, p.nz)], p.z, p.nz),
            ([p.ypeer()], p.y, 2),
            ([p.xpeer(d) for d in range(1, p.nx)], p.x, p.nx),
            ([p.sibling()], p.c, 2),
        ]

    def base(self, stage):
        return sum(size for _, _, size in self.stages[:stage])

    def send(self, stage):
        peers, at, _ = self.stages[stage]
        base = self.base(stage)
        self.slots[base + at] = self.mine[...]
        for i, peer in enumerate(peers):
            self.copies.start((self.key, stage, i), self.slots.at[base + at], self.slots.at[base + at], peer)

    def receive(self, stage):
        peers, at, size = self.stages[stage]
        base = self.base(stage)
        for i, peer in enumerate(peers):
            came = lax.rem(at - i - 1 + size, size)
            self.copies.arrived((self.key, stage, i), self.slots.at[base + came], peer)
        total = self.slots[base]
        for j in range(1, size):
            total = total + self.slots[base + j]
        self.mine[...] = total


def small_slots(nt, nf):
    return nt // 2 - 1 + 1 + nf // 2 - 1 + 1


def small_places(nt, nf):
    return nt // 2 + 2 + nf // 2 + 2


HEADS = 16
WIN = 128
WARMUP = 1000


EPSILON = 1e-05
LOG_TWO_PI = 1.8378770664093453
FREE_BITS = 0.8
SOFT_WIDTH = 0.1
HIGHEST = lax.Precision.HIGHEST


def row_dot(left, right):
    return lax.dot_general(left, right, (((1,), (1,)), ((), ())), preferred_element_type=jnp.float32)


def col_dot(left, right):
    return lax.dot_general(left, right, (((0,), (0,)), ((), ())), preferred_element_type=jnp.float32)


def plain_dot(left, right):
    return jnp.dot(left, right, preferred_element_type=jnp.float32)


def split_weights(shapes, order):
    cols = min(n for _, n in shapes)
    out = []
    for w in order:
        r, n = shapes[w]
        rows = min(r, 128)
        for i in range(r // rows):
            for j in range(n // cols):
                out.append((w, i * rows, rows, j * cols, cols))
    return out


def high_dot(left, right, left_dim, right_dim):
    return lax.dot_general(
        left,
        right,
        (((left_dim,), (right_dim,)), ((), ())),
        precision=HIGHEST,
        preferred_element_type=jnp.float32,
    )


def mixture_tables(logits, means, logvars):
    precision_tab = jnp.exp(-logvars)
    weighted = means * precision_tab
    top = jnp.max(logits, -1, keepdims=True)
    log_prior = logits - top - jnp.log(jnp.sum(jnp.exp(logits - top), -1, keepdims=True))
    return precision_tab, weighted, means * weighted, log_prior


def forward_kernel(nt, nf, piece, wide_piece, plan, names, *refs):
    r = SimpleNamespace(**dict(zip(names, refs)))
    p = Place(nt, nf)
    w_of, full_of = (r.w0, r.w1, r.w2, r.w3, r.w4, r.w5), (r.full0, r.full1, r.full2, r.full3, r.full4, r.full5)
    sib_of = (r.sib_n1, r.sib_att, r.sib_n2, r.sib_act, r.sib_n3, r.sib_lat)
    rows, features = r.cells.shape
    tiles, mine, vectors = r.tiles, r.mine, r.vectors
    edge = WIN
    lane = lax.broadcasted_iota(jnp.int32, (16, 128), 1)
    row = lax.broadcasted_iota(jnp.int32, (16, 128), 0)
    index = p.tile * nf + p.fs
    narrow_here = lane // piece == lax.rem(index, 128 // piece)
    wide_here = lane // wide_piece == lax.rem(index, 128 // wide_piece)
    here = ((row != 9) & narrow_here) | ((row == 9) & wide_here)
    mine[...] = jnp.where(here, r.packed[...].astype(jnp.float32), 0.0).astype(jnp.bfloat16)
    before = (lax.rem(p.tile + nt - 1, nt), p.fs)
    after = (lax.rem(p.tile + 1, nt), p.fs)
    greet(p.peers() + [before, after])
    copies = Copies(r.send, r.recv)
    local = r.local
    steps = [Gather(p, copies, r.own_sem, "vec", mine, tiles, 0, 16, 0, 128)]
    ends = {}
    for i, (w, f, n, c, m) in enumerate(plan):
        steps.append(Gather(p, copies, r.own_sem, i, w_of[w], full_of[w], f, n, c, m))
        ends[w] = i + 1
    lags = list(zip(("one", "two", "three", "four", "five"), GATHER_LAG))
    clock = [0]

    def pump(count=1):
        for _ in range(count):
            k = clock[0]
            for name, lag in lags[::-1]:
                if 0 <= k - lag < len(steps):
                    getattr(steps[k - lag], name)()
            clock[0] += 1

    def need(step):
        while clock[0] <= step + GATHER_LAG[-1]:
            pump()

    used = [0]

    def share(i, src):
        copies.start(("a", i), src, sib_of[i], p.sibling())

    def put_out(src, dst):
        copy = pltpu.make_async_copy(src, dst, local.at[used[0]])
        used[0] += 1
        copy.start()
        return copy

    pump(2)
    first_row = p.tile * rows
    bias = r.bias
    near = r.near
    flag_row = r.flags[...].astype(jnp.float32)
    count = 3 * edge
    for b in range(rows // edge):
        at = b * edge
        diagonal = lax.broadcasted_iota(jnp.int32, (edge, edge), 0) == lax.broadcasted_iota(jnp.int32, (edge, edge), 1)
        flag = jnp.sum(jnp.where(diagonal, flag_row[:, at : at + edge], 0.0), 1, keepdims=True)
        offset = lax.broadcasted_iota(jnp.int32, (edge, count), 1)
        key = first_row + at - edge + offset
        query = first_row + at + lax.broadcasted_iota(jnp.int32, (edge, count), 0)
        listed = key == query
        for n in range(near.shape[1]):
            listed = listed | (near[at : at + edge, n : n + 1] == key)
        own_bin = (key >= first_row) & (key < first_row + rows)
        allowed = listed & ((flag > 0.5) | own_bin)
        bias[b] = jnp.where(allowed, 0.0, -1e30)
        pump()
    need(0)
    for at in range(nt * nf // (128 // piece)):
        total = jnp.zeros((16, 128), jnp.float32)
        for j in range(128 // piece):
            t, f = divmod(at * (128 // piece) + j, nf)
            total = total + tiles[t // 2, t % 2, :, f * 128 : (f + 1) * 128].astype(jnp.float32)
        vectors[0:9, at * 128 : (at + 1) * 128] = total[0:9]
    for at in range(nt * nf // (128 // wide_piece)):
        total = jnp.zeros((1, 128), jnp.float32)
        for j in range(128 // wide_piece):
            t, f = divmod(at * (128 // wide_piece) + j, nf)
            total = total + tiles[t // 2, t % 2, :, f * 128 : (f + 1) * 128].astype(jnp.float32)[9:10]
        vectors[9 + at // 8 : 10 + at // 8, at % 8 * 128 : (at % 8 + 1) * 128] = total

    def norm(values, gain_row, out):
        gain, shift = vectors[gain_row : gain_row + 1, :], vectors[gain_row + 1 : gain_row + 2, :]

        def one(i, carry):
            at = pl.ds(pl.multiple_of(i * 32, 32), 32)
            v = values[at, :].astype(jnp.float32)
            center = v - jnp.mean(v, -1, keepdims=True)
            inverse = lax.rsqrt(jnp.mean(center * center, -1, keepdims=True) + EPSILON)
            out[at, :] = (center * inverse * gain + shift).astype(jnp.bfloat16)
            return carry

        lax.fori_loop(0, rows // 32, one, 0)

    def stream(pieces, buffers, sems, body):
        def copy_of(i):
            src = pieces[i]
            dst = buffers.at[i % 2, pl.ds(0, src.shape[0]), pl.ds(0, src.shape[1])]
            return pltpu.make_async_copy(src, dst, sems.at[i % 2])

        copy_of(0).start()
        for i in range(len(pieces)):
            if i + 1 < len(pieces):
                copy_of(i + 1).start()
            copy_of(i).wait()
            body(i, i % 2)

    wide, tall = r.wide, r.tall

    def full_cols(w, first, width):
        full = full_of[w]
        flat = full.reshape(full.shape[0] * full.shape[1] * full.shape[2], full.shape[3])
        return flat.at[:, pl.ds(first, width)]

    def full_rows(w, first, height):
        full = full_of[w]
        flat = full.reshape(full.shape[0] * full.shape[1] * full.shape[2], full.shape[3])
        return flat.at[pl.ds(first, height), :]

    def times(left, w, width, use, tick=False):
        total = full_of[w].shape[3]
        depth = left.shape[1]

        def body(i, b):
            def one(j, carry):
                at = pl.multiple_of(j * 256, 256)
                use(i, at, plain_dot(left[...], wide[b, pl.ds(0, depth), pl.ds(at, 256)]))
                return carry

            lax.fori_loop(0, width // 256, one, 0)
            if tick:
                pump()

        stream([full_cols(w, i * width, width) for i in range(total // width)], wide, r.wide_sem, body)

    normed_one = r.n1_v
    norm(r.cells, 0, normed_one)
    outs = [put_out(normed_one, r.n1)]
    share(0, normed_one)
    need(ends[0])
    queries, keys, values = r.q_v, r.k_v, r.v_v
    here_rows = pl.ds(edge, rows)

    def keep_triple(i, at, value):
        value = value.astype(jnp.bfloat16)
        lanes = pl.ds(at, 256)
        which, first = divmod(i * 512, features)
        lanes = pl.ds(pl.multiple_of(first + at, 256), 256)
        if which == 0:
            queries[:, lanes] = value
        elif which == 1:
            keys[here_rows, lanes] = value
        else:
            values[here_rows, lanes] = value

    times(normed_one, 0, 512, keep_triple)

    def halo(which, up):
        ref = (keys, values)[which]
        if up:
            return copies.make(("halo", which, up), ref.at[pl.ds(rows, edge)], ref.at[pl.ds(0, edge)], after)
        return copies.make(("halo", which, up), ref.at[pl.ds(edge, edge)], ref.at[pl.ds(rows + edge, edge)], before)

    @pl.when(p.tile < nt - 1)
    def _():
        for which in range(2):
            halo(which, True).start()

    @pl.when(p.tile > 0)
    def _():
        for which in range(2):
            halo(which, False).start()

    outs.append(put_out(queries, r.q))
    pump()

    @pl.when(p.tile > 0)
    def _():
        for which in range(2):
            halo(which, True).wait_recv()

    @pl.when(p.tile == 0)
    def _():
        for ref in (keys, values):
            ref[0:edge, :] = jnp.zeros((edge, features), jnp.bfloat16)

    @pl.when(p.tile < nt - 1)
    def _():
        for which in range(2):
            halo(which, False).wait_recv()

    @pl.when(p.tile == nt - 1)
    def _():
        for ref in (keys, values):
            ref[edge + rows :, :] = jnp.zeros((edge, features), jnp.bfloat16)

    outs.append(put_out(keys, r.kext))
    outs.append(put_out(values, r.vext))

    pairs = features // 128
    scale = (features // HEADS) ** (-0.5)
    attended = r.att_v

    def probs_out(i, b):
        return pltpu.make_async_copy(r.p_v.at[b], r.probs.at[pl.ds(2 * i, 2)], r.pair_sem.at[b])

    def pair(i, carry):
        b = lax.rem(i, 2)

        @pl.when(i >= 2)
        def _():
            probs_out(i - 2, b).wait()

        lanes = pl.ds(pl.multiple_of(i * 128, 128), 128)
        zero = jnp.zeros((), jnp.bfloat16)
        for block in range(rows // edge):
            own_rows, keys_at = pl.ds(block * edge, edge), pl.ds(block * edge, count)
            head = lax.broadcasted_iota(jnp.int32, (edge, 128), 1) // 64
            key_head = lax.broadcasted_iota(jnp.int32, (count, 128), 1) // 64
            total = jnp.zeros((edge, 128), jnp.float32)
            for e in range(2):
                query = jnp.where(head == e, queries[own_rows, lanes], zero)
                score = row_dot(query, keys[keys_at, lanes]) * scale + bias[block]
                top = jnp.max(score, -1, keepdims=True)
                power = jnp.exp(score - top)
                prob = (power / jnp.sum(power, -1, keepdims=True)).astype(jnp.bfloat16)
                r.p_v[b, e, block] = prob
                total = total + plain_dot(prob, jnp.where(key_head == e, values[keys_at, lanes], zero))
            attended[own_rows, lanes] = total.astype(jnp.bfloat16)
        probs_out(i, b).start()
        return carry

    for i in range(pairs // 2):
        lax.fori_loop(2 * i, 2 * i + 2, pair, 0)
        pump()
    for i in range(pairs - 2, pairs):
        probs_out(i, i % 2).wait()
    outs.append(put_out(attended, r.att))
    share(1, attended)
    need(ends[1])
    hidden = r.hid_v

    def keep_hidden(i, at, value):
        lanes = pl.ds(pl.multiple_of(i * 512 + at, 256), 256)
        hidden[:, lanes] = r.cells[:, lanes].astype(jnp.float32) + value

    times(attended, 1, 512, keep_hidden)
    outs.append(put_out(hidden, r.hid))
    normed_two = r.n2_v
    norm(hidden, 2, normed_two)
    outs.append(put_out(normed_two, r.n2))
    share(2, normed_two)
    need(ends[2])

    root = 0.7978845608028654
    activated, pre_v = r.act_v, r.pre_v

    def pre_out(i):
        return pltpu.make_async_copy(pre_v.at[i % 2], r.pre.at[:, pl.ds(i * 512, 512)], r.pre_sem.at[i % 2])

    def keep_pre(i, at, value):
        vec_row, first = divmod(i * 512, features)
        lanes = pl.ds(pl.multiple_of(first + at, 256), 256)
        u = value + vectors[9 + vec_row : 10 + vec_row, lanes]
        pre_v[i % 2, :, pl.ds(at, 256)] = u
        gate = 0.5 * (1.0 + jnp.tanh(root * (u + 0.044715 * u * u * u)))
        activated[:, pl.ds(pl.multiple_of(i * 512 + at, 256), 256)] = (u * gate).astype(jnp.bfloat16)

    def up_body(i, b):
        if i >= 2:
            pre_out(i - 2).wait()

        def one(j, carry):
            at = pl.multiple_of(j * 256, 256)
            keep_pre(i, at, plain_dot(normed_two[...], wide[b, :, pl.ds(at, 256)]))
            return carry

        lax.fori_loop(0, 2, one, 0)
        pre_out(i).start()
        if i % 4 == 3:
            pump()

    depth = activated.shape[1]
    up_count = depth // 512
    stream([full_cols(2, i * 512, 512) for i in range(up_count)], wide, r.wide_sem, up_body)
    for i in range(up_count - 2, up_count):
        pre_out(i).wait()
    outs.append(put_out(activated, r.act))
    share(3, activated)
    need(ends[3])
    second = r.two_v

    def down_body(i, b):
        def one(j, carry):
            lanes = pl.ds(pl.multiple_of(j * 256, 256), 256)
            part = plain_dot(activated[:, i * 512 : (i + 1) * 512], tall[b, :, lanes])
            if i == 0:
                second[:, lanes] = hidden[:, lanes] + vectors[4:5, lanes] + part
            else:
                second[:, lanes] += part
            return carry

        lax.fori_loop(0, features // 256, one, 0)

    stream([full_rows(3, i * 512, 512) for i in range(up_count)], tall, r.tall_sem, down_body)
    outs.append(put_out(second, r.two))
    normed_three = r.n3_v
    norm(second, 5, normed_three)
    outs.append(put_out(normed_three, r.n3))
    share(4, normed_three)
    need(ends[4])
    encoded = r.enc_v

    def keep_encoded(i, at, value):
        lanes = pl.ds(pl.multiple_of(i * 512 + at, 256), 256)
        encoded[:, lanes] = value + vectors[7:8, lanes]

    times(normed_three, 4, 512, keep_encoded)
    outs.append(put_out(encoded, r.enc))
    latent, latent32 = r.lat_v, r.z_v
    half = features // 2
    tables = mixture_tables(r.logits[...], r.means[...], r.logvars[...])
    precision_tab, weighted, squared, log_prior = tables
    logvars = r.logvars[...]
    ones = jnp.ones((8, half), jnp.float32)
    constant = log_prior - 0.5 * (
        LOG_TWO_PI * half + high_dot(ones, logvars, 1, 1)[0:1] + high_dot(ones, squared, 1, 1)[0:1]
    )
    r.tab[...] = jnp.zeros_like(r.tab)
    r.klp[...] = jnp.zeros_like(r.klp)

    def latent_rows(i, carry):
        at = pl.ds(pl.multiple_of(i * 128, 128), 128)
        log_var, noise = encoded[at, half:], r.noise[at, :]
        z = encoded[at, 0:half] + jnp.exp(0.5 * log_var) * noise
        latent32[at, :] = z
        latent[at, :] = z.astype(jnp.bfloat16)
        square = z * z
        ell = constant - 0.5 * (high_dot(square, precision_tab, 1, 1) - 2.0 * high_dot(z, weighted, 1, 1))
        ell = ell - jnp.max(ell, -1, keepdims=True)
        log_resp = ell - jnp.log(jnp.sum(jnp.exp(ell), -1, keepdims=True))
        r.lr[at, :] = log_resp
        resp = jnp.exp(log_resp)
        r.tab[0] += high_dot(resp, z, 0, 0)
        r.tab[1] += high_dot(resp, square, 0, 0)
        r.tab[2] += high_dot(resp, jnp.ones_like(z), 0, 0)
        r.klp[0:1, :] += -0.5 * jnp.sum(LOG_TWO_PI + log_var + noise * noise, 0, keepdims=True)
        return carry

    lax.fori_loop(0, rows // 128, latent_rows, 0)
    cross = r.tab[2] * (LOG_TWO_PI + logvars + squared) + precision_tab * r.tab[1] - 2.0 * weighted * r.tab[0]
    r.klp[0:1, :] += 0.5 * jnp.sum(cross, 0, keepdims=True)
    outs.append(put_out(latent, r.lat))
    outs.append(put_out(latent32, r.z))
    share(5, latent)
    need(ends[5])
    decoded = r.dec_v

    def keep_decoded(i, at, value):
        lanes = pl.ds(pl.multiple_of(i * 512 + at, 256), 256)
        decoded[:, lanes] = (second[:, lanes] + value + vectors[8:9, lanes]).astype(jnp.bfloat16)

    times(latent, 5, 512, keep_decoded)
    outs.append(put_out(decoded, r.decoded))
    for i in range(6):
        copies.arrived(("a", i), sib_of[i], p.sibling())
    for copy in outs:
        copy.wait()

    @pl.when(p.tile < nt - 1)
    def _():
        for which in range(2):
            halo(which, True).wait_send()

    @pl.when(p.tile > 0)
    def _():
        for which in range(2):
            halo(which, False).wait_send()

    copies.drain()


def forward(cells, flags, near, noise, shards, small_vectors, mixture, nt, nf):
    piece, wide_piece = small_vectors[0].shape[0], small_vectors[9].shape[0]
    packed = jnp.stack([jnp.tile(v, 128 // v.shape[0]) for v in small_vectors])
    packed = jnp.pad(packed, ((0, 6), (0, 0)))
    shapes = [s.shape for s in shards]
    plan = split_weights(shapes, range(6))
    rows, features = cells.shape
    lats = noise.shape[1]
    depth = shapes[2][1] * nf
    keys = rows + 2 * WIN
    blocks = rows // WIN
    bf, f32 = jnp.bfloat16, jnp.float32
    nz = nt // 2
    slots = gather_slots(nt, nf) * (len(plan) + 1) + 4 + 6
    comps = mixture[1].shape[0]
    hbm, vmem = pl.BlockSpec(memory_space=pltpu.HBM), pl.BlockSpec(memory_space=pltpu.VMEM)
    fulls = [((nz, 2, s, n * nf), bf, hbm) for s, n in shapes]
    outs = dict(
        full0=fulls[0],
        full1=fulls[1],
        full2=fulls[2],
        full3=fulls[3],
        full4=fulls[4],
        full5=fulls[5],
        sib_n1=((rows, features), bf, hbm),
        sib_att=((rows, features), bf, hbm),
        sib_n2=((rows, features), bf, hbm),
        sib_act=((rows, depth), bf, hbm),
        sib_n3=((rows, features), bf, hbm),
        sib_lat=((rows, lats), bf, hbm),
        z=((rows, lats), f32, hbm),
        lr=((rows, comps), f32, vmem),
        tab=((3, comps, lats), f32, vmem),
        klp=((8, lats), f32, vmem),
        n1=((rows, features), bf, hbm),
        q=((rows, features), bf, hbm),
        kext=((keys, features), bf, hbm),
        vext=((keys, features), bf, hbm),
        probs=((HEADS, blocks, WIN, 3 * WIN), bf, hbm),
        att=((rows, features), bf, hbm),
        hid=((rows, features), f32, hbm),
        n2=((rows, features), bf, hbm),
        pre=((rows, depth), f32, hbm),
        act=((rows, depth), bf, hbm),
        two=((rows, features), f32, hbm),
        n3=((rows, features), bf, hbm),
        enc=((rows, features), f32, hbm),
        lat=((rows, lats), bf, hbm),
        decoded=((rows, features), bf, hbm),
        vectors=((16, features), f32, vmem),
    )
    dma = pltpu.SemaphoreType.DMA
    scratch = dict(
        tiles=pltpu.VMEM((nz, 2, 16, nf * 128), bf),
        mine=pltpu.VMEM((16, 128), bf),
        bias=pltpu.VMEM((blocks, WIN, 3 * WIN), f32),
        n1_v=pltpu.VMEM((rows, features), bf),
        q_v=pltpu.VMEM((rows, features), bf),
        k_v=pltpu.VMEM((keys, features), bf),
        v_v=pltpu.VMEM((keys, features), bf),
        p_v=pltpu.VMEM((2, 2, blocks, WIN, 3 * WIN), bf),
        pair_sem=dma((2,)),
        att_v=pltpu.VMEM((rows, features), bf),
        hid_v=pltpu.VMEM((rows, features), f32),
        n2_v=pltpu.VMEM((rows, features), bf),
        pre_v=pltpu.VMEM((2, rows, 512), f32),
        pre_sem=dma((2,)),
        act_v=pltpu.VMEM((rows, depth), bf),
        two_v=pltpu.VMEM((rows, features), f32),
        n3_v=pltpu.VMEM((rows, features), bf),
        enc_v=pltpu.VMEM((rows, features), f32),
        lat_v=pltpu.VMEM((rows, lats), bf),
        dec_v=pltpu.VMEM((rows, features), bf),
        wide=pltpu.VMEM((2, features, 512), bf),
        wide_sem=dma((2,)),
        tall=pltpu.VMEM((2, 512, features), bf),
        tall_sem=dma((2,)),
        send=dma((slots,)),
        recv=dma((slots,)),
        own_sem=dma((slots,)),
        local=dma((20,)),
        z_v=pltpu.VMEM((rows, lats), f32),
    )
    given = dict(
        w0=shards[0],
        w1=shards[1],
        w2=shards[2],
        w3=shards[3],
        w4=shards[4],
        w5=shards[5],
        noise=noise,
        packed=packed,
        cells=cells,
        flags=flags,
        near=near,
        logits=mixture[0][None],
        means=mixture[1],
        logvars=mixture[2],
    )
    names = [*given, *outs, *scratch]
    result = pl.pallas_call(
        functools.partial(forward_kernel, nt, nf, piece, wide_piece, plan, names),
        out_shape=[jax.ShapeDtypeStruct(o[0], o[1]) for o in outs.values()],
        in_specs=[hbm] * 6 + [vmem] * 8,
        out_specs=[o[2] for o in outs.values()],
        scratch_shapes=list(scratch.values()),
        compiler_params=pltpu.CompilerParams(collective_id=0, has_side_effects=True, vmem_limit_bytes=56 << 20),
        name="forward",
    )(*given.values())
    return SimpleNamespace(**dict(zip(outs, result)))


class Chunk:
    def __init__(self, number, weight, first_row, rows, first_col, cols):
        self.number, self.weight = number, weight
        self.first_row, self.rows, self.first_col, self.cols = first_row, rows, first_col, cols
        self.done = 0


def chunk_plan(shapes):
    return [Chunk(k, *item) for k, item in enumerate(split_weights(shapes, (5, 4, 3, 2, 1, 0)))]


LAG = 4
FILL = (1, 1, 1, 1)


class Ring:
    STEPS = 5

    def __init__(self, place, copies, plan, slots, own, diag, from_y, from_x, from_z, outs, free):
        self.p, self.copies, self.plan, self.slots, self.free = place, copies, plan, slots, free
        self.own, self.diag, self.from_y, self.from_x, self.from_z = own, diag, from_y, from_x, from_z
        self.outs, self.open, self.now = outs, [], 0

    def sides(self):
        p = self.p
        out = [(p.zpeer(d), d - 1, p.nz - d - 1) for d in range(1, p.nz)]
        out.append((p.ypeer(), p.nz - 1, p.nz - 1))
        return out + [(p.xpeer(d), p.nz + d - 1, p.nz + p.nx - d - 1) for d in range(1, p.nx)]

    def make_room(self, k):
        if k >= self.slots:
            old = self.plan[k - self.slots]
            while old.done < self.STEPS - 1:
                self.step(old)
            if old in self.open:
                self.open.remove(old)
            for copy in old.sent:
                copy.wait_send()

    def add(self, k):
        chunk = self.plan[k]
        if k >= self.slots:
            for _, here, _ in self.sides():
                pl.semaphore_wait(self.free.at[here], 1)
        chunk.sent = []
        self.open.append(chunk)
        self.step(chunk)

    def tick(self, lag=LAG):
        self.now += 1
        for chunk in list(self.open):
            if chunk.done < self.STEPS - 1 and self.now - chunk.at >= lag:
                self.step(chunk)
            if chunk.done == self.STEPS - 1:
                self.open.remove(chunk)

    def finish(self):
        while self.open:
            self.tick(1)
        for chunk in self.plan[-self.slots :]:
            for copy in chunk.sent:
                copy.wait_send()

    def step(self, chunk):
        (self.one, self.two, self.three, self.four)[chunk.done](chunk)
        chunk.done += 1
        chunk.at = self.now

    def start(self, chunk, key, src, dst, peer):
        copy = self.copies.make(("ring", chunk.number) + key, src, dst, peer)
        copy.start()
        chunk.sent.append(copy)

    def arrived(self, chunk, key, where, peer):
        self.copies.arrived(("ring", chunk.number) + key, where, peer)

    def parts(self, chunk):
        half = half_of(chunk.rows)
        high = pl.ds(half, chunk.rows - half) if half < chunk.rows else None
        return chunk.number % self.slots, pl.ds(0, chunk.rows), pl.ds(0, half), high

    def one(self, chunk):
        p, (s, _, low, high) = self.p, self.parts(chunk)
        for d in range(1, p.nx):
            far = p.xat(d)
            src, dst = self.own.at[s, far, :, 1 - p.y, low], self.diag.at[s, d - 1, :, low]
            self.start(chunk, ("yx", d), src, dst, p.xpeer(d))
            if high is not None:
                src, dst = self.own.at[s, far, :, 1 - p.y, high], self.diag.at[s, d - 1, :, high]
                self.start(chunk, ("xy", d), src, dst, p.ypeer())

    def two(self, chunk):
        p, (s, rows, low, high) = self.p, self.parts(chunk)
        for d in range(1, p.nx):
            self.arrived(chunk, ("yx", d), self.diag.at[s, d - 1, :, low], p.xpeer(d))
            if high is not None:
                self.arrived(chunk, ("xy", d), self.diag.at[s, d - 1, :, high], p.ypeer())

        def add(q, carry):
            for d in range(1, p.nx):
                got = self.diag[s, d - 1, q, low, :].astype(jnp.float32)
                had = self.own[s, p.x, q, 1 - p.y, low, :].astype(jnp.float32)
                self.own[s, p.x, q, 1 - p.y, low, :] = (had + got).astype(jnp.bfloat16)
                if high is not None:
                    far = p.xat(d)
                    got = self.diag[s, d - 1, q, high, :].astype(jnp.float32)
                    had = self.own[s, far, q, p.y, high, :].astype(jnp.float32)
                    self.own[s, far, q, p.y, high, :] = (had + got).astype(jnp.bfloat16)
            return carry

        lax.fori_loop(0, p.nz, add, 0)
        src = self.own.at[s, p.x, :, 1 - p.y, rows]
        self.start(chunk, ("y",), src, self.from_y.at[s, :, rows], p.ypeer())
        for d in range(1, p.nx):
            src = self.own.at[s, p.xat(d), :, p.y, rows]
            self.start(chunk, ("x", d), src, self.from_x.at[s, d - 1, :, rows], p.xpeer(d))

    def three(self, chunk):
        p, (s, rows, _, _) = self.p, self.parts(chunk)
        self.arrived(chunk, ("y",), self.from_y.at[s, :, rows], p.ypeer())
        for d in range(1, p.nx):
            self.arrived(chunk, ("x", d), self.from_x.at[s, d - 1, :, rows], p.xpeer(d))

        def add(q, carry):
            total = self.own[s, p.x, q, p.y, rows, :].astype(jnp.float32)
            total = total + self.from_y[s, q, rows, :].astype(jnp.float32)
            for d in range(1, p.nx):
                total = total + self.from_x[s, d - 1, q, rows, :].astype(jnp.float32)
            self.own[s, p.x, q, p.y, rows, :] = total.astype(jnp.bfloat16)
            return carry

        lax.fori_loop(0, p.nz, add, 0)
        for d in range(1, p.nz):
            to = lax.rem(p.z + d, p.nz)
            src = self.own.at[s, p.x, to, p.y, rows]
            self.start(chunk, ("z", d), src, self.from_z.at[s, d - 1, rows], p.zpeer(d))

    def four(self, chunk):
        p, (s, rows, _, _) = self.p, self.parts(chunk)
        total = self.own[s, p.x, p.z, p.y, rows, :].astype(jnp.float32)
        for d in range(1, p.nz):
            self.arrived(chunk, ("z", d), self.from_z.at[s, d - 1, rows], p.zpeer(d))
            total = total + self.from_z[s, d - 1, rows, :].astype(jnp.float32)
        out = self.outs[chunk.weight]
        out[pl.ds(chunk.first_row, chunk.rows), pl.ds(chunk.first_col, chunk.cols)] = total
        if chunk.number + self.slots < len(self.plan):
            for peer, _, there in self.sides():
                pl.semaphore_signal(self.free.at[there], inc=1, device_id=peer, device_id_type=MESH)


def ring_slots(nt, nf):
    return 3 * (nf // 2 - 1) + 1 + nt // 2 - 1


WEIGHTS = 6


def backward_kernel(nt, nf, plan, slots, names, *refs):
    r = SimpleNamespace(**dict(zip(names, refs)))
    out_of = (r.out0, r.out1, r.out2, r.out3, r.out4, r.out5)
    p = Place(nt, nf)
    held, vectors = r.held, r.vectors
    rows, features = r.gtwo_v.shape
    before = (lax.rem(p.tile + nt - 1, nt), p.fs)
    after = (lax.rem(p.tile + 1, nt), p.fs)
    greet(p.peers() + [before, after])
    copies = Copies(r.send, r.recv)
    local = r.local
    for chunk in plan:
        chunk.done = 0
    ring = Ring(
        p, copies, plan, slots, r.own, r.diag, r.from_y, r.from_x, r.from_z,
        out_of, r.free,
    )
    small = Small(p, copies, "small", r.rest, r.places)
    late = Small(p, copies, "late", r.last, r.late_places)
    small_work = [functools.partial(step, stage) for stage in range(4) for step in (small.send, small.receive)]
    used = [0]

    def fetch(src, dst):
        copy = pltpu.make_async_copy(src, dst, local.at[used[0]])
        used[0] += 1
        copy.start()
        return copy

    inputs = (r.n1, r.att, r.n2, r.act, r.n3, r.lat)
    siblings = (r.sib_n1, r.sib_att, r.sib_n2, r.sib_act, r.sib_n3, r.sib_lat)
    grads = [r.g_tri, r.g_mer, r.g_exp, r.g_red, r.g_enc, r.g_dec]
    others = [r.s_tri, r.s_mer, r.s_exp, r.s_red, r.s_enc, r.s_dec]

    def spread_in(src, dst):
        n = dst.shape[2]
        return [fetch(src.at[:, f * n : (f + 1) * n], dst.at[f]) for f in range(nf)]

    def ship(w):
        for x in range(p.nx):
            copies.start(("g", w, x), grads[w].at[x * 2 + 1 - p.c], others[w].at[x], p.sibling())

    average = Small(p, copies, "kl", r.kl, r.kl_places)
    r.kl[...] = r.klp[...]
    average.send(0)
    loads = spread_in(r.gout, r.g_dec)
    load_z = fetch(r.z, r.pre_v.at[0])
    load_noise = fetch(r.noise, r.pre_v.at[1])
    half = features // 2
    acc = r.acc
    load_var = fetch(r.enc.at[:, pl.ds(half, half)], acc.at[:, pl.ds(half, half)])
    load_two = fetch(r.two, r.hid_v)
    load_cells = fetch(r.cells, r.cells_v)
    for copy in loads:
        copy.wait()
    ship(5)

    keys = []
    for chunk in plan:
        if (chunk.weight, chunk.first_row) not in keys:
            keys.append((chunk.weight, chunk.first_row))

    def load_left(j):
        w, first = keys[j]
        chunk_rows = min(out_of[w].shape[0], 128)
        shard = out_of[w].shape[0]
        for side, src in enumerate((inputs[w], siblings[w])):
            if chunk_rows == shard:
                width = nt * shard
                copy = pltpu.make_async_copy(
                    src, r.left.at[j % 2, side, :, pl.ds(0, width)], r.left_sem.at[j % 2, side]
                )
                copy.start()
            else:
                for t in range(nt):
                    copy = pltpu.make_async_copy(
                        src.at[:, pl.ds(t * shard + first, chunk_rows)],
                        r.left.at[j % 2, side, :, pl.ds(t * chunk_rows, chunk_rows)],
                        r.left_sem.at[j % 2, side],
                    )
                    copy.start()

    state = {"loaded": 0, "ready": -1, "got": set()}

    def sums(k):
        chunk = plan[k]
        w, cols = chunk.weight, chunk.cols
        j = keys.index((w, chunk.first_row))
        while state["loaded"] <= min(j + 1, len(keys) - 1):
            load_left(state["loaded"])
            state["loaded"] += 1
        width = nt * chunk.rows
        if state["ready"] < j:
            for side in range(2):
                where = r.left.at[j % 2, side, :, pl.ds(0, width)]
                pltpu.make_async_copy(where, where, r.left_sem.at[j % 2, side]).wait()
            state["ready"] = j
        if w not in state["got"]:
            state["got"].add(w)
            for x in range(p.nx):
                copies.arrived(("g", w, x), others[w].at[x], p.sibling())
        ring.make_room(k)
        slot = k % slots
        step_rows = 256
        zs = step_rows // (2 * chunk.rows)
        piece = pl.ds(chunk.first_col, cols)

        def one(g, carry):
            lanes = pl.ds(pl.multiple_of(g * step_rows, step_rows), step_rows)
            mine = r.left[j % 2, 0, :, lanes].T
            theirs = r.left[j % 2, 1, :, lanes].T
            for x in range(p.nx):
                total = plain_dot(mine, grads[w][x * 2 + p.c, :, piece])
                total = total + plain_dot(theirs, others[w][x, :, piece])
                total = total.astype(jnp.bfloat16).reshape(zs, 2, chunk.rows, cols)
                r.own[slot, x, pl.ds(g * zs, zs), :, pl.ds(0, chunk.rows), :] = total
            return carry

        lax.fori_loop(0, width // step_rows, one, 0)
        ring.add(k)

    def stream(pieces, buffers, sems, body):
        def copy_of(i):
            src = pieces[i]
            dst = buffers.at[i % 2, pl.ds(0, src.shape[0]), pl.ds(0, src.shape[1])]
            return pltpu.make_async_copy(src, dst, sems.at[i % 2])

        copy_of(0).start()
        for i in range(len(pieces)):
            if i + 1 < len(pieces):
                copy_of(i + 1).start()
            copy_of(i).wait()
            body(i, i % 2)

    wide, tall = r.wide, r.tall

    def times_rows(grad, full, use):
        n = grad.shape[2]
        depth = full.shape[0]
        pieces = [full.at[pl.ds(i * 512, 512), :] for i in range(depth // 512)]

        def body(i, b):
            def one(j, carry):
                at = pl.ds(pl.multiple_of(j * 256, 256), 256)
                total = row_dot(grad[0], tall[b, at, 0:n])
                for f in range(1, nf):
                    total = total + row_dot(grad[f], tall[b, at, f * n : (f + 1) * n])
                use(i * 512 + j * 256, total)
                return carry

            lax.fori_loop(0, 2, one, 0)

        stream(pieces, tall, r.tall_sem, body)

    def times_cols(grad, full, acc, width):
        n = grad.shape[2]
        pieces = [full.at[:, pl.ds(i * width, width)] for i in range(nf * n // width)]

        def body(i, b):
            f, off = divmod(i * width, n)

            def one(j, carry):
                at = pl.ds(pl.multiple_of(j * 256, 256), 256)
                part = row_dot(grad[f, :, off : off + width], wide[b, at, 0:width])
                if i == 0:
                    acc[:, at] = part
                else:
                    acc[:, at] += part
                return carry

            lax.fori_loop(0, features // 256, one, 0)

        stream(pieces, wide, r.wide_sem, body)

    def norm_back(values, grad, gain_row, place_row, use):
        gain = vectors[gain_row : gain_row + 1, :]
        held[place_row : place_row + 2, :] = jnp.zeros((2, features), jnp.float32)

        def one(i, carry):
            at = pl.ds(pl.multiple_of(i * 32, 32), 32)
            v = values[at, :].astype(jnp.float32)
            center = v - jnp.mean(v, -1, keepdims=True)
            inverse = lax.rsqrt(jnp.mean(center * center, -1, keepdims=True) + EPSILON)
            unit = center * inverse
            e = grad[at, :]
            scaled = e * gain
            back = inverse * (
                scaled - jnp.mean(scaled, -1, keepdims=True) - unit * jnp.mean(scaled * unit, -1, keepdims=True)
            )
            held[place_row : place_row + 1, :] += jnp.sum(e * unit, 0, keepdims=True)
            held[place_row + 1 : place_row + 2, :] += jnp.sum(e, 0, keepdims=True)
            use(at, back)
            return carry

        lax.fori_loop(0, rows // 32, one, 0)

    def put(grad, at, value):
        n = grad.shape[2]
        for f in range(nf):
            grad[f, at, :] = value[:, f * n : (f + 1) * n].astype(jnp.bfloat16)

    held[...] = jnp.zeros_like(held)
    chunks_of = [[c.number for c in plan if c.weight == w] for w in range(WEIGHTS)]

    def column_sums(row, grad):
        n = grad.shape[2]
        for f in range(nf):
            held[row : row + 1, f * n : (f + 1) * n] = jnp.sum(grad[f].astype(jnp.float32), 0, keepdims=True)

    average.receive(0)
    average.send(1)

    def keep_latent(first, value):
        acc[:, pl.ds(pl.multiple_of(first, 256), 256)] = value

    times_rows(r.g_dec, r.w_dec, keep_latent)
    average.receive(1)
    average.send(2)
    for k in chunks_of[5]:
        sums(k)
    average.receive(2)
    average.send(3)
    column_sums(8, r.g_dec)

    precision_tab, weighted, squared, log_prior = mixture_tables(r.logits[...], r.means[...], r.logvars[...])
    means, logvars = r.means[...], r.logvars[...]
    comps = means.shape[0]
    weight = r.kl_step[0].astype(jnp.float32) / WARMUP
    average.receive(3)
    total_cells = rows * nt * nf
    slope = weight / (1.0 + jnp.exp((FREE_BITS - r.kl[0:1, :] / total_cells) / SOFT_WIDTH))
    sloped, sloped_weighted = slope * precision_tab, slope * weighted
    ones = jnp.ones((8, half), jnp.float32)
    constant = high_dot(ones, slope * (LOG_TWO_PI + logvars + squared), 1, 1)[0:1]
    r.mix[...] = jnp.zeros_like(r.mix)
    load_z.wait()
    load_noise.wait()
    load_var.wait()

    def divergence(i, carry):
        at = pl.ds(pl.multiple_of(i * 128, 128), 128)
        z, noise = r.pre_v[0, at, :], r.pre_v[1, at, :]
        std = jnp.exp(0.5 * acc[at, half:])
        square = z * z
        log_resp = r.lr[at, :]
        resp = jnp.exp(log_resp)
        value = -0.5 * (constant + high_dot(square, sloped, 1, 1) - 2.0 * high_dot(z, sloped_weighted, 1, 1))
        value = weight * (log_resp + 1.0 - log_prior) - value
        e = resp * (value - jnp.sum(resp * value, -1, keepdims=True))
        on_square = high_dot(e, precision_tab, 1, 0) - slope * high_dot(resp, precision_tab, 1, 0)
        on_z = high_dot(e, weighted, 1, 0) - slope * high_dot(resp, weighted, 1, 0)
        grad_latent = acc[at, 0:half] + on_z - z * on_square
        grad_var = grad_latent * 0.5 * std * noise - 0.5 * slope
        n = r.g_enc.shape[2]
        for f in range(nf):
            part = grad_latent if (f + 1) * n <= half else grad_var
            first = f * n % half
            r.g_enc[f, at, :] = part[:, first : first + n].astype(jnp.bfloat16)
        r.mix[0] += high_dot(e, z, 0, 0)
        r.mix[1] += high_dot(e, square, 0, 0)
        r.mix[2] += high_dot(e, jnp.ones_like(z), 0, 0)
        held[29:30, 0:comps] += jnp.sum(e - weight * resp, 0, keepdims=True)
        return carry

    lax.fori_loop(0, rows // 128, divergence, 0)
    ship(4)
    column_sums(7, r.g_enc)

    def keep_third(first, value):
        acc[:, pl.ds(pl.multiple_of(first, 256), 256)] = value

    times_rows(r.g_enc, r.w_enc, keep_third)
    for k in chunks_of[4]:
        sums(k)
    gtwo = r.gtwo_v
    load_two.wait()

    def to_two(at, back):
        n = r.g_dec.shape[2]
        for f in range(nf):
            lanes = slice(f * n, (f + 1) * n)
            value = r.g_dec[f, at, :].astype(jnp.float32) + back[:, lanes]
            low = value.astype(jnp.bfloat16)
            gtwo[at, lanes] = value
            r.g_red[f, at, :] = low
            held[4:5, lanes] += jnp.sum(low.astype(jnp.float32), 0, keepdims=True)

    norm_back(r.hid_v, acc, 5, 5, to_two)
    ship(3)
    load_hid = fetch(r.hid, r.hid_v)
    zero_order = r.mix[2] - slope * r.tab[2]
    first_order = r.mix[0] - slope * r.tab[0]
    second_order = r.mix[1] - slope * r.tab[1]
    held[13 : 13 + comps, 0:half] = precision_tab * (first_order - means * zero_order)
    held[13 : 13 + comps, half:] = -0.5 * (
        zero_order - precision_tab * (second_order - 2.0 * means * first_order + means * means * zero_order)
    )
    on_prior = held[29:30, 0:comps]
    held[29:30, 0:comps] = on_prior - jnp.exp(log_prior) * jnp.sum(on_prior, -1, keepdims=True)

    pre = r.pre
    pre_v, pre_sem = r.pre_v, r.pre_sem
    tiles = pre.shape[1] // 512

    def pre_copy(i):
        return pltpu.make_async_copy(pre.at[:, pl.ds(i * 512, 512)], pre_v.at[i % 2], pre_sem.at[i % 2])

    pre_copy(0).start()
    n_exp = r.g_exp.shape[2]
    root = 0.7978845608028654

    depth = r.w_red.shape[0]
    pieces = [r.w_red.at[pl.ds(i * 512, 512), :] for i in range(depth // 512)]
    n_red = r.g_red.shape[2]

    def ff_body(i, b):
        if i + 1 < tiles:
            pre_copy(i + 1).start()
        pre_copy(i).wait()
        f, off = divmod(i * 512, n_exp)

        def one(j, carry):
            at = pl.ds(pl.multiple_of(j * 256, 256), 256)
            total = row_dot(r.g_red[0], tall[b, at, 0:n_red])
            for q in range(1, nf):
                total = total + row_dot(r.g_red[q], tall[b, at, q * n_red : (q + 1) * n_red])
            u = pre_v[i % 2, :, at]
            square = u * u
            t = jnp.tanh(root * u * (1.0 + 0.044715 * square))
            slope = 0.5 * (1.0 + t) + (0.5 * root) * u * (1.0 - t * t) * (1.0 + 0.134145 * square)
            value = (total * slope).astype(jnp.bfloat16)
            here = pl.ds(pl.multiple_of(off + j * 256, 256), 256)
            r.g_exp[f, :, here] = value
            row, lane = divmod(i * 512, features)
            there = pl.ds(pl.multiple_of(lane + j * 256, 256), 256)
            held[9 + row : 10 + row, there] = jnp.sum(value.astype(jnp.float32), 0, keepdims=True)
            return carry

        lax.fori_loop(0, 2, one, 0)
        if i == tiles // 2:
            ring.tick()

    stream(pieces, tall, r.tall_sem, ff_body)
    ship(2)
    ring.tick()
    for k in chunks_of[3]:
        sums(k)
        ring.tick()
    times_cols(r.g_exp, r.w_exp, acc, 512)
    ring.tick()
    load_hid.wait()

    def to_one(at, back):
        value = gtwo[at, :] + back
        gtwo[at, :] = value
        put(r.g_mer, at, value)

    norm_back(r.hid_v, acc, 2, 2, to_one)
    ship(1)
    r.rest[...] = held[...]
    small_work.pop(0)()
    grad_att = r.gatt

    def keep_att(first, value):
        grad_att[:, pl.ds(pl.multiple_of(first, 256), 256)] = value.astype(jnp.bfloat16)

    times_rows(r.g_mer, r.w_mer, keep_att)
    ring.tick()
    filler = chunks_of[2] + chunks_of[1]

    pairs = features // 128
    win = r.kext.shape[0] - rows
    edge = win // 2
    count = 3 * edge
    scale = (features // HEADS) ** (-0.5)

    def fetch_pair(i, b):
        lanes = pl.ds(pl.multiple_of(i * 128, 128), 128)
        return [
            pltpu.make_async_copy(r.probs.at[pl.ds(2 * i, 2)], r.p_v.at[b], r.pair_sem.at[b, 0]),
            pltpu.make_async_copy(r.q.at[:, lanes], r.q_v.at[b], r.pair_sem.at[b, 1]),
            pltpu.make_async_copy(r.kext.at[:, lanes], r.k_v.at[b], r.pair_sem.at[b, 2]),
            pltpu.make_async_copy(r.vext.at[:, lanes], r.v_v.at[b], r.pair_sem.at[b, 3]),
        ]

    n_tri = r.g_tri.shape[2]
    rims, came = r.rims, r.came
    dkv = r.dkv

    def pair(i, carry):
        b = lax.rem(i, 2)

        @pl.when(i + 1 < pairs)
        def _():
            for copy in fetch_pair(i + 1, 1 - b):
                copy.start()

        for copy in fetch_pair(i, b):
            copy.wait()
        lanes = pl.ds(pl.multiple_of(i * 128, 128), 128)
        dkv[...] = jnp.zeros_like(dkv)
        for block in range(rows // edge):
            own_rows, keys_at = pl.ds(block * edge, edge), pl.ds(block * edge, count)
            head = lax.broadcasted_iota(jnp.int32, (edge, 128), 1) // 64
            key_head = lax.broadcasted_iota(jnp.int32, (count, 128), 1) // 64
            dq = jnp.zeros((edge, 128), jnp.float32)
            for e in range(2):
                prob = r.p_v[b, e, block]
                zero = jnp.zeros((), jnp.bfloat16)
                go = jnp.where(head == e, grad_att[own_rows, lanes], zero)
                query = jnp.where(head == e, r.q_v[b, own_rows, :], zero)
                key = jnp.where(key_head == e, r.k_v[b, keys_at, :], zero)
                grad_prob = row_dot(go, r.v_v[b, keys_at, :])
                prob32 = prob.astype(jnp.float32)
                delta = jnp.sum(grad_prob * prob32, -1, keepdims=True)
                score = (prob32 * (grad_prob - delta) * scale).astype(jnp.bfloat16)
                dq = dq + plain_dot(score, key)
                dkv[0, keys_at, :] += col_dot(score, query)
                dkv[1, keys_at, :] += col_dot(prob, go)
            at = i * 128
            r.g_tri[lax.div(at, n_tri), own_rows, pl.ds(pl.multiple_of(lax.rem(at, n_tri), 128), 128)] = dq.astype(
                jnp.bfloat16
            )
        for side in range(2):
            at = (side + 1) * features + i * 128
            value = dkv[side].astype(jnp.bfloat16)
            r.g_tri[lax.div(at, n_tri), :, pl.ds(pl.multiple_of(lax.rem(at, n_tri), 128), 128)] = value[edge : edge + rows]
            rims[0, side, :, lanes] = value[0:edge]
            rims[1, side, :, lanes] = value[edge + rows :]
        return carry

    def rim_copy(i, side, up):
        lanes = pl.ds(i * 256, 256)
        src = rims.at[1 if up else 0, side, :, lanes]
        dst = came.at[0 if up else 1, side, :, lanes]
        return copies.make(("rim", i, side, up), src, dst, after if up else before)

    for copy in fetch_pair(0, 0):
        copy.start()
    groups = pairs // 2
    for i in range(groups):
        lax.fori_loop(2 * i, 2 * i + 2, pair, 0)

        @pl.when(p.tile < nt - 1)
        def _():
            for side in range(2):
                rim_copy(i, side, True).start()

        @pl.when(p.tile > 0)
        def _():
            for side in range(2):
                rim_copy(i, side, False).start()

        if i % 2 == 1:
            small_work.pop(0)()
            small_work.pop(0)()
        for _ in range(FILL[i] if i < len(FILL) else 0):
            sums(filler.pop(0))
        ring.tick()

    def add_rim(up):
        where = pl.ds(0, edge) if up else pl.ds(rows - edge, edge)
        for i in range(groups):
            for side in range(2):
                rim_copy(i, side, up).wait_recv()

        def one(j, carry):
            for side in range(2):
                at = (side + 1) * features + j * 128
                lanes = pl.ds(pl.multiple_of(lax.rem(at, n_tri), 128), 128)
                got = came[0 if up else 1, side, :, pl.ds(pl.multiple_of(j * 128, 128), 128)]
                had = r.g_tri[lax.div(at, n_tri), where, lanes]
                total = had.astype(jnp.float32) + got.astype(jnp.float32)
                r.g_tri[lax.div(at, n_tri), where, lanes] = total.astype(jnp.bfloat16)
            return carry

        lax.fori_loop(0, pairs, one, 0)

    while filler:
        sums(filler.pop(0))
        ring.tick()
    small_work.pop(0)()
    small_work.pop(0)()

    @pl.when(p.tile > 0)
    def _():
        add_rim(True)

    @pl.when(p.tile < nt - 1)
    def _():
        add_rim(False)

    @pl.when(p.tile < nt - 1)
    def _():
        for i in range(groups):
            for side in range(2):
                rim_copy(i, side, True).wait_send()

    @pl.when(p.tile > 0)
    def _():
        for i in range(groups):
            for side in range(2):
                rim_copy(i, side, False).wait_send()

    ship(0)
    for k in chunks_of[0]:
        sums(k)
        ring.tick()
    small_work.pop(0)()
    times_cols(r.g_tri, r.w_tri, acc, n_tri)
    load_cells.wait()
    ring.tick()

    def to_cells(at, back):
        gtwo[at, :] = gtwo[at, :] + back

    norm_back(r.cells_v, acc, 0, 0, to_cells)
    out = fetch(gtwo, r.cells_grad)
    r.last[...] = held[0:8, :]
    for stage in range(4):
        late.send(stage)
        ring.tick(1)
        late.receive(stage)
    ring.finish()
    r.total[...] = r.rest[...]
    r.total[0:2, :] = r.last[0:2, :]
    out.wait()
    copies.drain()


def backward(given, shapes, nt, nf):
    plan = chunk_plan(shapes)
    nz, nx = nt // 2, nf // 2
    rows, features = given["cells"].shape
    depth = given["pre"].shape[1]
    lats = given["z"].shape[1]
    comps = given["means"].shape[0]
    block = (max(c.rows for c in plan), plan[0].cols)
    per_slot = (nx * nt + (max(nx - 1, 1) + 1 + max(nx - 1, 1)) * nz + max(nz - 1, 1)) * block[0] * block[1] * 2
    room = (20 << 20) - 8 * rows * max(nt * c.rows for c in plan)
    slots = max(1, min(len(plan), room // per_slot))
    keys = given["kext"].shape[0]
    edge = (keys - rows) // 2
    small = (32, features)
    bf, f32 = jnp.bfloat16, jnp.float32
    hbm, vmem = pl.BlockSpec(memory_space=pltpu.HBM), pl.BlockSpec(memory_space=pltpu.VMEM)
    smem = pl.BlockSpec(memory_space=pltpu.SMEM)
    outs = dict(
        cells_grad=((rows, features), f32, hbm),
        out0=(shapes[0], f32, vmem),
        out1=(shapes[1], f32, vmem),
        out2=(shapes[2], f32, vmem),
        out3=(shapes[3], f32, vmem),
        out4=(shapes[4], f32, vmem),
        out5=(shapes[5], f32, vmem),
        total=(small, f32, vmem),
    )
    n_copies = len(plan) * ring_slots(nt, nf) + 3 * small_slots(nt, nf) + 6 * nx + features // 256 * 4
    columns = [s[1] for s in shapes]
    dma = pltpu.SemaphoreType.DMA
    near, far = max(nx - 1, 1), max(nz - 1, 1)
    scratch = dict(
        own=pltpu.VMEM((slots, nx, nz, 2) + block, bf),
        diag=pltpu.VMEM((slots, near, nz) + block, bf),
        from_y=pltpu.VMEM((slots, nz) + block, bf),
        from_x=pltpu.VMEM((slots, near, nz) + block, bf),
        from_z=pltpu.VMEM((slots, far) + block, bf),
        g_tri=pltpu.VMEM((nf, rows, columns[0]), bf),
        g_mer=pltpu.VMEM((nf, rows, columns[1]), bf),
        g_exp=pltpu.VMEM((nf, rows, columns[2]), bf),
        g_red=pltpu.VMEM((nf, rows, columns[3]), bf),
        g_enc=pltpu.VMEM((nf, rows, columns[4]), bf),
        g_dec=pltpu.VMEM((nf, rows, columns[5]), bf),
        s_tri=pltpu.VMEM((nx, rows, columns[0]), bf),
        s_mer=pltpu.VMEM((nx, rows, columns[1]), bf),
        s_exp=pltpu.VMEM((nx, rows, columns[2]), bf),
        s_red=pltpu.VMEM((nx, rows, columns[3]), bf),
        s_enc=pltpu.VMEM((nx, rows, columns[4]), bf),
        s_dec=pltpu.VMEM((nx, rows, columns[5]), bf),
        left=pltpu.VMEM((2, 2, rows, max(nt * c.rows for c in plan)), bf),
        left_sem=dma((2, 2)),
        wide=pltpu.VMEM((2, features, max(columns[0], 512)), bf),
        wide_sem=dma((2,)),
        tall=pltpu.VMEM((2, 512, features), bf),
        tall_sem=dma((2,)),
        pre_v=pltpu.VMEM((2, rows, 512), f32),
        pre_sem=dma((2,)),
        gtwo_v=pltpu.VMEM((rows, features), f32),
        hid_v=pltpu.VMEM((rows, features), f32),
        cells_v=pltpu.VMEM((rows, features), bf),
        acc=pltpu.VMEM((rows, features), f32),
        gatt=pltpu.VMEM((rows, features), bf),
        p_v=pltpu.VMEM((2, 2, rows // edge, edge, 3 * edge), bf),
        q_v=pltpu.VMEM((2, rows, 128), bf),
        k_v=pltpu.VMEM((2, keys, 128), bf),
        v_v=pltpu.VMEM((2, keys, 128), bf),
        pair_sem=dma((2, 4)),
        dkv=pltpu.VMEM((2, keys, 128), f32),
        rims=pltpu.VMEM((2, 2, edge, features), bf),
        came=pltpu.VMEM((2, 2, edge, features), bf),
        mix=pltpu.VMEM((3, comps, lats), f32),
        kl=pltpu.VMEM((8, lats), f32),
        kl_places=pltpu.VMEM((small_places(nt, nf), 8, lats), f32),
        held=pltpu.VMEM(small, f32),
        rest=pltpu.VMEM(small, f32),
        places=pltpu.VMEM((small_places(nt, nf),) + small, f32),
        last=pltpu.VMEM((8, features), f32),
        late_places=pltpu.VMEM((small_places(nt, nf), 8, features), f32),
        send=dma((n_copies,)),
        recv=dma((n_copies,)),
        local=dma((nf + 8,)),
        free=pltpu.SemaphoreType.REGULAR((nz + nx,)),
    )
    on_chip = dict(vectors=vmem, lr=vmem, tab=vmem, klp=vmem, logits=vmem, means=vmem, logvars=vmem, kl_step=smem)
    result = pl.pallas_call(
        functools.partial(backward_kernel, nt, nf, plan, slots, [*given, *outs, *scratch]),
        out_shape=[jax.ShapeDtypeStruct(o[0], o[1]) for o in outs.values()],
        in_specs=[on_chip.get(name, hbm) for name in given],
        out_specs=[o[2] for o in outs.values()],
        scratch_shapes=list(scratch.values()),
        compiler_params=pltpu.CompilerParams(collective_id=2, has_side_effects=True, vmem_limit_bytes=62 << 20),
        name="backward",
    )(*given.values())
    return result[0], result[1 : 1 + WEIGHTS], result[1 + WEIGHTS]


def per_device(
    cells,
    spatial_flag,
    neighbours,
    kl_step,
    noise,
    out_cot,
    first_gain,
    first_shift,
    triple_proj,
    merge_proj,
    second_gain,
    second_shift,
    expand_weight,
    expand_bias,
    reduce_weight,
    reduce_bias,
    third_gain,
    third_shift,
    encode_weight,
    encode_bias,
    decode_weight,
    decode_bias,
    mixture_logits,
    mixture_means,
    mixture_logvars,
):
    nt, nf = lax.axis_size("tile"), lax.axis_size("fs")
    features = cells.shape[2]
    mixture = (mixture_logits, mixture_means, mixture_logvars)
    weights = (triple_proj, merge_proj, expand_weight, reduce_weight, encode_weight, decode_weight)
    kept = forward(
        cells[0],
        spatial_flag,
        neighbours[0],
        noise[0],
        weights,
        (
            first_gain,
            first_shift,
            second_gain,
            second_shift,
            reduce_bias,
            third_gain,
            third_shift,
            encode_bias,
            decode_bias,
            expand_bias,
        ),
        mixture,
        nt,
        nf,
    )

    def whole(full):
        return full.reshape(-1, full.shape[-1])

    given = dict(
        two=kept.two,
        pre=kept.pre,
        act=kept.act,
        hid=kept.hid,
        n2=kept.n2,
        att=kept.att,
        probs=kept.probs,
        q=kept.q,
        kext=kept.kext,
        vext=kept.vext,
        cells=cells[0],
        n1=kept.n1,
        lat=kept.lat,
        n3=kept.n3,
        sib_n1=kept.sib_n1,
        sib_att=kept.sib_att,
        sib_n2=kept.sib_n2,
        sib_act=kept.sib_act,
        sib_n3=kept.sib_n3,
        sib_lat=kept.sib_lat,
        z=kept.z,
        enc=kept.enc,
        noise=noise[0],
        gout=out_cot[0],
        w_tri=whole(kept.full0),
        w_mer=whole(kept.full1),
        w_exp=whole(kept.full2),
        w_red=whole(kept.full3),
        w_enc=whole(kept.full4),
        w_dec=whole(kept.full5),
        vectors=kept.vectors,
        lr=kept.lr,
        tab=kept.tab,
        klp=kept.klp,
        logits=mixture_logits[None],
        means=mixture_means,
        logvars=mixture_logvars,
        kl_step=kl_step,
    )
    cells_grad, sums, small = backward(given, [w.shape for w in weights], nt, nf)
    triple_sum, merge_sum, expand_sum, reduce_sum, encode_sum, decode_sum = sums
    index = lax.axis_index("tile") * nf + lax.axis_index("fs")
    piece, wide = first_gain.shape[0], expand_bias.shape[0]
    pieces = lax.dynamic_slice_in_dim(small[:9], index * piece, piece, 1)
    expand_piece = lax.dynamic_slice_in_dim(small[9:13].reshape(-1), index * wide, wide, 0)
    comps, lats = mixture_means.shape
    return (
        kept.decoded[None],
        cells_grad[None],
        pieces[0],
        pieces[1],
        triple_sum,
        merge_sum,
        pieces[2],
        pieces[3],
        expand_sum,
        expand_piece,
        reduce_sum,
        pieces[4],
        pieces[5],
        pieces[6],
        encode_sum,
        pieces[7],
        decode_sum,
        pieces[8],
        small[29, :comps],
        small[13 : 13 + comps, :lats],
        small[13 : 13 + comps, lats : 2 * lats],
    )


def solution(mesh):
    placed = (
        P("fs", "tile", None),
        P("fs", "tile"),
        P("fs", "tile", None),
        P(),
        P("fs", "tile", None),
        P("fs", "tile", None),
        P(("tile", "fs")),
        P(("tile", "fs")),
        P("tile", "fs"),
        P("tile", "fs"),
        P(("tile", "fs")),
        P(("tile", "fs")),
        P("tile", "fs"),
        P(("tile", "fs")),
        P("tile", "fs"),
        P(("tile", "fs")),
        P(("tile", "fs")),
        P(("tile", "fs")),
        P("tile", "fs"),
        P(("tile", "fs")),
        P("tile", "fs"),
        P(("tile", "fs")),
        P(),
        P(),
        P(),
    )
    return jax.shard_map(
        per_device,
        mesh=mesh,
        in_specs=placed,
        out_specs=(
            P("fs", "tile", None),
            P("fs", "tile", None),
            P(("tile", "fs")),
            P(("tile", "fs")),
            P("tile", "fs"),
            P("tile", "fs"),
            P(("tile", "fs")),
            P(("tile", "fs")),
            P("tile", "fs"),
            P(("tile", "fs")),
            P("tile", "fs"),
            P(("tile", "fs")),
            P(("tile", "fs")),
            P(("tile", "fs")),
            P("tile", "fs"),
            P(("tile", "fs")),
            P("tile", "fs"),
            P(("tile", "fs")),
            P(),
            P(),
            P(),
        ),
        check_vma=False,
    )
```

```python
import functools
from types import SimpleNamespace
import jax
import jax.numpy as jnp
from jax import lax
from jax.experimental import pallas as pl
from jax.experimental.pallas import tpu as pltpu

from jax.sharding import PartitionSpec as P

MESH = pl.DeviceIdType.MESH


class Place:
    def __init__(self, nt, nf):
        self.nt, self.nf = nt, nf
        self.nz, self.nx = nt // 2, nf // 2
        tile, fs = lax.axis_index("tile"), lax.axis_index("fs")
        self.tile, self.fs = tile, fs
        self.z, self.y = tile // 2, tile % 2
        self.x, self.c = fs // 2, fs % 2

    def zpeer(self, d):
        return (lax.rem(self.z + d, self.nz) * 2 + self.y, self.fs)

    def ypeer(self):
        return (self.z * 2 + 1 - self.y, self.fs)

    def xat(self, d):
        return lax.rem(self.x + d + self.nx, self.nx)

    def xpeer(self, d):
        return (self.tile, self.xat(d) * 2 + self.c)

    def sibling(self):
        return (self.tile, self.x * 2 + 1 - self.c)

    def peers(self):
        return (
            [self.zpeer(d) for d in range(1, self.nz)]
            + [self.ypeer()]
            + [self.xpeer(d) for d in range(1, self.nx)]
            + [self.sibling()]
        )


def greet(peers):
    barrier = pltpu.get_barrier_semaphore()
    for peer in peers:
        pl.semaphore_signal(barrier, inc=1, device_id=peer, device_id_type=MESH)
    pl.semaphore_wait(barrier, len(peers))


def half_of(rows):
    return max(rows * 5 // 8 // 16 * 16, 16) if rows % 32 == 0 else rows


class Copies:
    def __init__(self, send, recv):
        self.send, self.recv, self.used, self.slots, self.sent = send, recv, 0, {}, []

    def slot(self, key):
        if key not in self.slots:
            self.slots[key] = self.used
            self.used += 1
        return self.slots[key]

    def make(self, key, src, dst, peer):
        at = self.slot(key)
        return pltpu.make_async_remote_copy(
            src_ref=src,
            dst_ref=dst,
            send_sem=self.send.at[at],
            recv_sem=self.recv.at[at],
            device_id=peer,
            device_id_type=MESH,
        )

    def start(self, key, src, dst, peer):
        copy = self.make(key, src, dst, peer)
        copy.start()
        self.sent.append(copy)

    def arrived(self, key, where, peer):
        self.make(key, where, where, peer).wait_recv()

    def drain(self):
        for copy in self.sent:
            copy.wait_send()
        self.sent = []


GATHER_LAG = (0, 2, 4, 6, 7)


class Gather:
    def __init__(self, place, copies, local, key, shard, full, first, rows, left, cols):
        self.p, self.copies, self.local, self.key = place, copies, local, key
        self.shard, self.full, self.first, self.rows = shard, full, first, rows
        self.n, self.left, self.cols = shard.shape[1], left, cols

    def at(self, z, y, x, c, first=0, rows=None):
        rows = self.rows if rows is None else rows
        column = pl.multiple_of((x * 2 + c) * self.n + self.left, 128)
        return self.full.at[z, y, pl.ds(self.first + first, rows), pl.ds(column, self.cols)]

    def one(self):
        p = self.p
        mine = self.shard.at[pl.ds(self.first, self.rows), pl.ds(self.left, self.cols)]
        here = self.at(p.z, p.y, p.x, p.c)
        self.own = pltpu.make_async_copy(mine, here, self.local.at[self.copies.slot((self.key, "own"))])
        self.own.start()
        for d in range(1, p.nz):
            self.copies.start((self.key, "z", d), mine, here, p.zpeer(d))

    def two(self):
        p, key = self.p, self.key
        self.own.wait()
        for d in range(1, p.nz):
            zz = lax.rem(p.z - d + p.nz, p.nz)
            self.copies.arrived((key, "z", d), self.at(zz, p.y, p.x, p.c), p.zpeer(d))
        block = self.at(slice(None), p.y, p.x, p.c)
        self.copies.start((key, "y"), block, block, p.ypeer())
        for d in range(1, p.nx):
            self.copies.start((key, "x", d), block, block, p.xpeer(d))
        self.copies.start((key, "c"), block, block, p.sibling())

    def three(self):
        p, key = self.p, self.key
        half = half_of(self.rows)
        block = self.at(slice(None), 1 - p.y, p.x, p.c)
        self.copies.arrived((key, "y"), block, p.ypeer())
        part = self.at(slice(None), 1 - p.y, p.x, p.c, 0, half)
        for d in range(1, p.nx):
            self.copies.start((key, "yx", d), part, part, p.xpeer(d))
        for d in range(1, p.nx):
            far = p.xat(-d)
            other = self.at(slice(None), p.y, far, p.c)
            self.copies.arrived((key, "x", d), other, p.xpeer(d))
            if half < self.rows:
                part = self.at(slice(None), p.y, far, p.c, half, self.rows - half)
                self.copies.start((key, "xy", d), part, part, p.ypeer())
            self.copies.start((key, "xc", d), other, other, p.sibling())
        self.copies.start((key, "yc"), block, block, p.sibling())

    def four(self):
        p, key = self.p, self.key
        half = half_of(self.rows)
        for d in range(1, p.nx):
            far = p.xat(-d)
            self.copies.arrived((key, "yx", d), self.at(slice(None), 1 - p.y, far, p.c, 0, half), p.xpeer(d))
            if half < self.rows:
                part = self.at(slice(None), 1 - p.y, far, p.c, half, self.rows - half)
                self.copies.arrived((key, "xy", d), part, p.ypeer())
            block = self.at(slice(None), 1 - p.y, far, p.c)
            self.copies.start((key, "dc", d), block, block, p.sibling())

    def five(self):
        p, key = self.p, self.key
        other = 1 - p.c
        self.copies.arrived((key, "c"), self.at(slice(None), p.y, p.x, other), p.sibling())
        self.copies.arrived((key, "yc"), self.at(slice(None), 1 - p.y, p.x, other), p.sibling())
        for d in range(1, p.nx):
            far = p.xat(-d)
            self.copies.arrived((key, "xc", d), self.at(slice(None), p.y, far, other), p.sibling())
            self.copies.arrived((key, "dc", d), self.at(slice(None), 1 - p.y, far, other), p.sibling())


def gather_slots(nt, nf):
    return 1 + (nt // 2 - 1) + 3 + 5 * (nf // 2 - 1)


class Small:
    def __init__(self, place, copies, key, mine, slots):
        self.p, self.copies, self.key, self.mine, self.slots = place, copies, key, mine, slots
        p = place
        self.stages = [
            ([p.zpeer(d) for d in range(1, p.nz)], p.z, p.nz),
            ([p.ypeer()], p.y, 2),
            ([p.xpeer(d) for d in range(1, p.nx)], p.x, p.nx),
            ([p.sibling()], p.c, 2),
        ]

    def base(self, stage):
        return sum(size for _, _, size in self.stages[:stage])

    def send(self, stage):
        peers, at, _ = self.stages[stage]
        base = self.base(stage)
        self.slots[base + at] = self.mine[...]
        for i, peer in enumerate(peers):
            self.copies.start((self.key, stage, i), self.slots.at[base + at], self.slots.at[base + at], peer)

    def receive(self, stage):
        peers, at, size = self.stages[stage]
        base = self.base(stage)
        for i, peer in enumerate(peers):
            came = lax.rem(at - i - 1 + size, size)
            self.copies.arrived((self.key, stage, i), self.slots.at[base + came], peer)
        total = self.slots[base]
        for j in range(1, size):
            total = total + self.slots[base + j]
        self.mine[...] = total


def small_slots(nt, nf):
    return nt // 2 - 1 + 1 + nf // 2 - 1 + 1


def small_places(nt, nf):
    return nt // 2 + 2 + nf // 2 + 2


HEADS = 16
WIN = 128
WARMUP = 1000


EPSILON = 1e-05
LOG_TWO_PI = 1.8378770664093453
FREE_BITS = 0.8
SOFT_WIDTH = 0.1
HIGHEST = lax.Precision.HIGHEST


def row_dot(left, right):
    return lax.dot_general(left, right, (((1,), (1,)), ((), ())), preferred_element_type=jnp.float32)


def col_dot(left, right):
    return lax.dot_general(left, right, (((0,), (0,)), ((), ())), preferred_element_type=jnp.float32)


def plain_dot(left, right):
    return jnp.dot(left, right, preferred_element_type=jnp.float32)


def split_weights(shapes, order):
    cols = min(n for _, n in shapes)
    out = []
    for w in order:
        r, n = shapes[w]
        rows = min(r, 128)
        for i in range(r // rows):
            for j in range(n // cols):
                out.append((w, i * rows, rows, j * cols, cols))
    return out


def high_dot(left, right, left_dim, right_dim):
    return lax.dot_general(
        left,
        right,
        (((left_dim,), (right_dim,)), ((), ())),
        precision=HIGHEST,
        preferred_element_type=jnp.float32,
    )


def mixture_tables(logits, means, logvars):
    precision_tab = jnp.exp(-logvars)
    weighted = means * precision_tab
    top = jnp.max(logits, -1, keepdims=True)
    log_prior = logits - top - jnp.log(jnp.sum(jnp.exp(logits - top), -1, keepdims=True))
    return precision_tab, weighted, means * weighted, log_prior


def forward_kernel(nt, nf, piece, wide_piece, plan, names, *refs):
    r = SimpleNamespace(**dict(zip(names, refs)))
    p = Place(nt, nf)
    w_of, full_of = (r.w0, r.w1, r.w2, r.w3, r.w4, r.w5), (r.full0, r.full1, r.full2, r.full3, r.full4, r.full5)
    sib_of = (r.sib_n1, r.sib_att, r.sib_n2, r.sib_act, r.sib_n3, r.sib_lat)
    rows, features = r.cells.shape
    tiles, mine, vectors = r.tiles, r.mine, r.vectors
    edge = WIN
    lane = lax.broadcasted_iota(jnp.int32, (16, 128), 1)
    row = lax.broadcasted_iota(jnp.int32, (16, 128), 0)
    index = p.tile * nf + p.fs
    narrow_here = lane // piece == lax.rem(index, 128 // piece)
    wide_here = lane // wide_piece == lax.rem(index, 128 // wide_piece)
    here = ((row != 9) & narrow_here) | ((row == 9) & wide_here)
    mine[...] = jnp.where(here, r.packed[...].astype(jnp.float32), 0.0).astype(jnp.bfloat16)
    before = (lax.rem(p.tile + nt - 1, nt), p.fs)
    after = (lax.rem(p.tile + 1, nt), p.fs)
    greet(p.peers() + [before, after])
    copies = Copies(r.send, r.recv)
    local = r.local
    steps = [Gather(p, copies, r.own_sem, "vec", mine, tiles, 0, 16, 0, 128)]
    ends = {}
    for i, (w, f, n, c, m) in enumerate(plan):
        steps.append(Gather(p, copies, r.own_sem, i, w_of[w], full_of[w], f, n, c, m))
        ends[w] = i + 1
    lags = list(zip(("one", "two", "three", "four", "five"), GATHER_LAG))
    clock = [0]

    def pump(count=1):
        for _ in range(count):
            k = clock[0]
            for name, lag in lags[::-1]:
                if 0 <= k - lag < len(steps):
                    getattr(steps[k - lag], name)()
            clock[0] += 1

    def need(step):
        while clock[0] <= step + GATHER_LAG[-1]:
            pump()

    used = [0]

    def share(i, src):
        copies.start(("a", i), src, sib_of[i], p.sibling())

    def put_out(src, dst):
        copy = pltpu.make_async_copy(src, dst, local.at[used[0]])
        used[0] += 1
        copy.start()
        return copy

    pump(2)
    first_row = p.tile * rows
    bias = r.bias
    near = r.near
    flag_row = r.flags[...].astype(jnp.float32)
    count = 3 * edge
    for b in range(rows // edge):
        at = b * edge
        diagonal = lax.broadcasted_iota(jnp.int32, (edge, edge), 0) == lax.broadcasted_iota(jnp.int32, (edge, edge), 1)
        flag = jnp.sum(jnp.where(diagonal, flag_row[:, at : at + edge], 0.0), 1, keepdims=True)
        offset = lax.broadcasted_iota(jnp.int32, (edge, count), 1)
        key = first_row + at - edge + offset
        query = first_row + at + lax.broadcasted_iota(jnp.int32, (edge, count), 0)
        listed = key == query
        listing = near[:, at : at + edge].T
        for n in range(near.shape[0]):
            listed = listed | (listing[:, n : n + 1] == key)
        own_bin = (key >= first_row) & (key < first_row + rows)
        allowed = listed & ((flag > 0.5) | own_bin)
        bias[b] = jnp.where(allowed, 0.0, -1e30)
        pump()
    need(0)
    for at in range(nt * nf // (128 // piece)):
        total = jnp.zeros((16, 128), jnp.float32)
        for j in range(128 // piece):
            t, f = divmod(at * (128 // piece) + j, nf)
            total = total + tiles[t // 2, t % 2, :, f * 128 : (f + 1) * 128].astype(jnp.float32)
        vectors[0:9, at * 128 : (at + 1) * 128] = total[0:9]
    for at in range(nt * nf // (128 // wide_piece)):
        total = jnp.zeros((1, 128), jnp.float32)
        for j in range(128 // wide_piece):
            t, f = divmod(at * (128 // wide_piece) + j, nf)
            total = total + tiles[t // 2, t % 2, :, f * 128 : (f + 1) * 128].astype(jnp.float32)[9:10]
        vectors[9 + at // 8 : 10 + at // 8, at % 8 * 128 : (at % 8 + 1) * 128] = total

    def norm(values, gain_row, out):
        gain, shift = vectors[gain_row : gain_row + 1, :], vectors[gain_row + 1 : gain_row + 2, :]

        def one(i, carry):
            at = pl.ds(pl.multiple_of(i * 32, 32), 32)
            v = values[at, :].astype(jnp.float32)
            center = v - jnp.mean(v, -1, keepdims=True)
            inverse = lax.rsqrt(jnp.mean(center * center, -1, keepdims=True) + EPSILON)
            out[at, :] = (center * inverse * gain + shift).astype(jnp.bfloat16)
            return carry

        lax.fori_loop(0, rows // 32, one, 0)

    def stream(pieces, buffers, sems, body):
        def copy_of(i):
            src = pieces[i]
            dst = buffers.at[i % 2, pl.ds(0, src.shape[0]), pl.ds(0, src.shape[1])]
            return pltpu.make_async_copy(src, dst, sems.at[i % 2])

        copy_of(0).start()
        for i in range(len(pieces)):
            if i + 1 < len(pieces):
                copy_of(i + 1).start()
            copy_of(i).wait()
            body(i, i % 2)

    wide, tall = r.wide, r.tall

    def full_cols(w, first, width):
        full = full_of[w]
        flat = full.reshape(full.shape[0] * full.shape[1] * full.shape[2], full.shape[3])
        return flat.at[:, pl.ds(first, width)]

    def full_rows(w, first, height):
        full = full_of[w]
        flat = full.reshape(full.shape[0] * full.shape[1] * full.shape[2], full.shape[3])
        return flat.at[pl.ds(first, height), :]

    def times(left, w, width, use, tick=False):
        total = full_of[w].shape[3]
        depth = left.shape[1]

        def body(i, b):
            def one(j, carry):
                at = pl.multiple_of(j * 256, 256)
                use(i, at, plain_dot(left[...], wide[b, pl.ds(0, depth), pl.ds(at, 256)]))
                return carry

            lax.fori_loop(0, width // 256, one, 0)
            if tick:
                pump()

        stream([full_cols(w, i * width, width) for i in range(total // width)], wide, r.wide_sem, body)

    normed_one = r.n1_v
    norm(r.cells, 0, normed_one)
    outs = [put_out(normed_one, r.n1)]
    share(0, normed_one)
    need(ends[0])
    queries, keys, values = r.q_v, r.k_v, r.v_v
    here_rows = pl.ds(edge, rows)

    def keep_triple(i, at, value):
        value = value.astype(jnp.bfloat16)
        lanes = pl.ds(at, 256)
        which, first = divmod(i * 512, features)
        lanes = pl.ds(pl.multiple_of(first + at, 256), 256)
        if which == 0:
            queries[:, lanes] = value
        elif which == 1:
            keys[here_rows, lanes] = value
        else:
            values[here_rows, lanes] = value

    times(normed_one, 0, 512, keep_triple)

    def halo(which, up):
        ref = (keys, values)[which]
        if up:
            return copies.make(("halo", which, up), ref.at[pl.ds(rows, edge)], ref.at[pl.ds(0, edge)], after)
        return copies.make(("halo", which, up), ref.at[pl.ds(edge, edge)], ref.at[pl.ds(rows + edge, edge)], before)

    @pl.when(p.tile < nt - 1)
    def _():
        for which in range(2):
            halo(which, True).start()

    @pl.when(p.tile > 0)
    def _():
        for which in range(2):
            halo(which, False).start()

    outs.append(put_out(queries, r.q))
    pump()

    @pl.when(p.tile > 0)
    def _():
        for which in range(2):
            halo(which, True).wait_recv()

    @pl.when(p.tile == 0)
    def _():
        for ref in (keys, values):
            ref[0:edge, :] = jnp.zeros((edge, features), jnp.bfloat16)

    @pl.when(p.tile < nt - 1)
    def _():
        for which in range(2):
            halo(which, False).wait_recv()

    @pl.when(p.tile == nt - 1)
    def _():
        for ref in (keys, values):
            ref[edge + rows :, :] = jnp.zeros((edge, features), jnp.bfloat16)

    outs.append(put_out(keys, r.kext))
    outs.append(put_out(values, r.vext))

    pairs = features // 128
    scale = (features // HEADS) ** (-0.5)
    attended = r.att_v

    def probs_out(i, b):
        return pltpu.make_async_copy(r.p_v.at[b], r.probs.at[pl.ds(2 * i, 2)], r.pair_sem.at[b])

    def pair(i, carry):
        b = lax.rem(i, 2)

        @pl.when(i >= 2)
        def _():
            probs_out(i - 2, b).wait()

        lanes = pl.ds(pl.multiple_of(i * 128, 128), 128)
        zero = jnp.zeros((), jnp.bfloat16)
        for block in range(rows // edge):
            own_rows, keys_at = pl.ds(block * edge, edge), pl.ds(block * edge, count)
            head = lax.broadcasted_iota(jnp.int32, (edge, 128), 1) // 64
            key_head = lax.broadcasted_iota(jnp.int32, (count, 128), 1) // 64
            total = jnp.zeros((edge, 128), jnp.float32)
            for e in range(2):
                query = jnp.where(head == e, queries[own_rows, lanes], zero)
                score = row_dot(query, keys[keys_at, lanes]) * scale + bias[block]
                top = jnp.max(score, -1, keepdims=True)
                power = jnp.exp(score - top)
                prob = (power / jnp.sum(power, -1, keepdims=True)).astype(jnp.bfloat16)
                r.p_v[b, e, block] = prob
                total = total + plain_dot(prob, jnp.where(key_head == e, values[keys_at, lanes], zero))
            attended[own_rows, lanes] = total.astype(jnp.bfloat16)
        probs_out(i, b).start()
        return carry

    for i in range(pairs // 2):
        lax.fori_loop(2 * i, 2 * i + 2, pair, 0)
        pump()
    for i in range(pairs - 2, pairs):
        probs_out(i, i % 2).wait()
    outs.append(put_out(attended, r.att))
    share(1, attended)
    need(ends[1])
    hidden = r.hid_v

    def keep_hidden(i, at, value):
        lanes = pl.ds(pl.multiple_of(i * 512 + at, 256), 256)
        hidden[:, lanes] = r.cells[:, lanes].astype(jnp.float32) + value

    times(attended, 1, 512, keep_hidden)
    outs.append(put_out(hidden, r.hid))
    normed_two = r.n2_v
    norm(hidden, 2, normed_two)
    outs.append(put_out(normed_two, r.n2))
    share(2, normed_two)
    need(ends[2])

    root = 0.7978845608028654
    activated, pre_v = r.act_v, r.pre_v

    def pre_out(i):
        return pltpu.make_async_copy(pre_v.at[i % 2], r.pre.at[:, pl.ds(i * 512, 512)], r.pre_sem.at[i % 2])

    def keep_pre(i, at, value):
        vec_row, first = divmod(i * 512, features)
        lanes = pl.ds(pl.multiple_of(first + at, 256), 256)
        u = value + vectors[9 + vec_row : 10 + vec_row, lanes]
        pre_v[i % 2, :, pl.ds(at, 256)] = u
        gate = 0.5 * (1.0 + jnp.tanh(root * (u + 0.044715 * u * u * u)))
        activated[:, pl.ds(pl.multiple_of(i * 512 + at, 256), 256)] = (u * gate).astype(jnp.bfloat16)

    def up_body(i, b):
        if i >= 2:
            pre_out(i - 2).wait()

        def one(j, carry):
            at = pl.multiple_of(j * 256, 256)
            keep_pre(i, at, plain_dot(normed_two[...], wide[b, :, pl.ds(at, 256)]))
            return carry

        lax.fori_loop(0, 2, one, 0)
        pre_out(i).start()
        if i % 4 == 3:
            pump()

    depth = activated.shape[1]
    up_count = depth // 512
    stream([full_cols(2, i * 512, 512) for i in range(up_count)], wide, r.wide_sem, up_body)
    for i in range(up_count - 2, up_count):
        pre_out(i).wait()
    outs.append(put_out(activated, r.act))
    share(3, activated)
    need(ends[3])
    second = r.two_v

    def down_body(i, b):
        def one(j, carry):
            lanes = pl.ds(pl.multiple_of(j * 256, 256), 256)
            part = plain_dot(activated[:, i * 512 : (i + 1) * 512], tall[b, :, lanes])
            if i == 0:
                second[:, lanes] = hidden[:, lanes] + vectors[4:5, lanes] + part
            else:
                second[:, lanes] += part
            return carry

        lax.fori_loop(0, features // 256, one, 0)

    stream([full_rows(3, i * 512, 512) for i in range(up_count)], tall, r.tall_sem, down_body)
    outs.append(put_out(second, r.two))
    normed_three = r.n3_v
    norm(second, 5, normed_three)
    outs.append(put_out(normed_three, r.n3))
    share(4, normed_three)
    need(ends[4])
    encoded = r.enc_v

    def keep_encoded(i, at, value):
        lanes = pl.ds(pl.multiple_of(i * 512 + at, 256), 256)
        encoded[:, lanes] = value + vectors[7:8, lanes]

    times(normed_three, 4, 512, keep_encoded)
    outs.append(put_out(encoded, r.enc))
    latent, latent32 = r.lat_v, r.z_v
    half = features // 2
    tables = mixture_tables(r.logits[...], r.means[...], r.logvars[...])
    precision_tab, weighted, squared, log_prior = tables
    logvars = r.logvars[...]
    ones = jnp.ones((8, half), jnp.float32)
    constant = log_prior - 0.5 * (
        LOG_TWO_PI * half + high_dot(ones, logvars, 1, 1)[0:1] + high_dot(ones, squared, 1, 1)[0:1]
    )
    r.tab[...] = jnp.zeros_like(r.tab)
    r.klp[...] = jnp.zeros_like(r.klp)

    def latent_rows(i, carry):
        at = pl.ds(pl.multiple_of(i * 128, 128), 128)
        log_var, noise = encoded[at, half:], r.noise[at, :]
        z = encoded[at, 0:half] + jnp.exp(0.5 * log_var) * noise
        latent32[at, :] = z
        latent[at, :] = z.astype(jnp.bfloat16)
        square = z * z
        ell = constant - 0.5 * (high_dot(square, precision_tab, 1, 1) - 2.0 * high_dot(z, weighted, 1, 1))
        ell = ell - jnp.max(ell, -1, keepdims=True)
        log_resp = ell - jnp.log(jnp.sum(jnp.exp(ell), -1, keepdims=True))
        r.lr[at, :] = log_resp
        resp = jnp.exp(log_resp)
        r.tab[0] += high_dot(resp, z, 0, 0)
        r.tab[1] += high_dot(resp, square, 0, 0)
        r.tab[2] += high_dot(resp, jnp.ones_like(z), 0, 0)
        r.klp[0:1, :] += -0.5 * jnp.sum(LOG_TWO_PI + log_var + noise * noise, 0, keepdims=True)
        return carry

    lax.fori_loop(0, rows // 128, latent_rows, 0)
    cross = r.tab[2] * (LOG_TWO_PI + logvars + squared) + precision_tab * r.tab[1] - 2.0 * weighted * r.tab[0]
    r.klp[0:1, :] += 0.5 * jnp.sum(cross, 0, keepdims=True)
    outs.append(put_out(latent, r.lat))
    outs.append(put_out(latent32, r.z))
    share(5, latent)
    need(ends[5])
    decoded = r.dec_v

    def keep_decoded(i, at, value):
        lanes = pl.ds(pl.multiple_of(i * 512 + at, 256), 256)
        decoded[:, lanes] = (second[:, lanes] + value + vectors[8:9, lanes]).astype(jnp.bfloat16)

    times(latent, 5, 512, keep_decoded)
    outs.append(put_out(decoded, r.decoded))
    for i in range(6):
        copies.arrived(("a", i), sib_of[i], p.sibling())
    for copy in outs:
        copy.wait()

    @pl.when(p.tile < nt - 1)
    def _():
        for which in range(2):
            halo(which, True).wait_send()

    @pl.when(p.tile > 0)
    def _():
        for which in range(2):
            halo(which, False).wait_send()

    copies.drain()


def forward(cells, flags, near, noise, shards, small_vectors, mixture, nt, nf):
    piece, wide_piece = small_vectors[0].shape[0], small_vectors[9].shape[0]
    packed = jnp.stack([jnp.tile(v, 128 // v.shape[0]) for v in small_vectors])
    packed = jnp.pad(packed, ((0, 6), (0, 0)))
    shapes = [s.shape for s in shards]
    plan = split_weights(shapes, range(6))
    rows, features = cells.shape
    lats = noise.shape[1]
    depth = shapes[2][1] * nf
    keys = rows + 2 * WIN
    blocks = rows // WIN
    bf, f32 = jnp.bfloat16, jnp.float32
    nz = nt // 2
    slots = gather_slots(nt, nf) * (len(plan) + 1) + 4 + 6
    comps = mixture[1].shape[0]
    hbm, vmem = pl.BlockSpec(memory_space=pltpu.HBM), pl.BlockSpec(memory_space=pltpu.VMEM)
    fulls = [((nz, 2, s, n * nf), bf, hbm) for s, n in shapes]
    outs = dict(
        full0=fulls[0],
        full1=fulls[1],
        full2=fulls[2],
        full3=fulls[3],
        full4=fulls[4],
        full5=fulls[5],
        sib_n1=((rows, features), bf, hbm),
        sib_att=((rows, features), bf, hbm),
        sib_n2=((rows, features), bf, hbm),
        sib_act=((rows, depth), bf, hbm),
        sib_n3=((rows, features), bf, hbm),
        sib_lat=((rows, lats), bf, hbm),
        z=((rows, lats), f32, hbm),
        lr=((rows, comps), f32, vmem),
        tab=((3, comps, lats), f32, vmem),
        klp=((8, lats), f32, vmem),
        n1=((rows, features), bf, hbm),
        q=((rows, features), bf, hbm),
        kext=((keys, features), bf, hbm),
        vext=((keys, features), bf, hbm),
        probs=((HEADS, blocks, WIN, 3 * WIN), bf, hbm),
        att=((rows, features), bf, hbm),
        hid=((rows, features), f32, hbm),
        n2=((rows, features), bf, hbm),
        pre=((rows, depth), f32, hbm),
        act=((rows, depth), bf, hbm),
        two=((rows, features), f32, hbm),
        n3=((rows, features), bf, hbm),
        enc=((rows, features), f32, hbm),
        lat=((rows, lats), bf, hbm),
        decoded=((rows, features), bf, hbm),
        vectors=((16, features), f32, vmem),
    )
    dma = pltpu.SemaphoreType.DMA
    scratch = dict(
        tiles=pltpu.VMEM((nz, 2, 16, nf * 128), bf),
        mine=pltpu.VMEM((16, 128), bf),
        bias=pltpu.VMEM((blocks, WIN, 3 * WIN), f32),
        n1_v=pltpu.VMEM((rows, features), bf),
        q_v=pltpu.VMEM((rows, features), bf),
        k_v=pltpu.VMEM((keys, features), bf),
        v_v=pltpu.VMEM((keys, features), bf),
        p_v=pltpu.VMEM((2, 2, blocks, WIN, 3 * WIN), bf),
        pair_sem=dma((2,)),
        att_v=pltpu.VMEM((rows, features), bf),
        hid_v=pltpu.VMEM((rows, features), f32),
        n2_v=pltpu.VMEM((rows, features), bf),
        pre_v=pltpu.VMEM((2, rows, 512), f32),
        pre_sem=dma((2,)),
        act_v=pltpu.VMEM((rows, depth), bf),
        two_v=pltpu.VMEM((rows, features), f32),
        n3_v=pltpu.VMEM((rows, features), bf),
        enc_v=pltpu.VMEM((rows, features), f32),
        lat_v=pltpu.VMEM((rows, lats), bf),
        dec_v=pltpu.VMEM((rows, features), bf),
        wide=pltpu.VMEM((2, features, 512), bf),
        wide_sem=dma((2,)),
        tall=pltpu.VMEM((2, 512, features), bf),
        tall_sem=dma((2,)),
        send=dma((slots,)),
        recv=dma((slots,)),
        own_sem=dma((slots,)),
        local=dma((20,)),
        z_v=pltpu.VMEM((rows, lats), f32),
    )
    given = dict(
        w0=shards[0],
        w1=shards[1],
        w2=shards[2],
        w3=shards[3],
        w4=shards[4],
        w5=shards[5],
        noise=noise,
        packed=packed,
        cells=cells,
        flags=flags,
        near=near,
        logits=mixture[0][None],
        means=mixture[1],
        logvars=mixture[2],
    )
    names = [*given, *outs, *scratch]
    result = pl.pallas_call(
        functools.partial(forward_kernel, nt, nf, piece, wide_piece, plan, names),
        out_shape=[jax.ShapeDtypeStruct(o[0], o[1]) for o in outs.values()],
        in_specs=[hbm] * 6 + [vmem] * 8,
        out_specs=[o[2] for o in outs.values()],
        scratch_shapes=list(scratch.values()),
        compiler_params=pltpu.CompilerParams(collective_id=0, has_side_effects=True, vmem_limit_bytes=56 << 20),
        name="forward",
    )(*given.values())
    return SimpleNamespace(**dict(zip(outs, result)))


class Chunk:
    def __init__(self, number, weight, first_row, rows, first_col, cols):
        self.number, self.weight = number, weight
        self.first_row, self.rows, self.first_col, self.cols = first_row, rows, first_col, cols
        self.done = 0


def chunk_plan(shapes):
    return [Chunk(k, *item) for k, item in enumerate(split_weights(shapes, (5, 4, 3, 2, 1, 0)))]


LAG = 4
FILL = (1, 1, 1, 1)


class Ring:
    STEPS = 5

    def __init__(self, place, copies, plan, slots, own, diag, from_y, from_x, from_z, outs, free):
        self.p, self.copies, self.plan, self.slots, self.free = place, copies, plan, slots, free
        self.own, self.diag, self.from_y, self.from_x, self.from_z = own, diag, from_y, from_x, from_z
        self.outs, self.open, self.now = outs, [], 0

    def sides(self):
        p = self.p
        out = [(p.zpeer(d), d - 1, p.nz - d - 1) for d in range(1, p.nz)]
        out.append((p.ypeer(), p.nz - 1, p.nz - 1))
        return out + [(p.xpeer(d), p.nz + d - 1, p.nz + p.nx - d - 1) for d in range(1, p.nx)]

    def make_room(self, k):
        if k >= self.slots:
            old = self.plan[k - self.slots]
            while old.done < self.STEPS - 1:
                self.step(old)
            if old in self.open:
                self.open.remove(old)
            for copy in old.sent:
                copy.wait_send()

    def add(self, k):
        chunk = self.plan[k]
        if k >= self.slots:
            for _, here, _ in self.sides():
                pl.semaphore_wait(self.free.at[here], 1)
        chunk.sent = []
        self.open.append(chunk)
        self.step(chunk)

    def tick(self, lag=LAG):
        self.now += 1
        for chunk in list(self.open):
            if chunk.done < self.STEPS - 1 and self.now - chunk.at >= lag:
                self.step(chunk)
            if chunk.done == self.STEPS - 1:
                self.open.remove(chunk)

    def finish(self):
        while self.open:
            self.tick(1)
        for chunk in self.plan[-self.slots :]:
            for copy in chunk.sent:
                copy.wait_send()

    def step(self, chunk):
        (self.one, self.two, self.three, self.four)[chunk.done](chunk)
        chunk.done += 1
        chunk.at = self.now

    def start(self, chunk, key, src, dst, peer):
        copy = self.copies.make(("ring", chunk.number) + key, src, dst, peer)
        copy.start()
        chunk.sent.append(copy)

    def arrived(self, chunk, key, where, peer):
        self.copies.arrived(("ring", chunk.number) + key, where, peer)

    def parts(self, chunk):
        half = half_of(chunk.rows)
        high = pl.ds(half, chunk.rows - half) if half < chunk.rows else None
        return chunk.number % self.slots, pl.ds(0, chunk.rows), pl.ds(0, half), high

    def one(self, chunk):
        p, (s, _, low, high) = self.p, self.parts(chunk)
        for d in range(1, p.nx):
            far = p.xat(d)
            src, dst = self.own.at[s, far, :, 1 - p.y, low], self.diag.at[s, d - 1, :, low]
            self.start(chunk, ("yx", d), src, dst, p.xpeer(d))
            if high is not None:
                src, dst = self.own.at[s, far, :, 1 - p.y, high], self.diag.at[s, d - 1, :, high]
                self.start(chunk, ("xy", d), src, dst, p.ypeer())

    def two(self, chunk):
        p, (s, rows, low, high) = self.p, self.parts(chunk)
        for d in range(1, p.nx):
            self.arrived(chunk, ("yx", d), self.diag.at[s, d - 1, :, low], p.xpeer(d))
            if high is not None:
                self.arrived(chunk, ("xy", d), self.diag.at[s, d - 1, :, high], p.ypeer())

        def add(q, carry):
            for d in range(1, p.nx):
                got = self.diag[s, d - 1, q, low, :].astype(jnp.float32)
                had = self.own[s, p.x, q, 1 - p.y, low, :].astype(jnp.float32)
                self.own[s, p.x, q, 1 - p.y, low, :] = (had + got).astype(jnp.bfloat16)
                if high is not None:
                    far = p.xat(d)
                    got = self.diag[s, d - 1, q, high, :].astype(jnp.float32)
                    had = self.own[s, far, q, p.y, high, :].astype(jnp.float32)
                    self.own[s, far, q, p.y, high, :] = (had + got).astype(jnp.bfloat16)
            return carry

        lax.fori_loop(0, p.nz, add, 0)
        src = self.own.at[s, p.x, :, 1 - p.y, rows]
        self.start(chunk, ("y",), src, self.from_y.at[s, :, rows], p.ypeer())
        for d in range(1, p.nx):
            src = self.own.at[s, p.xat(d), :, p.y, rows]
            self.start(chunk, ("x", d), src, self.from_x.at[s, d - 1, :, rows], p.xpeer(d))

    def three(self, chunk):
        p, (s, rows, _, _) = self.p, self.parts(chunk)
        self.arrived(chunk, ("y",), self.from_y.at[s, :, rows], p.ypeer())
        for d in range(1, p.nx):
            self.arrived(chunk, ("x", d), self.from_x.at[s, d - 1, :, rows], p.xpeer(d))

        def add(q, carry):
            total = self.own[s, p.x, q, p.y, rows, :].astype(jnp.float32)
            total = total + self.from_y[s, q, rows, :].astype(jnp.float32)
            for d in range(1, p.nx):
                total = total + self.from_x[s, d - 1, q, rows, :].astype(jnp.float32)
            self.own[s, p.x, q, p.y, rows, :] = total.astype(jnp.bfloat16)
            return carry

        lax.fori_loop(0, p.nz, add, 0)
        for d in range(1, p.nz):
            to = lax.rem(p.z + d, p.nz)
            src = self.own.at[s, p.x, to, p.y, rows]
            self.start(chunk, ("z", d), src, self.from_z.at[s, d - 1, rows], p.zpeer(d))

    def four(self, chunk):
        p, (s, rows, _, _) = self.p, self.parts(chunk)
        total = self.own[s, p.x, p.z, p.y, rows, :].astype(jnp.float32)
        for d in range(1, p.nz):
            self.arrived(chunk, ("z", d), self.from_z.at[s, d - 1, rows], p.zpeer(d))
            total = total + self.from_z[s, d - 1, rows, :].astype(jnp.float32)
        out = self.outs[chunk.weight]
        out[pl.ds(chunk.first_row, chunk.rows), pl.ds(chunk.first_col, chunk.cols)] = total
        if chunk.number + self.slots < len(self.plan):
            for peer, _, there in self.sides():
                pl.semaphore_signal(self.free.at[there], inc=1, device_id=peer, device_id_type=MESH)


def ring_slots(nt, nf):
    return 3 * (nf // 2 - 1) + 1 + nt // 2 - 1


WEIGHTS = 6


def backward_kernel(nt, nf, plan, slots, names, *refs):
    r = SimpleNamespace(**dict(zip(names, refs)))
    out_of = (r.out0, r.out1, r.out2, r.out3, r.out4, r.out5)
    p = Place(nt, nf)
    held, vectors = r.held, r.vectors
    rows, features = r.gtwo_v.shape
    before = (lax.rem(p.tile + nt - 1, nt), p.fs)
    after = (lax.rem(p.tile + 1, nt), p.fs)
    greet(p.peers() + [before, after])
    copies = Copies(r.send, r.recv)
    local = r.local
    for chunk in plan:
        chunk.done = 0
    ring = Ring(
        p, copies, plan, slots, r.own, r.diag, r.from_y, r.from_x, r.from_z,
        out_of, r.free,
    )
    small = Small(p, copies, "small", r.rest, r.places)
    late = Small(p, copies, "late", r.last, r.late_places)
    small_work = [functools.partial(step, stage) for stage in range(4) for step in (small.send, small.receive)]
    used = [0]

    def fetch(src, dst):
        copy = pltpu.make_async_copy(src, dst, local.at[used[0]])
        used[0] += 1
        copy.start()
        return copy

    inputs = (r.n1, r.att, r.n2, r.act, r.n3, r.lat)
    siblings = (r.sib_n1, r.sib_att, r.sib_n2, r.sib_act, r.sib_n3, r.sib_lat)
    grads = [r.g_tri, r.g_mer, r.g_exp, r.g_red, r.g_enc, r.g_dec]
    others = [r.s_tri, r.s_mer, r.s_exp, r.s_red, r.s_enc, r.s_dec]

    def spread_in(src, dst):
        n = dst.shape[2]
        return [fetch(src.at[:, f * n : (f + 1) * n], dst.at[f]) for f in range(nf)]

    def ship(w):
        for x in range(p.nx):
            copies.start(("g", w, x), grads[w].at[x * 2 + 1 - p.c], others[w].at[x], p.sibling())

    average = Small(p, copies, "kl", r.kl, r.kl_places)
    r.kl[...] = r.klp[...]
    average.send(0)
    loads = spread_in(r.gout, r.g_dec)
    load_z = fetch(r.z, r.pre_v.at[0])
    load_noise = fetch(r.noise, r.pre_v.at[1])
    half = features // 2
    acc = r.acc
    load_var = fetch(r.enc.at[:, pl.ds(half, half)], acc.at[:, pl.ds(half, half)])
    load_two = fetch(r.two, r.hid_v)
    load_cells = fetch(r.cells, r.cells_v)
    for copy in loads:
        copy.wait()
    ship(5)

    keys = []
    for chunk in plan:
        if (chunk.weight, chunk.first_row) not in keys:
            keys.append((chunk.weight, chunk.first_row))

    def load_left(j):
        w, first = keys[j]
        chunk_rows = min(out_of[w].shape[0], 128)
        shard = out_of[w].shape[0]
        for side, src in enumerate((inputs[w], siblings[w])):
            if chunk_rows == shard:
                width = nt * shard
                copy = pltpu.make_async_copy(
                    src, r.left.at[j % 2, side, :, pl.ds(0, width)], r.left_sem.at[j % 2, side]
                )
                copy.start()
            else:
                for t in range(nt):
                    copy = pltpu.make_async_copy(
                        src.at[:, pl.ds(t * shard + first, chunk_rows)],
                        r.left.at[j % 2, side, :, pl.ds(t * chunk_rows, chunk_rows)],
                        r.left_sem.at[j % 2, side],
                    )
                    copy.start()

    state = {"loaded": 0, "ready": -1, "got": set()}

    def sums(k):
        chunk = plan[k]
        w, cols = chunk.weight, chunk.cols
        j = keys.index((w, chunk.first_row))
        while state["loaded"] <= min(j + 1, len(keys) - 1):
            load_left(state["loaded"])
            state["loaded"] += 1
        width = nt * chunk.rows
        if state["ready"] < j:
            for side in range(2):
                where = r.left.at[j % 2, side, :, pl.ds(0, width)]
                pltpu.make_async_copy(where, where, r.left_sem.at[j % 2, side]).wait()
            state["ready"] = j
        if w not in state["got"]:
            state["got"].add(w)
            for x in range(p.nx):
                copies.arrived(("g", w, x), others[w].at[x], p.sibling())
        ring.make_room(k)
        slot = k % slots
        step_rows = 256
        zs = step_rows // (2 * chunk.rows)
        piece = pl.ds(chunk.first_col, cols)

        def one(g, carry):
            lanes = pl.ds(pl.multiple_of(g * step_rows, step_rows), step_rows)
            mine = r.left[j % 2, 0, :, lanes].T
            theirs = r.left[j % 2, 1, :, lanes].T
            for x in range(p.nx):
                total = plain_dot(mine, grads[w][x * 2 + p.c, :, piece])
                total = total + plain_dot(theirs, others[w][x, :, piece])
                total = total.astype(jnp.bfloat16).reshape(zs, 2, chunk.rows, cols)
                r.own[slot, x, pl.ds(g * zs, zs), :, pl.ds(0, chunk.rows), :] = total
            return carry

        lax.fori_loop(0, width // step_rows, one, 0)
        ring.add(k)

    def stream(pieces, buffers, sems, body):
        def copy_of(i):
            src = pieces[i]
            dst = buffers.at[i % 2, pl.ds(0, src.shape[0]), pl.ds(0, src.shape[1])]
            return pltpu.make_async_copy(src, dst, sems.at[i % 2])

        copy_of(0).start()
        for i in range(len(pieces)):
            if i + 1 < len(pieces):
                copy_of(i + 1).start()
            copy_of(i).wait()
            body(i, i % 2)

    wide, tall = r.wide, r.tall

    def times_rows(grad, full, use):
        n = grad.shape[2]
        depth = full.shape[0]
        pieces = [full.at[pl.ds(i * 512, 512), :] for i in range(depth // 512)]

        def body(i, b):
            def one(j, carry):
                at = pl.ds(pl.multiple_of(j * 256, 256), 256)
                total = row_dot(grad[0], tall[b, at, 0:n])
                for f in range(1, nf):
                    total = total + row_dot(grad[f], tall[b, at, f * n : (f + 1) * n])
                use(i * 512 + j * 256, total)
                return carry

            lax.fori_loop(0, 2, one, 0)

        stream(pieces, tall, r.tall_sem, body)

    def times_cols(grad, full, acc, width):
        n = grad.shape[2]
        pieces = [full.at[:, pl.ds(i * width, width)] for i in range(nf * n // width)]

        def body(i, b):
            f, off = divmod(i * width, n)

            def one(j, carry):
                at = pl.ds(pl.multiple_of(j * 256, 256), 256)
                part = row_dot(grad[f, :, off : off + width], wide[b, at, 0:width])
                if i == 0:
                    acc[:, at] = part
                else:
                    acc[:, at] += part
                return carry

            lax.fori_loop(0, features // 256, one, 0)

        stream(pieces, wide, r.wide_sem, body)

    def norm_back(values, grad, gain_row, place_row, use):
        gain = vectors[gain_row : gain_row + 1, :]
        held[place_row : place_row + 2, :] = jnp.zeros((2, features), jnp.float32)

        def one(i, carry):
            at = pl.ds(pl.multiple_of(i * 32, 32), 32)
            v = values[at, :].astype(jnp.float32)
            center = v - jnp.mean(v, -1, keepdims=True)
            inverse = lax.rsqrt(jnp.mean(center * center, -1, keepdims=True) + EPSILON)
            unit = center * inverse
            e = grad[at, :]
            scaled = e * gain
            back = inverse * (
                scaled - jnp.mean(scaled, -1, keepdims=True) - unit * jnp.mean(scaled * unit, -1, keepdims=True)
            )
            held[place_row : place_row + 1, :] += jnp.sum(e * unit, 0, keepdims=True)
            held[place_row + 1 : place_row + 2, :] += jnp.sum(e, 0, keepdims=True)
            use(at, back)
            return carry

        lax.fori_loop(0, rows // 32, one, 0)

    def put(grad, at, value):
        n = grad.shape[2]
        for f in range(nf):
            grad[f, at, :] = value[:, f * n : (f + 1) * n].astype(jnp.bfloat16)

    held[...] = jnp.zeros_like(held)
    chunks_of = [[c.number for c in plan if c.weight == w] for w in range(WEIGHTS)]

    def column_sums(row, grad):
        n = grad.shape[2]
        for f in range(nf):
            held[row : row + 1, f * n : (f + 1) * n] = jnp.sum(grad[f].astype(jnp.float32), 0, keepdims=True)

    average.receive(0)
    average.send(1)

    def keep_latent(first, value):
        acc[:, pl.ds(pl.multiple_of(first, 256), 256)] = value

    times_rows(r.g_dec, r.w_dec, keep_latent)
    average.receive(1)
    average.send(2)
    for k in chunks_of[5]:
        sums(k)
    average.receive(2)
    average.send(3)
    column_sums(8, r.g_dec)

    precision_tab, weighted, squared, log_prior = mixture_tables(r.logits[...], r.means[...], r.logvars[...])
    means, logvars = r.means[...], r.logvars[...]
    comps = means.shape[0]
    weight = r.kl_step[0].astype(jnp.float32) / WARMUP
    average.receive(3)
    total_cells = rows * nt * nf
    slope = weight / (1.0 + jnp.exp((FREE_BITS - r.kl[0:1, :] / total_cells) / SOFT_WIDTH))
    sloped, sloped_weighted = slope * precision_tab, slope * weighted
    ones = jnp.ones((8, half), jnp.float32)
    constant = high_dot(ones, slope * (LOG_TWO_PI + logvars + squared), 1, 1)[0:1]
    r.mix[...] = jnp.zeros_like(r.mix)
    load_z.wait()
    load_noise.wait()
    load_var.wait()

    def divergence(i, carry):
        at = pl.ds(pl.multiple_of(i * 128, 128), 128)
        z, noise = r.pre_v[0, at, :], r.pre_v[1, at, :]
        std = jnp.exp(0.5 * acc[at, half:])
        square = z * z
        log_resp = r.lr[at, :]
        resp = jnp.exp(log_resp)
        value = -0.5 * (constant + high_dot(square, sloped, 1, 1) - 2.0 * high_dot(z, sloped_weighted, 1, 1))
        value = weight * (log_resp + 1.0 - log_prior) - value
        e = resp * (value - jnp.sum(resp * value, -1, keepdims=True))
        on_square = high_dot(e, precision_tab, 1, 0) - slope * high_dot(resp, precision_tab, 1, 0)
        on_z = high_dot(e, weighted, 1, 0) - slope * high_dot(resp, weighted, 1, 0)
        grad_latent = acc[at, 0:half] + on_z - z * on_square
        grad_var = grad_latent * 0.5 * std * noise - 0.5 * slope
        n = r.g_enc.shape[2]
        for f in range(nf):
            part = grad_latent if (f + 1) * n <= half else grad_var
            first = f * n % half
            r.g_enc[f, at, :] = part[:, first : first + n].astype(jnp.bfloat16)
        r.mix[0] += high_dot(e, z, 0, 0)
        r.mix[1] += high_dot(e, square, 0, 0)
        r.mix[2] += high_dot(e, jnp.ones_like(z), 0, 0)
        held[29:30, 0:comps] += jnp.sum(e - weight * resp, 0, keepdims=True)
        return carry

    lax.fori_loop(0, rows // 128, divergence, 0)
    ship(4)
    column_sums(7, r.g_enc)

    def keep_third(first, value):
        acc[:, pl.ds(pl.multiple_of(first, 256), 256)] = value

    times_rows(r.g_enc, r.w_enc, keep_third)
    for k in chunks_of[4]:
        sums(k)
    gtwo = r.gtwo_v
    load_two.wait()

    def to_two(at, back):
        n = r.g_dec.shape[2]
        for f in range(nf):
            lanes = slice(f * n, (f + 1) * n)
            value = r.g_dec[f, at, :].astype(jnp.float32) + back[:, lanes]
            low = value.astype(jnp.bfloat16)
            gtwo[at, lanes] = value
            r.g_red[f, at, :] = low
            held[4:5, lanes] += jnp.sum(low.astype(jnp.float32), 0, keepdims=True)

    norm_back(r.hid_v, acc, 5, 5, to_two)
    ship(3)
    load_hid = fetch(r.hid, r.hid_v)
    zero_order = r.mix[2] - slope * r.tab[2]
    first_order = r.mix[0] - slope * r.tab[0]
    second_order = r.mix[1] - slope * r.tab[1]
    held[13 : 13 + comps, 0:half] = precision_tab * (first_order - means * zero_order)
    held[13 : 13 + comps, half:] = -0.5 * (
        zero_order - precision_tab * (second_order - 2.0 * means * first_order + means * means * zero_order)
    )
    on_prior = held[29:30, 0:comps]
    held[29:30, 0:comps] = on_prior - jnp.exp(log_prior) * jnp.sum(on_prior, -1, keepdims=True)

    pre = r.pre
    pre_v, pre_sem = r.pre_v, r.pre_sem
    tiles = pre.shape[1] // 512

    def pre_copy(i):
        return pltpu.make_async_copy(pre.at[:, pl.ds(i * 512, 512)], pre_v.at[i % 2], pre_sem.at[i % 2])

    pre_copy(0).start()
    n_exp = r.g_exp.shape[2]
    root = 0.7978845608028654

    depth = r.w_red.shape[0]
    pieces = [r.w_red.at[pl.ds(i * 512, 512), :] for i in range(depth // 512)]
    n_red = r.g_red.shape[2]

    def ff_body(i, b):
        if i + 1 < tiles:
            pre_copy(i + 1).start()
        pre_copy(i).wait()
        f, off = divmod(i * 512, n_exp)

        def one(j, carry):
            at = pl.ds(pl.multiple_of(j * 256, 256), 256)
            total = row_dot(r.g_red[0], tall[b, at, 0:n_red])
            for q in range(1, nf):
                total = total + row_dot(r.g_red[q], tall[b, at, q * n_red : (q + 1) * n_red])
            u = pre_v[i % 2, :, at]
            square = u * u
            t = jnp.tanh(root * u * (1.0 + 0.044715 * square))
            slope = 0.5 * (1.0 + t) + (0.5 * root) * u * (1.0 - t * t) * (1.0 + 0.134145 * square)
            value = (total * slope).astype(jnp.bfloat16)
            here = pl.ds(pl.multiple_of(off + j * 256, 256), 256)
            r.g_exp[f, :, here] = value
            row, lane = divmod(i * 512, features)
            there = pl.ds(pl.multiple_of(lane + j * 256, 256), 256)
            held[9 + row : 10 + row, there] = jnp.sum(value.astype(jnp.float32), 0, keepdims=True)
            return carry

        lax.fori_loop(0, 2, one, 0)
        if i == tiles // 2:
            ring.tick()

    stream(pieces, tall, r.tall_sem, ff_body)
    ship(2)
    ring.tick()
    for k in chunks_of[3]:
        sums(k)
        ring.tick()
    times_cols(r.g_exp, r.w_exp, acc, 512)
    ring.tick()
    load_hid.wait()

    def to_one(at, back):
        value = gtwo[at, :] + back
        gtwo[at, :] = value
        put(r.g_mer, at, value)

    norm_back(r.hid_v, acc, 2, 2, to_one)
    ring.tick()
    ship(1)
    r.rest[...] = held[...]
    small_work.pop(0)()
    grad_att = r.gatt

    def keep_att(first, value):
        grad_att[:, pl.ds(pl.multiple_of(first, 256), 256)] = value.astype(jnp.bfloat16)

    times_rows(r.g_mer, r.w_mer, keep_att)
    ring.tick()
    filler = chunks_of[2] + chunks_of[1]

    pairs = features // 128
    win = r.kext.shape[0] - rows
    edge = win // 2
    count = 3 * edge
    scale = (features // HEADS) ** (-0.5)

    def fetch_pair(i, b):
        lanes = pl.ds(pl.multiple_of(i * 128, 128), 128)
        return [
            pltpu.make_async_copy(r.probs.at[pl.ds(2 * i, 2)], r.p_v.at[b], r.pair_sem.at[b, 0]),
            pltpu.make_async_copy(r.q.at[:, lanes], r.q_v.at[b], r.pair_sem.at[b, 1]),
            pltpu.make_async_copy(r.kext.at[:, lanes], r.k_v.at[b], r.pair_sem.at[b, 2]),
            pltpu.make_async_copy(r.vext.at[:, lanes], r.v_v.at[b], r.pair_sem.at[b, 3]),
        ]

    n_tri = r.g_tri.shape[2]
    rims, came = r.rims, r.came
    dkv = r.dkv

    def pair(i, carry):
        b = lax.rem(i, 2)

        @pl.when(i + 1 < pairs)
        def _():
            for copy in fetch_pair(i + 1, 1 - b):
                copy.start()

        for copy in fetch_pair(i, b):
            copy.wait()
        lanes = pl.ds(pl.multiple_of(i * 128, 128), 128)
        dkv[...] = jnp.zeros_like(dkv)
        for block in range(rows // edge):
            own_rows, keys_at = pl.ds(block * edge, edge), pl.ds(block * edge, count)
            head = lax.broadcasted_iota(jnp.int32, (edge, 128), 1) // 64
            key_head = lax.broadcasted_iota(jnp.int32, (count, 128), 1) // 64
            dq = jnp.zeros((edge, 128), jnp.float32)
            for e in range(2):
                prob = r.p_v[b, e, block]
                zero = jnp.zeros((), jnp.bfloat16)
                go = jnp.where(head == e, grad_att[own_rows, lanes], zero)
                query = jnp.where(head == e, r.q_v[b, own_rows, :], zero)
                key = jnp.where(key_head == e, r.k_v[b, keys_at, :], zero)
                grad_prob = row_dot(go, r.v_v[b, keys_at, :])
                prob32 = prob.astype(jnp.float32)
                delta = jnp.sum(grad_prob * prob32, -1, keepdims=True)
                score = (prob32 * (grad_prob - delta) * scale).astype(jnp.bfloat16)
                dq = dq + plain_dot(score, key)
                dkv[0, keys_at, :] += col_dot(score, query)
                dkv[1, keys_at, :] += col_dot(prob, go)
            at = i * 128
            r.g_tri[lax.div(at, n_tri), own_rows, pl.ds(pl.multiple_of(lax.rem(at, n_tri), 128), 128)] = dq.astype(
                jnp.bfloat16
            )
        for side in range(2):
            at = (side + 1) * features + i * 128
            value = dkv[side].astype(jnp.bfloat16)
            r.g_tri[lax.div(at, n_tri), :, pl.ds(pl.multiple_of(lax.rem(at, n_tri), 128), 128)] = value[edge : edge + rows]
            rims[0, side, :, lanes] = value[0:edge]
            rims[1, side, :, lanes] = value[edge + rows :]
        return carry

    def rim_copy(i, side, up):
        lanes = pl.ds(i * 256, 256)
        src = rims.at[1 if up else 0, side, :, lanes]
        dst = came.at[0 if up else 1, side, :, lanes]
        return copies.make(("rim", i, side, up), src, dst, after if up else before)

    for copy in fetch_pair(0, 0):
        copy.start()
    groups = pairs // 2
    for i in range(groups):
        lax.fori_loop(2 * i, 2 * i + 2, pair, 0)

        @pl.when(p.tile < nt - 1)
        def _():
            for side in range(2):
                rim_copy(i, side, True).start()

        @pl.when(p.tile > 0)
        def _():
            for side in range(2):
                rim_copy(i, side, False).start()

        if i % 2 == 1:
            small_work.pop(0)()
            small_work.pop(0)()
        for _ in range(FILL[i] if i < len(FILL) else 0):
            sums(filler.pop(0))
        ring.tick()

    def add_rim(up):
        where = pl.ds(0, edge) if up else pl.ds(rows - edge, edge)
        for i in range(groups):
            for side in range(2):
                rim_copy(i, side, up).wait_recv()

        def one(j, carry):
            for side in range(2):
                at = (side + 1) * features + j * 128
                lanes = pl.ds(pl.multiple_of(lax.rem(at, n_tri), 128), 128)
                got = came[0 if up else 1, side, :, pl.ds(pl.multiple_of(j * 128, 128), 128)]
                had = r.g_tri[lax.div(at, n_tri), where, lanes]
                total = had.astype(jnp.float32) + got.astype(jnp.float32)
                r.g_tri[lax.div(at, n_tri), where, lanes] = total.astype(jnp.bfloat16)
            return carry

        lax.fori_loop(0, pairs, one, 0)

    while filler:
        sums(filler.pop(0))
        ring.tick()
    small_work.pop(0)()
    small_work.pop(0)()

    @pl.when(p.tile > 0)
    def _():
        add_rim(True)

    @pl.when(p.tile < nt - 1)
    def _():
        add_rim(False)

    @pl.when(p.tile < nt - 1)
    def _():
        for i in range(groups):
            for side in range(2):
                rim_copy(i, side, True).wait_send()

    @pl.when(p.tile > 0)
    def _():
        for i in range(groups):
            for side in range(2):
                rim_copy(i, side, False).wait_send()

    ship(0)
    for k in chunks_of[0]:
        sums(k)
        ring.tick()
    small_work.pop(0)()
    times_cols(r.g_tri, r.w_tri, acc, n_tri)
    load_cells.wait()
    ring.tick()

    def to_cells(at, back):
        gtwo[at, :] = gtwo[at, :] + back

    norm_back(r.cells_v, acc, 0, 0, to_cells)
    out = fetch(gtwo, r.cells_grad)
    r.last[...] = held[0:8, :]
    for stage in range(4):
        late.send(stage)
        ring.tick(1)
        late.receive(stage)
    ring.finish()
    r.total[...] = r.rest[...]
    r.total[0:2, :] = r.last[0:2, :]
    r.on_means[...] = r.rest[13 : 13 + comps, 0:half]
    r.on_logvars[...] = r.rest[13 : 13 + comps, half:]
    out.wait()
    copies.drain()


def backward(given, shapes, nt, nf):
    plan = chunk_plan(shapes)
    nz, nx = nt // 2, nf // 2
    rows, features = given["cells"].shape
    depth = given["pre"].shape[1]
    lats = given["z"].shape[1]
    comps = given["means"].shape[0]
    block = (max(c.rows for c in plan), plan[0].cols)
    per_slot = (nx * nt + (max(nx - 1, 1) + 1 + max(nx - 1, 1)) * nz + max(nz - 1, 1)) * block[0] * block[1] * 2
    room = (20 << 20) - 8 * rows * max(nt * c.rows for c in plan)
    slots = max(1, min(len(plan), room // per_slot))
    keys = given["kext"].shape[0]
    edge = (keys - rows) // 2
    small = (32, features)
    bf, f32 = jnp.bfloat16, jnp.float32
    hbm, vmem = pl.BlockSpec(memory_space=pltpu.HBM), pl.BlockSpec(memory_space=pltpu.VMEM)
    smem = pl.BlockSpec(memory_space=pltpu.SMEM)
    outs = dict(
        cells_grad=((rows, features), f32, hbm),
        out0=(shapes[0], f32, vmem),
        out1=(shapes[1], f32, vmem),
        out2=(shapes[2], f32, vmem),
        out3=(shapes[3], f32, vmem),
        out4=(shapes[4], f32, vmem),
        out5=(shapes[5], f32, vmem),
        total=(small, f32, vmem),
        on_means=((comps, lats), f32, vmem),
        on_logvars=((comps, lats), f32, vmem),
    )
    n_copies = len(plan) * ring_slots(nt, nf) + 3 * small_slots(nt, nf) + 6 * nx + features // 256 * 4
    columns = [s[1] for s in shapes]
    dma = pltpu.SemaphoreType.DMA
    near, far = max(nx - 1, 1), max(nz - 1, 1)
    scratch = dict(
        own=pltpu.VMEM((slots, nx, nz, 2) + block, bf),
        diag=pltpu.VMEM((slots, near, nz) + block, bf),
        from_y=pltpu.VMEM((slots, nz) + block, bf),
        from_x=pltpu.VMEM((slots, near, nz) + block, bf),
        from_z=pltpu.VMEM((slots, far) + block, bf),
        g_tri=pltpu.VMEM((nf, rows, columns[0]), bf),
        g_mer=pltpu.VMEM((nf, rows, columns[1]), bf),
        g_exp=pltpu.VMEM((nf, rows, columns[2]), bf),
        g_red=pltpu.VMEM((nf, rows, columns[3]), bf),
        g_enc=pltpu.VMEM((nf, rows, columns[4]), bf),
        g_dec=pltpu.VMEM((nf, rows, columns[5]), bf),
        s_tri=pltpu.VMEM((nx, rows, columns[0]), bf),
        s_mer=pltpu.VMEM((nx, rows, columns[1]), bf),
        s_exp=pltpu.VMEM((nx, rows, columns[2]), bf),
        s_red=pltpu.VMEM((nx, rows, columns[3]), bf),
        s_enc=pltpu.VMEM((nx, rows, columns[4]), bf),
        s_dec=pltpu.VMEM((nx, rows, columns[5]), bf),
        left=pltpu.VMEM((2, 2, rows, max(nt * c.rows for c in plan)), bf),
        left_sem=dma((2, 2)),
        wide=pltpu.VMEM((2, features, max(columns[0], 512)), bf),
        wide_sem=dma((2,)),
        tall=pltpu.VMEM((2, 512, features), bf),
        tall_sem=dma((2,)),
        pre_v=pltpu.VMEM((2, rows, 512), f32),
        pre_sem=dma((2,)),
        gtwo_v=pltpu.VMEM((rows, features), f32),
        hid_v=pltpu.VMEM((rows, features), f32),
        cells_v=pltpu.VMEM((rows, features), bf),
        acc=pltpu.VMEM((rows, features), f32),
        gatt=pltpu.VMEM((rows, features), bf),
        p_v=pltpu.VMEM((2, 2, rows // edge, edge, 3 * edge), bf),
        q_v=pltpu.VMEM((2, rows, 128), bf),
        k_v=pltpu.VMEM((2, keys, 128), bf),
        v_v=pltpu.VMEM((2, keys, 128), bf),
        pair_sem=dma((2, 4)),
        dkv=pltpu.VMEM((2, keys, 128), f32),
        rims=pltpu.VMEM((2, 2, edge, features), bf),
        came=pltpu.VMEM((2, 2, edge, features), bf),
        mix=pltpu.VMEM((3, comps, lats), f32),
        kl=pltpu.VMEM((8, lats), f32),
        kl_places=pltpu.VMEM((small_places(nt, nf), 8, lats), f32),
        held=pltpu.VMEM(small, f32),
        rest=pltpu.VMEM(small, f32),
        places=pltpu.VMEM((small_places(nt, nf),) + small, f32),
        last=pltpu.VMEM((8, features), f32),
        late_places=pltpu.VMEM((small_places(nt, nf), 8, features), f32),
        send=dma((n_copies,)),
        recv=dma((n_copies,)),
        local=dma((nf + 8,)),
        free=pltpu.SemaphoreType.REGULAR((nz + nx,)),
    )
    on_chip = dict(vectors=vmem, lr=vmem, tab=vmem, klp=vmem, logits=vmem, means=vmem, logvars=vmem, kl_step=smem)
    result = pl.pallas_call(
        functools.partial(backward_kernel, nt, nf, plan, slots, [*given, *outs, *scratch]),
        out_shape=[jax.ShapeDtypeStruct(o[0], o[1]) for o in outs.values()],
        in_specs=[on_chip.get(name, hbm) for name in given],
        out_specs=[o[2] for o in outs.values()],
        scratch_shapes=list(scratch.values()),
        compiler_params=pltpu.CompilerParams(collective_id=2, has_side_effects=True, vmem_limit_bytes=62 << 20),
        name="backward",
    )(*given.values())
    return result[0], result[1 : 1 + WEIGHTS], result[1 + WEIGHTS :]


def per_device(
    cells,
    spatial_flag,
    neighbours,
    kl_step,
    noise,
    out_cot,
    first_gain,
    first_shift,
    triple_proj,
    merge_proj,
    second_gain,
    second_shift,
    expand_weight,
    expand_bias,
    reduce_weight,
    reduce_bias,
    third_gain,
    third_shift,
    encode_weight,
    encode_bias,
    decode_weight,
    decode_bias,
    mixture_logits,
    mixture_means,
    mixture_logvars,
):
    nt, nf = lax.axis_size("tile"), lax.axis_size("fs")
    features = cells.shape[2]
    mixture = (mixture_logits, mixture_means, mixture_logvars)
    weights = (triple_proj, merge_proj, expand_weight, reduce_weight, encode_weight, decode_weight)
    kept = forward(
        cells[0],
        spatial_flag,
        neighbours[0].T,
        noise[0],
        weights,
        (
            first_gain,
            first_shift,
            second_gain,
            second_shift,
            reduce_bias,
            third_gain,
            third_shift,
            encode_bias,
            decode_bias,
            expand_bias,
        ),
        mixture,
        nt,
        nf,
    )

    def whole(full):
        return full.reshape(-1, full.shape[-1])

    given = dict(
        two=kept.two,
        pre=kept.pre,
        act=kept.act,
        hid=kept.hid,
        n2=kept.n2,
        att=kept.att,
        probs=kept.probs,
        q=kept.q,
        kext=kept.kext,
        vext=kept.vext,
        cells=cells[0],
        n1=kept.n1,
        lat=kept.lat,
        n3=kept.n3,
        sib_n1=kept.sib_n1,
        sib_att=kept.sib_att,
        sib_n2=kept.sib_n2,
        sib_act=kept.sib_act,
        sib_n3=kept.sib_n3,
        sib_lat=kept.sib_lat,
        z=kept.z,
        enc=kept.enc,
        noise=noise[0],
        gout=out_cot[0],
        w_tri=whole(kept.full0),
        w_mer=whole(kept.full1),
        w_exp=whole(kept.full2),
        w_red=whole(kept.full3),
        w_enc=whole(kept.full4),
        w_dec=whole(kept.full5),
        vectors=kept.vectors,
        lr=kept.lr,
        tab=kept.tab,
        klp=kept.klp,
        logits=mixture_logits[None],
        means=mixture_means,
        logvars=mixture_logvars,
        kl_step=kl_step,
    )
    cells_grad, sums, (small, means_sum, logvars_sum) = backward(given, [w.shape for w in weights], nt, nf)
    triple_sum, merge_sum, expand_sum, reduce_sum, encode_sum, decode_sum = sums
    index = lax.axis_index("tile") * nf + lax.axis_index("fs")
    piece, wide = first_gain.shape[0], expand_bias.shape[0]
    pieces = lax.dynamic_slice_in_dim(small[:9], index * piece, piece, 1)
    expand_piece = lax.dynamic_slice_in_dim(small[9:13].reshape(-1), index * wide, wide, 0)
    comps = mixture_means.shape[0]
    return (
        kept.decoded[None],
        cells_grad[None],
        pieces[0],
        pieces[1],
        triple_sum,
        merge_sum,
        pieces[2],
        pieces[3],
        expand_sum,
        expand_piece,
        reduce_sum,
        pieces[4],
        pieces[5],
        pieces[6],
        encode_sum,
        pieces[7],
        decode_sum,
        pieces[8],
        small[29, :comps],
        means_sum,
        logvars_sum,
    )


def solution(mesh):
    placed = (
        P("fs", "tile", None),
        P("fs", "tile"),
        P("fs", "tile", None),
        P(),
        P("fs", "tile", None),
        P("fs", "tile", None),
        P(("tile", "fs")),
        P(("tile", "fs")),
        P("tile", "fs"),
        P("tile", "fs"),
        P(("tile", "fs")),
        P(("tile", "fs")),
        P("tile", "fs"),
        P(("tile", "fs")),
        P("tile", "fs"),
        P(("tile", "fs")),
        P(("tile", "fs")),
        P(("tile", "fs")),
        P("tile", "fs"),
        P(("tile", "fs")),
        P("tile", "fs"),
        P(("tile", "fs")),
        P(),
        P(),
        P(),
    )
    return jax.shard_map(
        per_device,
        mesh=mesh,
        in_specs=placed,
        out_specs=(
            P("fs", "tile", None),
            P("fs", "tile", None),
            P(("tile", "fs")),
            P(("tile", "fs")),
            P("tile", "fs"),
            P("tile", "fs"),
            P(("tile", "fs")),
            P(("tile", "fs")),
            P("tile", "fs"),
            P(("tile", "fs")),
            P("tile", "fs"),
            P(("tile", "fs")),
            P(("tile", "fs")),
            P(("tile", "fs")),
            P("tile", "fs"),
            P(("tile", "fs")),
            P("tile", "fs"),
            P(("tile", "fs")),
            P(),
            P(),
            P(),
        ),
        check_vma=False,
    )
```
